32 devices in a mesh: fsdp: 4 (over z), ctx: 2 (over y), tp: 4 (over x, core).
Axes of the slice: x: 2, y: 2, z: 4, core: 2. Of those that a mesh axis runs over, the one named last changes fastest.
Arguments:
- block_input: bfloat16 [8, 2048, 1024], P('fsdp', 'ctx', 'tp'), may hold values from -45 to 45
- positions: int32 [8, 2048], P('fsdp', 'ctx'), may hold values from 0 to 2047, as said below
- first_gain: bfloat16 [1024], P('fsdp'), may hold values from 0.5 to 1.5
- first_shift: bfloat16 [1024], P('fsdp'), may hold values from -3 to 3
- second_gain: bfloat16 [1024], P('fsdp'), may hold values from 0.5 to 1.5
- second_shift: bfloat16 [1024], P('fsdp'), may hold values from -3 to 3
- triple_weight: bfloat16 [1024, 3, 1024], P('fsdp', None, 'tp'), as said below
- triple_bias: bfloat16 [3, 16, 64], P(None, 'tp', 'fsdp'), may hold values from -64 to 64
- mixer_weight: bfloat16 [1024, 1024], P('tp', 'fsdp'), may hold values from -2 to 2
- output_bias: bfloat16 [1024], P('fsdp'), may hold values from -3 to 3
- widen_weight: bfloat16 [1024, 4096], P('fsdp', 'tp'), may hold values from -0.1875 to 0.1875
- widen_bias: bfloat16 [32, 128], P('tp', 'fsdp'), may hold values from -3 to 3
- narrow_weight: bfloat16 [4096, 1024], P('tp', 'fsdp'), may hold values from -0.09375 to 0.09375
- cotangent: bfloat16 [8, 2048, 1024], P('fsdp', 'ctx', 'tp'), may hold values from -6 to 6
Outputs:
- block_output: bfloat16 [8, 2048, 1024], P('fsdp', 'ctx', 'tp')
- input_grad: bfloat16 [8, 2048, 1024], P('fsdp', 'ctx', 'tp')
- first_gain_grad: float32 [1024], P('fsdp')
- first_shift_grad: float32 [1024], P('fsdp')
- second_gain_grad: float32 [1024], P('fsdp')
- second_shift_grad: float32 [1024], P('fsdp')
- triple_weight_grad: float32 [1024, 3, 1024], P('fsdp', None, 'tp')
- triple_bias_grad: float32 [3, 16, 64], P(None, 'tp', 'fsdp')
- mixer_weight_grad: float32 [1024, 1024], P('tp', 'fsdp')
- output_bias_grad: float32 [1024], P('fsdp')
- widen_weight_grad: float32 [1024, 4096], P('fsdp', 'tp')
- widen_bias_grad: float32 [32, 128], P('tp', 'fsdp')
- narrow_weight_grad: float32 [4096, 1024], P('tp', 'fsdp')
The draws below stay inside these ranges and needn't reach their ends.
Inputs may be any that keep to these rules, and one draw needn't show every extreme that they name: `positions`: each row counts up by one from 0 and falls back to 0 where a packed document begins; a row holds at most four documents; the first sequence is one whole document. `triple_weight`: entries are at most 4 / sqrt(1024) in magnitude.
All inputs are finite; a program needn't handle non-finite values.
Results may differ from the reference program's by a relative error of at most 0.017.
Values may be sent and summed in bfloat16 or wider, within the bound.
A program may use at most 192 MiB of HBM per device.

```python
import math
import jax
import jax.numpy as jnp
from jax import lax

D = 1024
H = 16
HD = 64
ROT = 16
FF = 4096
LEN = 2048
SEQS = 8


def draw_block_input(key, part):
    noise_key = jax.random.fold_in(key, 0)
    values = jax.random.truncated_normal(noise_key, -5.0, 5.0, (SEQS, LEN, D), jnp.float32)
    return values.astype(jnp.bfloat16)


def draw_positions(key, part):
    cuts = jax.random.randint(key, (SEQS, 3, 1), 1, LEN, dtype=jnp.int32)
    whole = (jnp.arange(SEQS, dtype=jnp.int32) == 0)[:, None, None]
    cuts = jnp.where(whole, jnp.int32(LEN), cuts)
    index = jnp.arange(LEN, dtype=jnp.int32)
    starts = jnp.max(jnp.where(cuts <= index, cuts, 0), axis=1)
    return (index[None, :] - starts).astype(jnp.int32)


def draw_triple_weight(key, part):
    base_key = jax.random.fold_in(key, 3)
    values = jax.random.truncated_normal(base_key, -4.0, 4.0, (D, 3, D), jnp.float32)
    return (values * (1.0 / math.sqrt(D))).astype(jnp.bfloat16)


def draw_triple_bias(key, part):
    base_key = jax.random.fold_in(key, 5)
    values = jax.random.truncated_normal(base_key, -4.0, 4.0, (3, H, HD), jnp.float32) * 0.1
    return values.astype(jnp.bfloat16)


def strengthened(entries, own_key, source, target, parts, factor):
    owner, partner = [(jnp.arange(entries.shape[position]) // (entries.shape[position] // parts)).reshape([-1 if axis == position else 1 for axis in range(entries.ndim)]) for position in (source, target)]
    chosen = jax.random.permutation(own_key, parts)[partner]
    strong = (owner == chosen) | (owner == (partner + parts // 2) % parts)
    return jnp.where(strong, factor * entries, entries)


def steps_of(rng, dims, cuts, low, top_value):
    loudness = 1.0
    for axis_at, shards_of in cuts:
        heights = jax.random.uniform(jax.random.fold_in(jax.random.fold_in(rng, 6), axis_at), (shards_of,), jnp.float32, low / len(cuts), top_value / len(cuts))
        loudness = loudness * jnp.repeat(jnp.exp(heights), dims[axis_at] // shards_of).reshape((-1,) + (1,) * (len(dims) - 1 - axis_at))
    return loudness


def gaussian(own_key, extent, width, most, cuts=(), kind=jnp.bfloat16):
    result = width * jax.random.normal(own_key, extent, jnp.float32)
    if cuts:
        result = result * steps_of(own_key, extent, cuts, -0.22, 0.18)
    return jnp.clip(result, -most, most).astype(kind)


def noise_with(own_key, shape, spread, limit, shards, heavy, held_as=jnp.bfloat16):
    values = spread * jax.random.normal(own_key, shape, jnp.float32)
    if shards:
        values = values * steps_of(own_key, shape, shards, -0.22, 0.18)
    return jnp.clip(strengthened(values, jax.random.fold_in(own_key, 3), *heavy), -limit, limit).astype(held_as)


def setup_inputs(seed: int = 0) -> dict:
    streams_of = jax.random.split(jax.random.key(seed), 15)
    block_input = draw_block_input(jax.random.fold_in(streams_of[14], 71), 0)
    positions = draw_positions(jax.random.fold_in(streams_of[14], 71), 0)
    first_gain = jnp.clip(1.0 + 0.1 * jax.random.normal(streams_of[2], (D,), jnp.float32), 0.5, 1.5).astype(jnp.bfloat16)
    first_shift = gaussian(streams_of[3], (D,), 0.3, 3.0, ((0, 4),))
    second_gain = jnp.clip(1.0 + 0.1 * jax.random.normal(streams_of[4], (D,), jnp.float32), 0.5, 1.5).astype(jnp.bfloat16)
    second_shift = gaussian(streams_of[5], (D,), 0.3, 3.0, ((0, 4),))
    triple_weight = draw_triple_weight(jax.random.fold_in(streams_of[14], 71), 0)
    triple_bias = draw_triple_bias(jax.random.fold_in(streams_of[14], 71), 0)
    mixer_weight = gaussian(streams_of[8], (D, D), (HD // 8) ** -0.5, 2.0, ((0, 4), (1, 4)))
    output_bias = gaussian(streams_of[9], (D,), 0.3, 3.0, ((0, 4),))
    widen_weight = gaussian(streams_of[10], (D, FF), D ** -0.5, 0.1875, ((0, 4), (1, 4)))
    widen_bias = gaussian(streams_of[11], (FF // 128, 128), 0.5, 3.0, ((0, 4), (1, 4)))
    narrow_weight = gaussian(streams_of[12], (FF, D), FF ** -0.5, 0.09375, ((0, 4), (1, 4)))
    cotangent = noise_with(streams_of[13], (SEQS, LEN, D), 1.0, 6.0, ((0, 4), (1, 2), (2, 4)), (0, 2, 4, 2.0))
    return {"block_input": block_input, "positions": positions, "first_gain": first_gain, "first_shift": first_shift, "second_gain": second_gain, "second_shift": second_shift, "triple_weight": triple_weight, "triple_bias": triple_bias, "mixer_weight": mixer_weight, "output_bias": output_bias, "widen_weight": widen_weight, "widen_bias": widen_bias, "narrow_weight": narrow_weight, "cotangent": cotangent}


norm_eps = 1e-05
masked_score = -1e+30

def normalize(rows):
    centred = rows - lax.optimization_barrier(jnp.mean(rows, axis=-1, keepdims=True))
    inverse = lax.rsqrt(lax.optimization_barrier(jnp.mean(centred * centred, axis=-1, keepdims=True)) + norm_eps)
    return (centred * inverse, inverse)

def gelu_parts(widened):
    cumulative = 0.5 * (1.0 + lax.erf(widened * (1.0 / math.sqrt(2.0))))
    density = jnp.exp(-0.5 * widened * widened) * (1.0 / math.sqrt(2.0 * math.pi))
    return (widened * cumulative, cumulative + widened * density)

def rotate_forward(block, cosine, sine, half):
    first = block[..., :half]
    second = block[..., half:2 * half]
    return jnp.concatenate([first * cosine - second * sine, second * cosine + first * sine, block[..., 2 * half:]], axis=-1)

def rotate_back(block, cosine, sine, half):
    first = block[..., :half]
    second = block[..., half:2 * half]
    return jnp.concatenate([first * cosine + second * sine, second * cosine - first * sine, block[..., 2 * half:]], axis=-1)

def norm_back(grad, gain, normed, inverse):
    scaled = grad * gain
    return inverse * (scaled - lax.optimization_barrier(jnp.mean(scaled, axis=-1, keepdims=True)) - normed * lax.optimization_barrier(jnp.mean(scaled * normed, axis=-1, keepdims=True)))

def reference(block_input, positions, first_gain, first_shift, second_gain, second_shift, triple_weight, triple_bias, mixer_weight, output_bias, widen_weight, widen_bias, narrow_weight, cotangent):
    scale = HD ** (-0.5)
    half = ROT // 2
    gain_first = first_gain.astype(jnp.float32)
    shift_first = first_shift.astype(jnp.float32)
    gain_second = second_gain.astype(jnp.float32)
    shift_second = second_shift.astype(jnp.float32)
    flat_triple = triple_weight.reshape(D, 3 * D)
    bias_triple = triple_bias.astype(jnp.float32)
    bias_widen = widen_bias.reshape(FF).astype(jnp.float32)
    bias_output = output_bias.astype(jnp.float32)
    index = jnp.arange(LEN, dtype=jnp.int32)
    freqs = jnp.exp(jnp.arange(half, dtype=jnp.float32) * (-2.0 * math.log(10000.0) / ROT))

    def one_sequence(totals, inputs):
        rows_in, places, cot_rows = inputs
        normed, inverse = normalize(rows_in.astype(jnp.float32))
        first_rows = (normed * gain_first + shift_first).astype(jnp.bfloat16)
        second_rows = (normed * gain_second + shift_second).astype(jnp.bfloat16)
        projected = jnp.dot(first_rows, flat_triple, preferred_element_type=jnp.float32).reshape(LEN, 3, H, HD) + bias_triple
        angles = places.astype(jnp.float32)[:, None] * freqs[None, :]
        cosine = jnp.cos(angles)[:, None, None, :]
        sine = jnp.sin(angles)[:, None, None, :]
        turned = rotate_forward(projected[:, :2], cosine, sine, half)
        triple = jnp.concatenate([turned, projected[:, 2:]], axis=1).astype(jnp.bfloat16)
        by_heads = jnp.transpose(triple, (1, 2, 0, 3))
        visible = (index[None, :] <= index[:, None]) & (places[:, None] - places[None, :] == index[:, None] - index[None, :])

        def head_scores(queries, keys_in):
            scores = jnp.dot(queries, keys_in.T, preferred_element_type=jnp.float32) * scale
            return jnp.where(visible, scores, masked_score)

        def head_forward(args):
            queries, keys_in, values_in = args
            scores = head_scores(queries, keys_in)
            top = lax.optimization_barrier(jnp.max(scores, axis=1, keepdims=True))
            logsum = top + jnp.log(lax.optimization_barrier(jnp.sum(jnp.exp(scores - top), axis=1, keepdims=True)))
            weights = jnp.exp(scores - logsum).astype(jnp.bfloat16)
            mixed = jnp.dot(weights, values_in, preferred_element_type=jnp.float32).astype(jnp.bfloat16)
            return (mixed, logsum[:, 0])

        def head_backward(args):
            queries, keys_in, values_in, mixed, logsum, grad_mixed = args
            scores = head_scores(queries, keys_in)
            probs = jnp.exp(scores - logsum[:, None])
            values_grad = jnp.dot(probs.astype(jnp.bfloat16).T, grad_mixed, preferred_element_type=jnp.float32).astype(jnp.bfloat16)
            prob_grads = jnp.dot(grad_mixed, values_in.T, preferred_element_type=jnp.float32)
            delta = lax.optimization_barrier(jnp.sum(grad_mixed.astype(jnp.float32) * mixed.astype(jnp.float32), axis=1))
            score_grads = (probs * (prob_grads - delta[:, None])).astype(jnp.bfloat16)
            queries_grad = (jnp.dot(score_grads, keys_in, preferred_element_type=jnp.float32) * scale).astype(jnp.bfloat16)
            keys_grad = (jnp.dot(score_grads.T, queries, preferred_element_type=jnp.float32) * scale).astype(jnp.bfloat16)
            return (queries_grad, keys_grad, values_grad)
        mixed, logsum = lax.map(head_forward, (by_heads[0], by_heads[1], by_heads[2]))
        mixed_rows = jnp.transpose(mixed, (1, 0, 2)).reshape(LEN, D)
        widened = jnp.dot(second_rows, widen_weight, preferred_element_type=jnp.float32) + bias_widen
        activated_float, slope = gelu_parts(widened)
        activated = activated_float.astype(jnp.bfloat16)
        branches = jnp.dot(mixed_rows, mixer_weight, preferred_element_type=jnp.float32) + jnp.dot(activated, narrow_weight, preferred_element_type=jnp.float32)
        block_output = (rows_in.astype(jnp.float32) + branches + bias_output).astype(jnp.bfloat16)
        output_bias_grad = lax.optimization_barrier(jnp.sum(cot_rows.astype(jnp.float32), axis=0))
        narrow_grad = jnp.dot(activated.T, cot_rows, preferred_element_type=jnp.float32)
        hidden_grad = jnp.dot(cot_rows, narrow_weight.T, preferred_element_type=jnp.float32) * slope
        widen_bias_grad = lax.optimization_barrier(jnp.sum(hidden_grad, axis=0))
        hidden_rounded = hidden_grad.astype(jnp.bfloat16)
        widen_grad = jnp.dot(second_rows.T, hidden_rounded, preferred_element_type=jnp.float32)
        second_grad = jnp.dot(hidden_rounded, widen_weight.T, preferred_element_type=jnp.float32)
        mixer_grad = jnp.dot(mixed_rows.T, cot_rows, preferred_element_type=jnp.float32)
        mixed_grad = jnp.dot(cot_rows, mixer_weight.T, preferred_element_type=jnp.float32).astype(jnp.bfloat16)
        mixed_grad = jnp.transpose(mixed_grad.reshape(LEN, H, HD), (1, 0, 2))
        queries_grad, keys_grad, values_grad = lax.map(head_backward, (by_heads[0], by_heads[1], by_heads[2], mixed, logsum, mixed_grad))
        back = jnp.transpose(jnp.stack([queries_grad, keys_grad, values_grad], axis=0), (2, 0, 1, 3)).astype(jnp.float32)
        unturned = rotate_back(back[:, :2], cosine, sine, half)
        projected_grad = jnp.concatenate([unturned, back[:, 2:]], axis=1)
        triple_bias_grad = lax.optimization_barrier(jnp.sum(projected_grad, axis=0))
        projected_rounded = projected_grad.astype(jnp.bfloat16).reshape(LEN, 3 * D)
        triple_grad = jnp.dot(first_rows.T, projected_rounded, preferred_element_type=jnp.float32).reshape(D, 3, D)
        first_grad = jnp.dot(projected_rounded, flat_triple.T, preferred_element_type=jnp.float32)
        first_gain_grad = lax.optimization_barrier(jnp.sum(first_grad * normed, axis=0))
        first_shift_grad = lax.optimization_barrier(jnp.sum(first_grad, axis=0))
        second_gain_grad = lax.optimization_barrier(jnp.sum(second_grad * normed, axis=0))
        second_shift_grad = lax.optimization_barrier(jnp.sum(second_grad, axis=0))
        rows_grad = cot_rows.astype(jnp.float32) + norm_back(first_grad, gain_first, normed, inverse) + norm_back(second_grad, gain_second, normed, inverse)
        input_grad = rows_grad.astype(jnp.bfloat16)
        terms = (first_gain_grad, first_shift_grad, second_gain_grad, second_shift_grad, triple_grad, triple_bias_grad, mixer_grad, output_bias_grad, widen_grad, widen_bias_grad, narrow_grad)
        totals = tuple((total + term for total, term in zip(totals, terms)))
        return (totals, (block_output, input_grad))
    zeros = (jnp.zeros((D,), jnp.float32), jnp.zeros((D,), jnp.float32), jnp.zeros((D,), jnp.float32), jnp.zeros((D,), jnp.float32), jnp.zeros((D, 3, D), jnp.float32), jnp.zeros((3, H, HD), jnp.float32), jnp.zeros((D, D), jnp.float32), jnp.zeros((D,), jnp.float32), jnp.zeros((D, FF), jnp.float32), jnp.zeros((FF,), jnp.float32), jnp.zeros((FF, D), jnp.float32))
    totals, (block_output, input_grad) = lax.scan(one_sequence, zeros, (block_input, positions, cotangent))
    return (block_output, input_grad, totals[0], totals[1], totals[2], totals[3], totals[4], totals[5], totals[6], totals[7], totals[8], totals[9].reshape(FF // 128, 128), totals[10])
```

```python
import functools
import math

import jax
import jax.numpy as jnp
from jax import lax
from jax.experimental import pallas as pl
from jax.experimental.pallas import tpu as pltpu
from jax.sharding import PartitionSpec as P

ROT = 16


norm_eps = 1e-05
masked_score = -1e30


def normalize(rows):
    centred = rows - jnp.mean(rows, axis=-1, keepdims=True)
    inverse = lax.rsqrt(jnp.mean(centred * centred, axis=-1, keepdims=True) + norm_eps)
    return (centred * inverse, inverse)


def gelu_parts(widened):
    cumulative = 0.5 * (1.0 + lax.erf(widened * (1.0 / math.sqrt(2.0))))
    density = jnp.exp(-0.5 * widened * widened) * (1.0 / math.sqrt(2.0 * math.pi))
    return (widened * cumulative, cumulative + widened * density)


def rotary_tables(positions, rotary):
    half = rotary // 2
    freqs = jnp.exp(jnp.arange(half, dtype=jnp.float32) * (-2.0 * math.log(10000.0) / rotary))
    angles = positions.astype(jnp.float32)[:, None, :] * freqs[None, :, None]
    return (jnp.cos(angles)[:, None, None], jnp.sin(angles)[:, None, None])


def rotate_forward(block, cosine, sine, half):
    first = block[..., :half, :]
    second = block[..., half : 2 * half, :]
    return jnp.concatenate(
        [first * cosine - second * sine, second * cosine + first * sine, block[..., 2 * half :, :]],
        axis=-2,
    )


def rotate_back(block, cosine, sine, half):
    first = block[..., :half, :]
    second = block[..., half : 2 * half, :]
    return jnp.concatenate(
        [first * cosine + second * sine, second * cosine - first * sine, block[..., 2 * half :, :]],
        axis=-2,
    )


def attend_kernel(block, scale, between, qkv_ref, grad_ref, base_ref, back_ref, mixed_ref,
                  queries, query_rows, keys, key_rows, values, value_rows, grads, grad_rows,
                  base_rows, key_sum, value_sum):
    parts, head_size, span = grad_ref.shape[0], grad_ref.shape[2], grad_ref.shape[3]
    length = parts * span
    for part in range(parts):
        at = pl.ds(part * span, span)
        queries[:, at] = (qkv_ref[part, 0, 0].astype(jnp.float32) * scale).astype(jnp.bfloat16)
        keys[:, at] = qkv_ref[part, 0, 1]
        values[:, at] = qkv_ref[part, 0, 2]
        grads[:, at] = grad_ref[part, 0]
    for source, target in (
        (queries, query_rows),
        (keys, key_rows),
        (values, value_rows),
        (grads, grad_rows),
    ):
        target[...] = source[...].astype(jnp.float32).T.astype(jnp.bfloat16)
    base_row = base_ref[0]
    base_rows[...] = jnp.broadcast_to(base_row, (128, length)).T
    for start in range(0, length, block):
        between(start // block)
        count = start + block
        here = slice(start, count)
        scores = jnp.dot(key_rows[:count], queries[:, here], preferred_element_type=jnp.float32)
        wide_base = jnp.concatenate([base_rows[:count]] * (block // 128), axis=1)
        same = wide_base == base_row[:, here]
        key_index = lax.broadcasted_iota(jnp.int32, (block, block), 0)
        query_index = lax.broadcasted_iota(jnp.int32, (block, block), 1)
        last = jnp.where(
            same[start:] & (key_index <= query_index), scores[start:], masked_score
        )
        if start:
            earlier = jnp.where(same[:start], scores[:start], masked_score)
            scores = jnp.concatenate([earlier, last], axis=0)
        else:
            scores = last
        top = jnp.max(scores, axis=0, keepdims=True)
        raised = jnp.exp(scores - top)
        probs = raised * (1.0 / jnp.sum(raised, axis=0, keepdims=True))
        weights = probs.astype(jnp.bfloat16)
        mixed = jnp.dot(values[:, :count], weights, preferred_element_type=jnp.float32).astype(
            jnp.bfloat16
        )
        grad_block = grads[:, here]
        delta = jnp.sum(
            mixed.astype(jnp.float32) * grad_block.astype(jnp.float32), axis=0, keepdims=True
        )
        prob_grads = jnp.dot(value_rows[:count], grad_block, preferred_element_type=jnp.float32)
        score_grads = (probs * (prob_grads - delta)).astype(jnp.bfloat16)
        query_part = jnp.dot(keys[:, :count], score_grads, preferred_element_type=jnp.float32)
        key_part = jnp.dot(score_grads, query_rows[here], preferred_element_type=jnp.float32)
        value_part = jnp.dot(weights, grad_rows[here], preferred_element_type=jnp.float32)
        if start:
            key_sum[:start] += key_part[:start]
            value_sum[:start] += value_part[:start]
        key_sum[here] = key_part[start:]
        value_sum[here] = value_part[start:]
        part, inside = start // span, start % span
        mixed_ref[part, 0, :, inside : inside + block] = mixed
        back_ref[part, 0, 0, :, inside : inside + block] = (query_part * scale).astype(jnp.bfloat16)
    for part in range(parts):
        at = pl.ds(part * span, span)
        back_ref[part, 0, 1] = key_sum[at].T.astype(jnp.bfloat16)
        back_ref[part, 0, 2] = value_sum[at].T.astype(jnp.bfloat16)


def attend(by_heads, grad_heads, item_base, scale):
    parts, items, unused, head_size, span = by_heads.shape
    length = parts * span
    block = min(256, span)
    wide = pltpu.VMEM((head_size, length), jnp.bfloat16)
    tall = pltpu.VMEM((length, head_size), jnp.bfloat16)
    total = pltpu.VMEM((length, head_size), jnp.float32)
    return pl.pallas_call(
        functools.partial(attend_kernel, block, scale, lambda step: None),
        grid=(items,),
        in_specs=[
            pl.BlockSpec((parts, 1, 3, head_size, span), lambda i: (0, i, 0, 0, 0)),
            pl.BlockSpec((parts, 1, head_size, span), lambda i: (0, i, 0, 0)),
            pl.BlockSpec((1, 1, length), lambda i: (i, 0, 0)),
        ],
        out_specs=[
            pl.BlockSpec((parts, 1, 3, head_size, span), lambda i: (0, i, 0, 0, 0)),
            pl.BlockSpec((parts, 1, head_size, span), lambda i: (0, i, 0, 0)),
        ],
        out_shape=[
            jax.ShapeDtypeStruct(by_heads.shape, jnp.bfloat16),
            jax.ShapeDtypeStruct(grad_heads.shape, jnp.bfloat16),
        ],
        scratch_shapes=[wide, tall, wide, tall, wide, tall, wide, tall,
                        pltpu.VMEM((length, 128), jnp.float32), total, total],
        compiler_params=pltpu.CompilerParams(vmem_limit_bytes=48 * 1024 * 1024),
        cost_estimate=pl.CostEstimate(
            flops=7 * items * length * length * 256,
            bytes_accessed=4 * by_heads.size,
            transcendentals=items * length * length // 2,
        ),
    )(by_heads, grad_heads, item_base)


def sum_pair(share, axis):
    size = lax.axis_size(axis)
    if size == 2:
        other = lax.ppermute(share, axis, [(0, 1), (1, 0)])
        return share.astype(jnp.float32) + other.astype(jnp.float32)
    return lax.psum(share, axis).astype(jnp.float32)


def shards_general(
    block_input,
    positions,
    first_gain,
    first_shift,
    second_gain,
    second_shift,
    triple_weight,
    triple_bias,
    mixer_weight,
    output_bias,
    widen_weight,
    widen_bias,
    narrow_weight,
    cotangent,
):
    seqs, local_tokens, local_width = block_input.shape
    vectors = (first_gain, first_shift, second_gain, second_shift, output_bias, triple_bias, widen_bias)
    small = lax.all_gather(
        jnp.concatenate([vector.reshape(-1) for vector in vectors]), "fsdp", axis=0, tiled=False
    )
    groups = small.shape[0]
    pieces = []
    offset = 0
    for vector in vectors:
        pieces.append(small[:, offset : offset + vector.size].astype(jnp.float32))
        offset += vector.size
    gain_one, shift_one, gain_two, shift_two, bias_output = [
        piece.reshape(-1) for piece in pieces[:5]
    ]
    bias_triple = jnp.transpose(
        pieces[5].reshape((groups,) + triple_bias.shape), (1, 2, 0, 3)
    ).reshape(triple_bias.shape[0], triple_bias.shape[1], -1)
    bias_widen = jnp.transpose(
        pieces[6].reshape((groups,) + widen_bias.shape), (1, 0, 2)
    ).reshape(-1)
    all_positions = lax.all_gather(positions, "ctx", axis=1, tiled=True)
    whole_input = lax.all_gather(block_input, "tp", axis=2, tiled=True)
    weight_triple = lax.all_gather(triple_weight, "fsdp", axis=0, tiled=True)
    whole_cot = lax.all_gather(cotangent, "tp", axis=2, tiled=True)
    mixer_rows = mixer_weight.shape[0]
    joined = lax.all_gather(
        jnp.concatenate([mixer_weight, narrow_weight], axis=0), "fsdp", axis=1, tiled=True
    )
    weight_mixer, weight_narrow = joined[:mixer_rows], joined[mixer_rows:]
    weight_widen = lax.all_gather(widen_weight, "fsdp", axis=0, tiled=True)
    width = weight_triple.shape[0]
    heads_local, head_size = bias_triple.shape[1:]
    feature_start = lax.axis_index("tp") * local_width
    scale = head_size ** (-0.5)
    half = ROT // 2
    normed, inverse = normalize(whole_input.astype(jnp.float32))
    first_rows = (normed * gain_one + shift_one).astype(jnp.bfloat16)
    second_rows = (normed * gain_two + shift_two).astype(jnp.bfloat16)
    cosine, sine = rotary_tables(positions, ROT)
    weight_four = weight_triple.reshape(width, 3, heads_local, head_size)
    projected = jnp.einsum(
        "std,dchk->shckt", first_rows, weight_four, preferred_element_type=jnp.float32
    )
    projected = projected + jnp.transpose(bias_triple, (1, 0, 2))[None, :, :, :, None]
    turned = rotate_forward(projected[:, :, :2], cosine, sine, half)
    triple = jnp.concatenate([turned, projected[:, :, 2:]], axis=2).astype(jnp.bfloat16)
    parts = lax.axis_size("ctx")
    items = seqs * heads_local // parts
    by_heads = lax.all_to_all(
        triple.reshape(parts, items, 3, head_size, local_tokens),
        "ctx",
        split_axis=0,
        concat_axis=0,
        tiled=True,
    )
    mixer_four = weight_mixer.reshape(heads_local, head_size, width)
    mixed_grad = jnp.einsum(
        "ste,hke->shkt", whole_cot, mixer_four, preferred_element_type=jnp.float32
    ).astype(jnp.bfloat16)
    grad_heads = lax.all_to_all(
        mixed_grad.reshape(parts, items, head_size, local_tokens),
        "ctx",
        split_axis=0,
        concat_axis=0,
        tiled=True,
    )
    length = all_positions.shape[1]
    item_seq = (lax.axis_index("ctx") * items + jnp.arange(items, dtype=jnp.int32)) // heads_local
    base = (jnp.arange(length, dtype=jnp.int32)[None, :] - all_positions).astype(jnp.float32)
    item_base = jnp.take(base, item_seq, axis=0)[:, None, :]
    back_heads, mixed = attend(by_heads, grad_heads, item_base, scale)
    mixed_tokens = lax.all_to_all(
        mixed, "ctx", split_axis=0, concat_axis=0, tiled=True
    ).reshape(seqs, heads_local, head_size, local_tokens)
    back_float = (
        lax.all_to_all(back_heads, "ctx", split_axis=0, concat_axis=0, tiled=True)
        .reshape(seqs, heads_local, 3, head_size, local_tokens)
        .astype(jnp.float32)
    )
    widened = (
        jnp.einsum("std,df->stf", second_rows, weight_widen, preferred_element_type=jnp.float32)
        + bias_widen
    )
    activated_float, slope = gelu_parts(widened)
    activated = activated_float.astype(jnp.bfloat16)
    hidden_grad = (
        jnp.einsum("ste,fe->stf", whole_cot, weight_narrow, preferred_element_type=jnp.float32)
        * slope
    )
    widen_bias_grad = jnp.sum(hidden_grad, axis=(0, 1))
    hidden_rounded = hidden_grad.astype(jnp.bfloat16)
    narrow_grad = jnp.einsum(
        "stf,ste->fe", activated, whole_cot, preferred_element_type=jnp.float32
    ).astype(jnp.bfloat16)
    narrow_share = lax.psum_scatter(narrow_grad, "fsdp", scatter_dimension=1, tiled=True)
    widen_grad = jnp.einsum(
        "std,stf->df", second_rows, hidden_rounded, preferred_element_type=jnp.float32
    ).astype(jnp.bfloat16)
    widen_share = lax.psum_scatter(widen_grad, "fsdp", scatter_dimension=0, tiled=True)
    second_grad = jnp.einsum(
        "stf,df->std", hidden_rounded, weight_widen, preferred_element_type=jnp.float32
    ).astype(jnp.bfloat16)
    attention_part = jnp.einsum(
        "shkt,hke->ste", mixed_tokens, mixer_four, preferred_element_type=jnp.float32
    )
    branches = attention_part + jnp.einsum(
        "stf,fe->ste", activated, weight_narrow, preferred_element_type=jnp.float32
    )
    summed = lax.psum_scatter(
        branches.astype(jnp.bfloat16), "tp", scatter_dimension=2, tiled=True
    ).astype(jnp.float32)
    bias_slice = lax.dynamic_slice_in_dim(bias_output, feature_start, local_width, 0)
    block_output = (block_input.astype(jnp.float32) + summed + bias_slice).astype(jnp.bfloat16)
    mixer_grad = (
        jnp.einsum("shkt,ste->hke", mixed_tokens, whole_cot, preferred_element_type=jnp.float32)
        .reshape(weight_mixer.shape)
        .astype(jnp.bfloat16)
    )
    mixer_share = lax.psum_scatter(mixer_grad, "fsdp", scatter_dimension=1, tiled=True)
    unturned = rotate_back(back_float[:, :, :2], cosine, sine, half)
    projected_grad = jnp.concatenate([unturned, back_float[:, :, 2:]], axis=2)
    triple_bias_grad = jnp.transpose(jnp.sum(projected_grad, axis=(0, 4)), (1, 0, 2))
    projected_rounded = projected_grad.astype(jnp.bfloat16)
    first_grad = jnp.einsum(
        "shckt,dchk->std", projected_rounded, weight_four, preferred_element_type=jnp.float32
    ).astype(jnp.bfloat16)
    first_float = first_grad.astype(jnp.float32)
    second_float = second_grad.astype(jnp.float32)
    scaled = first_float * gain_one + second_float * gain_two
    scattered = lax.psum_scatter(
        scaled.astype(jnp.bfloat16), "tp", scatter_dimension=2, tiled=True
    ).astype(jnp.float32)
    row_sums = lax.psum(
        jnp.stack([jnp.sum(scaled, axis=-1), jnp.sum(scaled * normed, axis=-1)]), "tp"
    ) * (1.0 / width)
    triple_grad = (
        jnp.einsum(
            "std,shckt->dchk", first_rows, projected_rounded, preferred_element_type=jnp.float32
        )
        .reshape(weight_triple.shape)
        .astype(jnp.bfloat16)
    )
    triple_share = lax.psum_scatter(triple_grad, "fsdp", scatter_dimension=0, tiled=True)
    output_bias_grad = jnp.sum(whole_cot.astype(jnp.float32), axis=(0, 1))
    wide_sums = jnp.stack(
        [
            jnp.sum(first_float * normed, axis=(0, 1)),
            jnp.sum(first_float, axis=(0, 1)),
            jnp.sum(second_float * normed, axis=(0, 1)),
            jnp.sum(second_float, axis=(0, 1)),
            jnp.where(lax.axis_index("tp") == 0, output_bias_grad, 0.0),
        ]
    )
    wide_sums = lax.psum(wide_sums, ("fsdp", "ctx", "tp"))
    bias_sums = lax.psum(
        jnp.concatenate([triple_bias_grad.reshape(-1), widen_bias_grad]), ("fsdp", "ctx")
    )
    place = lax.axis_index("fsdp")
    vector_size = first_gain.shape[0]
    wide_sums = lax.dynamic_slice_in_dim(wide_sums, place * vector_size, vector_size, 1)
    triple_bias_out = lax.dynamic_slice_in_dim(
        bias_sums[: triple_bias_grad.size].reshape(triple_bias_grad.shape),
        place * triple_bias.shape[2],
        triple_bias.shape[2],
        2,
    )
    widen_bias_out = lax.dynamic_slice_in_dim(
        bias_sums[triple_bias_grad.size :].reshape(widen_bias.shape[0], -1),
        place * widen_bias.shape[1],
        widen_bias.shape[1],
        1,
    )
    own_normed = lax.dynamic_slice_in_dim(normed, feature_start, local_width, 2)
    input_grad = (
        cotangent.astype(jnp.float32)
        + inverse * (scattered - row_sums[0][..., None] - own_normed * row_sums[1][..., None])
    ).astype(jnp.bfloat16)
    return (
        block_output,
        input_grad,
        wide_sums[0],
        wide_sums[1],
        wide_sums[2],
        wide_sums[3],
        sum_pair(triple_share, "ctx"),
        triple_bias_out,
        sum_pair(mixer_share, "ctx"),
        wide_sums[4],
        sum_pair(widen_share, "ctx"),
        widen_bias_out,
        sum_pair(narrow_share, "ctx"),
    )


class Copies:
    def __init__(self, send, recv, local):
        self.send, self.recv, self.local = send, recv, local
        self.remotes = self.locals = 0

    def remote(self, source, target, device):
        index = self.remotes
        self.remotes += 1
        return pltpu.make_async_remote_copy(
            src_ref=source, dst_ref=target, send_sem=self.send.at[index], recv_sem=self.recv.at[index],
            device_id=device, device_id_type=pl.DeviceIdType.MESH,
        )

    def here(self, source, target):
        index = self.locals
        self.locals += 1
        return pltpu.make_async_copy(source, target, self.local.at[index])


def sem_shapes(remotes, local_copies):
    return [pltpu.SemaphoreType.DMA((remotes,)), pltpu.SemaphoreType.DMA((remotes,)),
            pltpu.SemaphoreType.DMA((local_copies,))]


def places(groups):
    z, c, t = lax.axis_index("fsdp"), lax.axis_index("ctx"), lax.axis_index("tp")
    near = t + 1 - 2 * lax.rem(t, 2)
    far = lax.rem(t + 2, 4)
    return z, c, t, near, far


def greet(devices):
    barrier = pltpu.get_barrier_semaphore()
    for device in devices:
        pl.semaphore_signal(barrier, inc=1, device_id=device, device_id_type=pl.DeviceIdType.MESH)
    pl.semaphore_wait(barrier, len(devices))


def aligned(index, step):
    return pl.ds(pl.multiple_of(index * step, step), step)


def gather_kernel(groups, x_in, c_in, pos_in, widen_in, narrow_in, vec_in,
                  x_out, c_out, pos_out, widen_out, narrow_out, vec_out, send, recv, local):
    z, c, t, near, far = places(groups)
    copies = Copies(send, recv, local)
    y_peer, near_peer, far_peer = (z, 1 - c, t), (z, c, near), (z, c, far)
    ring = [lax.rem(z + k, groups) for k in range(1, groups)]
    back = [lax.rem(z + groups - k, groups) for k in range(1, groups)]
    greet([y_peer, near_peer, far_peer] + [(peer, c, t) for peer in ring])
    span, width = x_in.shape[1:]
    started = []

    def start(copy):
        copy.start()
        started.append(copy)
        return copy

    def block(ref, half, feature):
        return ref.at[aligned(half, span), aligned(feature, width)]

    tensors = ((x_in, x_out), (c_in, c_out))
    small = [start(copies.remote(pos_in.at[1 - c], pos_out.at[c], y_peer))]
    small += [start(copies.remote(vec_in, vec_out.at[z], (peer, c, t))) for peer in ring]
    stays = [copies.here(pos_in.at[c], pos_out.at[c]), copies.here(vec_in, vec_out.at[z])]
    swaps, firsts = [], []
    for source, target in tensors:
        swaps.append(start(copies.remote(source.at[1 - c], block(target, c, t), y_peer)))
        firsts.append(
            [start(copies.remote(source.at[c], block(target, c, t), far_peer)),
             start(copies.remote(source.at[c], block(target, c, t), near_peer))]
        )
        stays.append(copies.here(source.at[c], block(target, c, t)))
    rows, hidden = widen_in.shape[0], narrow_in.shape[0]

    def widen_part(group, half):
        return widen_out.at[aligned(group * 2 + half, rows // 2)]

    def narrow_part(group, half):
        return narrow_out.at[aligned(half, hidden // 2), aligned(group, narrow_in.shape[1])]

    shares = []
    for source, part in (
        (widen_in.at[aligned(c, rows // 2)], widen_part),
        (narrow_in.at[aligned(c, hidden // 2)], narrow_part),
    ):
        shares.append(
            [(start(copies.remote(source, part(z, c), (peer, c, t))), part, origin)
             for peer, origin in zip(ring, back)]
        )
    stays.append(copies.here(widen_in, widen_out.at[aligned(z, rows)]))
    stays.append(copies.here(narrow_in, narrow_out.at[:, aligned(z, narrow_in.shape[1])]))
    for copy in stays:
        copy.start()
    received = []

    def second_half(index):
        target = tensors[index][1]
        swaps[index].wait_recv()
        other = block(target, 1 - c, t)
        return [start(copies.remote(other, other, far_peer)), start(copies.remote(other, other, near_peer))]

    def pass_on(index, pair, half):
        target = tensors[index][1]
        pair[0].wait_recv()
        there = block(target, half, far)
        received.append(start(copies.remote(there, there, near_peer)))
        received.append(pair[1])

    def relay(share):
        copy, part, origin = share
        copy.wait_recv()
        there = part(origin, c)
        received.append(start(copies.remote(there, there, y_peer)))

    seconds_x = second_half(0)
    pass_on(0, firsts[0], c)
    relay(shares[0][0])
    seconds_c = second_half(1)
    pass_on(0, seconds_x, 1 - c)
    for share in shares[0][1:]:
        relay(share)
    pass_on(1, firsts[1], c)
    for share in shares[1]:
        relay(share)
    pass_on(1, seconds_c, 1 - c)
    for copy in small + received:
        copy.wait_recv()
    for copy in started:
        copy.wait_send()
    for copy in stays:
        copy.wait()


def gather(groups, block_input, cotangent, positions, widen_weight, narrow_weight, vectors):
    seqs, span, width = block_input.shape
    length, whole = seqs * span, width * 4
    any_space = pl.BlockSpec(memory_space=pl.ANY)
    bf16 = jnp.bfloat16
    return pl.pallas_call(
        functools.partial(gather_kernel, groups),
        in_specs=[any_space] * 6,
        out_specs=[any_space] * 6,
        out_shape=[
            jax.ShapeDtypeStruct((length, whole), bf16),
            jax.ShapeDtypeStruct((length, whole), bf16),
            jax.ShapeDtypeStruct(positions.shape, positions.dtype),
            jax.ShapeDtypeStruct((widen_weight.shape[0] * groups, widen_weight.shape[1]), bf16),
            jax.ShapeDtypeStruct((narrow_weight.shape[0], narrow_weight.shape[1] * groups), bf16),
            jax.ShapeDtypeStruct((groups,) + vectors.shape, bf16),
        ],
        scratch_shapes=sem_shapes(15 + 5 * (groups - 1), 8),
        compiler_params=pltpu.CompilerParams(
            collective_id=0, has_side_effects=True, vmem_limit_bytes=8 * 1024 * 1024
        ),
        name="gather_rows",
    )(block_input, cotangent, positions, widen_weight, narrow_weight, vectors)


class Reduce:
    def __init__(self, groups, copies, arrays, outs, by_rows, owns, others, sums, inbox, done):
        self.groups, self.copies, self.arrays, self.outs, self.by_rows = groups, copies, arrays, outs, by_rows
        self.owns, self.others, self.sums, self.inbox, self.done = owns, others, sums, inbox, done
        self.z, self.c, self.t, _, _ = places(groups)
        self.y_peer = (self.z, 1 - self.c, self.t)
        self.order = list(range(1, groups)) + [0]
        self.loads, self.swaps, self.sends, self.backs, self.keeps = [], [], [], [], []

    def piece(self, a, group, half):
        array = self.arrays[a]
        if self.by_rows[a]:
            return array.at[aligned(group * 2 + half, array.shape[0] // (2 * self.groups))]
        return array.at[aligned(half, array.shape[0] // 2), aligned(group, array.shape[1] // self.groups)]

    def out_half(self, a, half):
        return self.outs[a].at[aligned(half, self.outs[a].shape[0] // 2)]

    def make(self):
        for a in range(len(self.arrays)):
            loads, swaps, sends = [], [], []
            for slot, k in enumerate(self.order):
                group = lax.rem(self.z + k, self.groups)
                loads.append(self.copies.here(self.piece(a, group, self.c), self.owns[a].at[slot]))
                swaps.append(self.copies.remote(self.piece(a, group, 1 - self.c), self.others[a].at[slot], self.y_peer))
                if k:
                    sends.append(self.copies.remote(
                        self.sums[a].at[slot], self.inbox[a].at[slot], (group, self.c, self.t)))
            self.loads.append(loads)
            self.swaps.append(swaps)
            self.sends.append(sends)
            self.backs.append(self.copies.remote(self.done[a], self.out_half(a, self.c), self.y_peer))
            self.keeps.append(self.copies.here(self.done[a], self.out_half(a, self.c)))

    def start(self, a):
        for swap, load in zip(self.swaps[a], self.loads[a]):
            swap.start()
            load.start()

    def add(self, a, slot):
        self.loads[a][slot].wait()
        self.swaps[a][slot].wait_recv()
        total = self.owns[a][slot].astype(jnp.float32) + self.others[a][slot].astype(jnp.float32)
        self.sums[a][slot] = total.astype(jnp.bfloat16)
        if slot < self.groups - 1:
            self.sends[a][slot].start()

    def total(self, a):
        total = self.sums[a][self.groups - 1].astype(jnp.float32)
        for slot in range(self.groups - 1):
            self.sends[a][slot].wait_recv()
            total = total + self.inbox[a][slot].astype(jnp.float32)
        self.done[a][...] = total.astype(jnp.bfloat16)
        self.backs[a].start()
        self.keeps[a].start()

    def finish(self):
        for a in range(len(self.arrays)):
            for swap in self.swaps[a]:
                swap.wait_send()
            for send in self.sends[a]:
                send.wait_send()
            self.backs[a].wait()
            self.keeps[a].wait()


def reduce_shapes(groups, shapes, by_rows):
    owns, others, sums, inbox, done, outs = [], [], [], [], [], []
    for (rows, columns), along in zip(shapes, by_rows):
        part = (rows // (2 * groups), columns) if along else (rows // 2, columns // groups)
        owns.append(pltpu.VMEM((groups,) + part, jnp.bfloat16))
        others.append(pltpu.VMEM((groups,) + part, jnp.bfloat16))
        sums.append(pltpu.VMEM((groups,) + part, jnp.bfloat16))
        inbox.append(pltpu.VMEM((groups - 1,) + part, jnp.bfloat16))
        done.append(pltpu.VMEM(part, jnp.bfloat16))
        outs.append(jax.ShapeDtypeStruct((2 * part[0], part[1]), jnp.bfloat16))
    return owns + others + sums + inbox + done, outs


def reduce_from(groups, copies, arrays, outs, by_rows, scratch):
    n = len(arrays)
    cut = [scratch[n * i : n * (i + 1)] for i in range(5)]
    made = Reduce(groups, copies, arrays, outs, by_rows, *cut)
    made.make()
    return made


def attend_reduce_kernel(block, scale, groups, items, by_rows, qkv_ref, grad_ref, base_ref, *refs):
    n = len(by_rows)
    arrays, refs = refs[:n], refs[n:]
    back_ref, mixed_ref, refs = refs[0], refs[1], refs[2:]
    outs, refs = refs[:n], refs[n:]
    attention, refs = refs[:11], refs[11:]
    scratch, (send, recv, local) = refs[:-3], refs[-3:]
    item = pl.program_id(0)
    reduce = reduce_from(groups, Copies(send, recv, local), arrays, outs, by_rows, scratch)
    blocks = grad_ref.shape[0] * grad_ref.shape[3] // block
    pieces = [(a, slot) for a in range(n) for slot in range(groups)]
    plan = {}
    total = items * blocks * (blocks + 1) // 2
    for index, piece in enumerate(pieces):
        due = total * (1.5 + index) / (len(pieces) + 1.0)
        steps = [(i, b) for i in range(items) for b in range(blocks)]
        costs = [i * blocks * (blocks + 1) // 2 + b * (b + 1) // 2 for i, b in steps]
        at = max(k for k in range(len(steps)) if costs[k] <= due)
        plan.setdefault(steps[at], []).append(piece)

    def begin():
        z, c, t, _, _ = places(groups)
        greet([(z, 1 - c, t)] + [(lax.rem(z + k, groups), c, t) for k in range(1, groups)])
        for a in range(n):
            reduce.start(a)

    pl.when(item == 0)(begin)

    def between(b):
        for i in range(items):
            for a, slot in plan.get((i, b), ()):
                pl.when(item == i)(functools.partial(reduce.add, a, slot))

    attend_kernel(block, scale, between, qkv_ref, grad_ref, base_ref, back_ref, mixed_ref, *attention)

    def end():
        for a in range(n):
            reduce.total(a)
        reduce.finish()

    pl.when(item == items - 1)(end)


def attend_reduce(by_heads, grad_heads, item_base, scale, groups, arrays, by_rows):
    parts, items, unused, head_size, span = by_heads.shape
    length = parts * span
    block = min(256, span)
    wide = pltpu.VMEM((head_size, length), jnp.bfloat16)
    tall = pltpu.VMEM((length, head_size), jnp.bfloat16)
    total = pltpu.VMEM((length, head_size), jnp.float32)
    shapes, outs = reduce_shapes(groups, [array.shape for array in arrays], by_rows)
    any_space = pl.BlockSpec(memory_space=pl.ANY)
    n = len(arrays)
    return pl.pallas_call(
        functools.partial(attend_reduce_kernel, block, scale, groups, items, by_rows),
        grid=(items,),
        in_specs=[
            pl.BlockSpec((parts, 1, 3, head_size, span), lambda i: (0, i, 0, 0, 0)),
            pl.BlockSpec((parts, 1, head_size, span), lambda i: (0, i, 0, 0)),
            pl.BlockSpec((1, 1, length), lambda i: (i, 0, 0)),
        ] + [any_space] * n,
        out_specs=[
            pl.BlockSpec((parts, 1, 3, head_size, span), lambda i: (0, i, 0, 0, 0)),
            pl.BlockSpec((parts, 1, head_size, span), lambda i: (0, i, 0, 0)),
        ] + [any_space] * n,
        out_shape=[
            jax.ShapeDtypeStruct(by_heads.shape, jnp.bfloat16),
            jax.ShapeDtypeStruct(grad_heads.shape, jnp.bfloat16),
        ] + outs,
        scratch_shapes=[wide, tall, wide, tall, wide, tall, wide, tall,
                        pltpu.VMEM((length, 128), jnp.float32), total, total]
        + shapes + sem_shapes(n * 2 * groups, n * (groups + 1)),
        compiler_params=pltpu.CompilerParams(
            collective_id=1, has_side_effects=True, vmem_limit_bytes=48 * 1024 * 1024
        ),
        cost_estimate=pl.CostEstimate(
            flops=7 * items * length * length * 256,
            bytes_accessed=4 * by_heads.size,
            transcendentals=items * length * length // 2,
        ),
        name="attend_reduce",
    )(by_heads, grad_heads, item_base, *arrays)


def scatter_kernel(groups, by_rows, out_part, grad_part, stats_in, wide_in, bias_in, *refs):
    n = len(by_rows)
    arrays, refs = refs[:n], refs[n:]
    out_ref, grad_ref, stats_out, wide_out, bias_out = refs[:5]
    outs, refs = refs[5 : 5 + n], refs[5 + n :]
    (mine, theirs, near_box, far_send, far_box, done,
     row_box, row_sum, wide_box, wide_two, wide_three, bias_two, bias_three) = refs[:13]
    scratch, (send, recv, local) = refs[13:-3], refs[-3:]
    z, c, t, near, far = places(groups)
    copies = Copies(send, recv, local)
    y_peer = (z, 1 - c, t)
    near_peer, far_peer, cross_peer = (z, c, near), (z, c, far), (z, c, 3 - t)
    ring = [lax.rem(z + k, groups) for k in range(1, groups)]
    greet([y_peer, near_peer, far_peer, cross_peer] + [(peer, c, t) for peer in ring])
    span, width = out_ref.shape[1:]
    length = 2 * span
    chunk = span // 2
    started, finals = [], []

    def start(copy):
        copy.start()
        started.append(copy)
        return copy

    def columns(ref, feature):
        return ref.at[:, aligned(feature, width)]

    nears, loads = [], []
    row = lax.rem(t, 2)
    for index, part in enumerate((out_part, grad_part)):
        nears.append([
            start(copies.remote(columns(part, lax.rem(near + 2, 4)), near_box.at[index, 0], near_peer)),
            start(copies.remote(columns(part, near), near_box.at[index, 1], near_peer)),
        ])
        pair = [copies.here(columns(part, far), theirs.at[index]), copies.here(columns(part, t), mine.at[index])]
        for copy in pair:
            copy.start()
        loads.append(pair)
    tp_peers = [((t + k) - 4 * ((t + k) // 4)) for k in range(1, 4)]
    row_box[t] = stats_in[0:2]
    wide_box[t] = wide_in[...]
    rows_sent = [start(copies.remote(row_box.at[t], row_box.at[t], (z, c, peer))) for peer in tp_peers]
    wides_sent = [start(copies.remote(wide_box.at[t], wide_box.at[t], (z, c, peer))) for peer in tp_peers]
    bias_two[c] = bias_in[...]
    bias_swap = start(copies.remote(bias_two.at[c], bias_two.at[c], y_peer))
    reduce = reduce_from(groups, copies, arrays, outs, by_rows, scratch)
    for a in range(n):
        reduce.start(a)

    def rows_of(step):
        if step < 2:
            return pl.ds(pl.multiple_of((1 - c) * span + step * chunk, chunk), chunk)
        return pl.ds(pl.multiple_of(c * span + (step - 2) * chunk, chunk), chunk)

    fars = []
    for index in range(2):
        nears[index][0].wait_recv()
        loads[index][0].wait()
        sent = []
        for step in range(4):
            rows = rows_of(step)
            far_send[index, rows] = (
                theirs[index, rows].astype(jnp.float32) + near_box[index, 0, rows].astype(jnp.float32)
            ).astype(jnp.bfloat16)
            sent.append(start(copies.remote(far_send.at[index, rows], far_box.at[index, rows], far_peer)))
        fars.append(sent)
    for copy in rows_sent + wides_sent:
        copy.wait_recv()
    totals = row_box[0] + row_box[1] + row_box[2] + row_box[3]
    row_sum[0:2] = totals
    row_sum[2:4] = stats_in[2:4]
    half_rows = row_sum.shape[1] // 2
    here_rows, there_rows = aligned(c, half_rows), aligned(1 - c, half_rows)
    finals.append(start(copies.remote(row_sum.at[:, there_rows], stats_out.at[c], y_peer)))
    keep_stats = copies.here(row_sum.at[:, here_rows], stats_out.at[c])
    keep_stats.start()
    wide_two[c] = wide_box[0] + wide_box[1] + wide_box[2] + wide_box[3]
    wide_swap = start(copies.remote(wide_two.at[c], wide_two.at[c], y_peer))
    bias_swap.wait_recv()
    bias_three[z] = bias_two[0] + bias_two[1]
    bias_sent = [start(copies.remote(bias_three.at[z], bias_three.at[z], (peer, c, t))) for peer in ring]
    wide_swap.wait_recv()
    wide_three[z] = wide_two[0] + wide_two[1]
    wide_sent = [start(copies.remote(wide_three.at[z], wide_three.at[z], (peer, c, t))) for peer in ring]

    keeps = []

    def close(index, step, target):
        rows = rows_of(step)
        fars[index][step].wait_recv()
        done[index, rows] = (
            mine[index, rows].astype(jnp.float32)
            + near_box[index, 1, rows].astype(jnp.float32)
            + far_box[index, rows].astype(jnp.float32)
        ).astype(jnp.bfloat16)
        place = pl.ds((step % 2) * chunk, chunk)
        if step < 2:
            finals.append(start(copies.remote(done.at[index, rows], target.at[c, place], y_peer)))
        else:
            keep = copies.here(done.at[index, rows], target.at[c, place])
            keep.start()
            keeps.append(keep)

    slots = [(a, slot) for a in range(n) for slot in range(groups)]
    for index, target in enumerate((out_ref, grad_ref)):
        nears[index][1].wait_recv()
        loads[index][1].wait()
        for step in range(4):
            close(index, step, target)
            if index == 0:
                take = len(slots) // (4 - step) if step < 3 else len(slots)
                for a, slot in slots[:take]:
                    reduce.add(a, slot)
                slots = slots[take:]
        if index == 0:
            for copy in bias_sent + wide_sent:
                copy.wait_recv()
            bias_total, wide_total = bias_three[0], wide_three[0]
            for group in range(1, groups):
                bias_total = bias_total + bias_three[group]
                wide_total = wide_total + wide_three[group]
            bias_out[...] = bias_total
            wide_out[...] = wide_total
            for a in range(n):
                reduce.total(a)
    for copy in finals:
        copy.wait_recv()
    for copy in started:
        copy.wait_send()
    for copy in keeps + [keep_stats]:
        copy.wait()
    reduce.finish()


def scatter(groups, out_part, grad_part, stats, wide, bias, arrays, by_rows):
    length, whole = out_part.shape
    width, span = whole // 4, length // 2
    any_space = pl.BlockSpec(memory_space=pl.ANY)
    in_vmem = pl.BlockSpec(memory_space=pltpu.VMEM)
    n = len(arrays)
    shapes, outs = reduce_shapes(groups, [array.shape for array in arrays], by_rows)
    bf16, f32 = jnp.bfloat16, jnp.float32
    return pl.pallas_call(
        functools.partial(scatter_kernel, groups, by_rows),
        in_specs=[any_space] * 2 + [in_vmem] * 3 + [any_space] * n,
        out_specs=[any_space] * 3 + [in_vmem] * 2 + [any_space] * n,
        out_shape=[
            jax.ShapeDtypeStruct((2, span, width), bf16),
            jax.ShapeDtypeStruct((2, span, width), bf16),
            jax.ShapeDtypeStruct((2, 4, stats.shape[1] // 2, stats.shape[2]), f32),
            jax.ShapeDtypeStruct(wide.shape, f32),
            jax.ShapeDtypeStruct(bias.shape, f32),
        ] + outs,
        scratch_shapes=[
            pltpu.VMEM((2, length, width), bf16),
            pltpu.VMEM((2, length, width), bf16),
            pltpu.VMEM((2, 2, length, width), bf16),
            pltpu.VMEM((2, length, width), bf16),
            pltpu.VMEM((2, length, width), bf16),
            pltpu.VMEM((2, length, width), bf16),
            pltpu.VMEM((4, 2) + stats.shape[1:], f32),
            pltpu.VMEM(stats.shape, f32),
            pltpu.VMEM((4,) + wide.shape, f32),
            pltpu.VMEM((2,) + wide.shape, f32),
            pltpu.VMEM((groups,) + wide.shape, f32),
            pltpu.VMEM((2,) + bias.shape, f32),
            pltpu.VMEM((groups,) + bias.shape, f32),
        ] + shapes + sem_shapes(26 + 2 * (groups - 1) + n * 2 * groups, 9 + n * (groups + 1)),
        compiler_params=pltpu.CompilerParams(
            collective_id=2, has_side_effects=True, vmem_limit_bytes=40 * 1024 * 1024
        ),
        name="scatter_rows",
    )(out_part, grad_part, stats, wide, bias, *arrays)


def shards_sequence(
    block_input,
    positions,
    first_gain,
    first_shift,
    second_gain,
    second_shift,
    triple_weight,
    triple_bias,
    mixer_weight,
    output_bias,
    widen_weight,
    widen_bias,
    narrow_weight,
    cotangent,
):
    seqs, span, local_width = block_input.shape
    length = seqs * span
    groups = lax.axis_size("fsdp")
    vectors = (first_gain, first_shift, second_gain, second_shift, output_bias, triple_bias, widen_bias)
    flat = jnp.concatenate([vector.reshape(-1) for vector in vectors])
    padded = -(-flat.size // 2048) * 2048
    packed = jnp.pad(flat, (0, padded - flat.size)).reshape(-1, 128)
    rows_in, cot_rows, places_out, weight_widen, weight_narrow, small = gather(
        groups, block_input, cotangent, positions.reshape(seqs, span // 128, 128), widen_weight, narrow_weight, packed
    )
    small = small.reshape(groups, -1)
    pieces = []
    offset = 0
    for vector in vectors:
        pieces.append(small[:, offset : offset + vector.size].astype(jnp.float32))
        offset += vector.size
    gain_one, shift_one, gain_two, shift_two, bias_output = [piece.reshape(-1) for piece in pieces[:5]]
    bias_triple = jnp.transpose(
        pieces[5].reshape((groups,) + triple_bias.shape), (1, 2, 0, 3)
    ).reshape(triple_bias.shape[0], triple_bias.shape[1], -1)
    bias_widen = jnp.transpose(pieces[6].reshape((groups,) + widen_bias.shape), (1, 0, 2)).reshape(-1)
    weight_triple = lax.all_gather(triple_weight, "fsdp", axis=0, tiled=True)
    weight_mixer = lax.all_gather(mixer_weight, "fsdp", axis=1, tiled=True)
    width = weight_triple.shape[0]
    heads_local, head_size = bias_triple.shape[1:]
    scale = head_size ** (-0.5)
    half = ROT // 2
    float_rows = rows_in.astype(jnp.float32)
    mean = jnp.mean(float_rows, axis=-1)
    centred = float_rows - mean[:, None]
    inverse = lax.rsqrt(jnp.mean(centred * centred, axis=-1) + norm_eps)
    normed = centred * inverse[:, None]
    first_rows = (normed * gain_one + shift_one).astype(jnp.bfloat16)
    second_rows = (normed * gain_two + shift_two).astype(jnp.bfloat16)
    widened = jnp.einsum("td,df->tf", second_rows, weight_widen, preferred_element_type=jnp.float32) + bias_widen
    activated_float, slope = gelu_parts(widened)
    activated = activated_float.astype(jnp.bfloat16)
    hidden_grad = jnp.einsum("te,fe->tf", cot_rows, weight_narrow, preferred_element_type=jnp.float32) * slope
    widen_bias_grad = jnp.sum(hidden_grad, axis=0)
    hidden_rounded = hidden_grad.astype(jnp.bfloat16)
    narrow_grad = jnp.einsum(
        "tf,te->fe", activated, cot_rows, preferred_element_type=jnp.float32
    ).astype(jnp.bfloat16)
    widen_grad = jnp.einsum(
        "td,tf->df", second_rows, hidden_rounded, preferred_element_type=jnp.float32
    ).astype(jnp.bfloat16)
    second_grad = jnp.einsum(
        "tf,df->td", hidden_rounded, weight_widen, preferred_element_type=jnp.float32
    ).astype(jnp.bfloat16)
    all_positions = places_out.reshape(1, length)
    cosine, sine = rotary_tables(all_positions, ROT)
    weight_four = weight_triple.reshape(width, 3, heads_local, head_size)
    projected = jnp.einsum(
        "std,dchk->shckt", first_rows[None], weight_four, preferred_element_type=jnp.float32
    )
    projected = projected + jnp.transpose(bias_triple, (1, 0, 2))[None, :, :, :, None]
    turned = rotate_forward(projected[:, :, :2], cosine, sine, half)
    triple = jnp.concatenate([turned, projected[:, :, 2:]], axis=2).astype(jnp.bfloat16)
    mixer_four = weight_mixer.reshape(heads_local, head_size, width)
    mixed_grad = jnp.einsum(
        "ste,hke->shkt", cot_rows[None], mixer_four, preferred_element_type=jnp.float32
    ).astype(jnp.bfloat16)
    base = (jnp.arange(length, dtype=jnp.int32)[None, :] - all_positions).astype(jnp.float32)
    item_base = jnp.broadcast_to(base[:, None, :], (heads_local, 1, length))
    back_heads, mixed, widen_share, narrow_share = attend_reduce(
        triple, mixed_grad, item_base, scale, groups, (widen_grad, narrow_grad), (True, False)
    )
    back_float = back_heads.astype(jnp.float32)
    attention_part = jnp.einsum(
        "shkt,hke->ste", mixed, mixer_four, preferred_element_type=jnp.float32
    )[0]
    branches = attention_part + jnp.einsum(
        "tf,fe->te", activated, weight_narrow, preferred_element_type=jnp.float32
    )
    mixer_grad = (
        jnp.einsum("shkt,ste->hke", mixed, cot_rows[None], preferred_element_type=jnp.float32)
        .reshape(weight_mixer.shape)
        .astype(jnp.bfloat16)
    )
    unturned = rotate_back(back_float[:, :, :2], cosine, sine, half)
    projected_grad = jnp.concatenate([unturned, back_float[:, :, 2:]], axis=2)
    triple_bias_grad = jnp.transpose(jnp.sum(projected_grad, axis=(0, 4)), (1, 0, 2))
    projected_rounded = projected_grad.astype(jnp.bfloat16)
    first_grad = jnp.einsum(
        "shckt,dchk->std", projected_rounded, weight_four, preferred_element_type=jnp.float32
    )[0].astype(jnp.bfloat16)
    first_float = first_grad.astype(jnp.float32)
    second_float = second_grad.astype(jnp.float32)
    scaled = first_float * gain_one + second_float * gain_two
    stats = jnp.stack(
        [jnp.sum(scaled, axis=-1) * (1.0 / width), jnp.sum(scaled * normed, axis=-1) * (1.0 / width), mean, inverse]
    ).reshape(4, length // 128, 128)
    triple_grad = (
        jnp.einsum(
            "std,shckt->dchk", first_rows[None], projected_rounded, preferred_element_type=jnp.float32
        )
        .reshape(width, -1)
        .astype(jnp.bfloat16)
    )
    zero = jnp.zeros((width,), jnp.float32)
    wide_sums = jnp.stack(
        [
            jnp.sum(first_float * normed, axis=0),
            jnp.sum(first_float, axis=0),
            jnp.sum(second_float * normed, axis=0),
            jnp.sum(second_float, axis=0),
            jnp.where(lax.axis_index("tp") == 0, jnp.sum(cot_rows.astype(jnp.float32), axis=0), 0.0),
            zero, zero, zero,
        ]
    )
    bias_flat = jnp.concatenate([triple_bias_grad.reshape(-1), widen_bias_grad])
    bias_padded = -(-bias_flat.size // 1024) * 1024
    bias_rows = jnp.pad(bias_flat, (0, bias_padded - bias_flat.size)).reshape(-1, 128)
    summed, scattered, row_stats, wide_sums, bias_sums, triple_share, mixer_share = scatter(
        groups, branches.astype(jnp.bfloat16), scaled.astype(jnp.bfloat16), stats, wide_sums, bias_rows,
        (triple_grad, mixer_grad), (True, False),
    )
    bias_sums = bias_sums.reshape(-1)
    feature_start = lax.axis_index("tp") * local_width
    bias_slice = lax.dynamic_slice_in_dim(bias_output, feature_start, local_width, 0)
    own_rows = block_input.astype(jnp.float32)
    block_output = (own_rows + summed.astype(jnp.float32) + bias_slice).astype(jnp.bfloat16)
    row_stats = row_stats.reshape(seqs, 4, span)
    own_normed = (own_rows - row_stats[:, 2, :, None]) * row_stats[:, 3, :, None]
    input_grad = (
        cotangent.astype(jnp.float32)
        + row_stats[:, 3, :, None]
        * (scattered.astype(jnp.float32) - row_stats[:, 0, :, None] - own_normed * row_stats[:, 1, :, None])
    ).astype(jnp.bfloat16)
    place = lax.axis_index("fsdp")
    vector_size = first_gain.shape[0]
    wide_sums = lax.dynamic_slice_in_dim(wide_sums, place * vector_size, vector_size, 1)
    triple_bias_out = lax.dynamic_slice_in_dim(
        bias_sums[: triple_bias_grad.size].reshape(triple_bias_grad.shape),
        place * triple_bias.shape[2],
        triple_bias.shape[2],
        2,
    )
    widen_bias_out = lax.dynamic_slice_in_dim(
        bias_sums[triple_bias_grad.size : bias_flat.size].reshape(widen_bias.shape[0], -1),
        place * widen_bias.shape[1],
        widen_bias.shape[1],
        1,
    )
    return (
        block_output,
        input_grad,
        wide_sums[0],
        wide_sums[1],
        wide_sums[2],
        wide_sums[3],
        triple_share.astype(jnp.float32).reshape(triple_weight.shape),
        triple_bias_out,
        mixer_share.astype(jnp.float32),
        wide_sums[4],
        widen_share.astype(jnp.float32),
        widen_bias_out,
        narrow_share.astype(jnp.float32),
    )


def shards(block_input, *others):
    seqs = block_input.shape[0]
    if seqs == 2 and lax.axis_size("ctx") == 2 and lax.axis_size("tp") == 4 and lax.axis_size("fsdp") > 1:
        return shards_sequence(block_input, *others)
    return shards_general(block_input, *others)


def solution(mesh):
    in_specs = (
        P("fsdp", "ctx", "tp"),
        P("fsdp", "ctx"),
        P("fsdp"),
        P("fsdp"),
        P("fsdp"),
        P("fsdp"),
        P("fsdp", None, "tp"),
        P(None, "tp", "fsdp"),
        P("tp", "fsdp"),
        P("fsdp"),
        P("fsdp", "tp"),
        P("tp", "fsdp"),
        P("tp", "fsdp"),
        P("fsdp", "ctx", "tp"),
    )
    out_specs = (
        P("fsdp", "ctx", "tp"),
        P("fsdp", "ctx", "tp"),
        P("fsdp"),
        P("fsdp"),
        P("fsdp"),
        P("fsdp"),
        P("fsdp", None, "tp"),
        P(None, "tp", "fsdp"),
        P("tp", "fsdp"),
        P("fsdp"),
        P("fsdp", "tp"),
        P("tp", "fsdp"),
        P("tp", "fsdp"),
    )
    return jax.shard_map(shards, mesh=mesh, in_specs=in_specs, out_specs=out_specs, check_vma=False)
```

```python
import functools
import math

import jax
import jax.numpy as jnp
from jax import lax
from jax.experimental import pallas as pl
from jax.experimental.pallas import tpu as pltpu
from jax.sharding import PartitionSpec as P

ROT = 16


norm_eps = 1e-05
masked_score = -1e30


def normalize(rows):
    centred = rows - jnp.mean(rows, axis=-1, keepdims=True)
    inverse = lax.rsqrt(jnp.mean(centred * centred, axis=-1, keepdims=True) + norm_eps)
    return (centred * inverse, inverse)


def gelu_parts(widened):
    cumulative = 0.5 * (1.0 + lax.erf(widened * (1.0 / math.sqrt(2.0))))
    density = jnp.exp(-0.5 * widened * widened) * (1.0 / math.sqrt(2.0 * math.pi))
    return (widened * cumulative, cumulative + widened * density)


def rotary_tables(positions, rotary):
    half = rotary // 2
    freqs = jnp.exp(jnp.arange(half, dtype=jnp.float32) * (-2.0 * math.log(10000.0) / rotary))
    angles = positions.astype(jnp.float32)[:, None, :] * freqs[None, :, None]
    return (jnp.cos(angles)[:, None, None], jnp.sin(angles)[:, None, None])


def rotate_forward(block, cosine, sine, half):
    first = block[..., :half, :]
    second = block[..., half : 2 * half, :]
    return jnp.concatenate(
        [first * cosine - second * sine, second * cosine + first * sine, block[..., 2 * half :, :]],
        axis=-2,
    )


def rotate_back(block, cosine, sine, half):
    first = block[..., :half, :]
    second = block[..., half : 2 * half, :]
    return jnp.concatenate(
        [first * cosine + second * sine, second * cosine - first * sine, block[..., 2 * half :, :]],
        axis=-2,
    )


def attend_kernel(block, scale, between, qkv_ref, grad_ref, base_ref, back_ref, mixed_ref,
                  queries, query_rows, keys, key_rows, values, value_rows, grads, grad_rows,
                  base_rows, key_sum, value_sum):
    parts, head_size, span = grad_ref.shape[0], grad_ref.shape[2], grad_ref.shape[3]
    length = parts * span
    for part in range(parts):
        at = pl.ds(part * span, span)
        queries[:, at] = (qkv_ref[part, 0, 0].astype(jnp.float32) * scale).astype(jnp.bfloat16)
        keys[:, at] = qkv_ref[part, 0, 1]
        values[:, at] = qkv_ref[part, 0, 2]
        grads[:, at] = grad_ref[part, 0]
    for source, target in (
        (queries, query_rows),
        (keys, key_rows),
        (values, value_rows),
        (grads, grad_rows),
    ):
        target[...] = source[...].astype(jnp.float32).T.astype(jnp.bfloat16)
    base_row = base_ref[0]
    base_rows[...] = jnp.broadcast_to(base_row, (128, length)).T
    for start in range(0, length, block):
        between(start // block)
        count = start + block
        here = slice(start, count)
        scores = jnp.dot(key_rows[:count], queries[:, here], preferred_element_type=jnp.float32)
        wide_base = jnp.concatenate([base_rows[:count]] * (block // 128), axis=1)
        same = wide_base == base_row[:, here]
        key_index = lax.broadcasted_iota(jnp.int32, (block, block), 0)
        query_index = lax.broadcasted_iota(jnp.int32, (block, block), 1)
        last = jnp.where(
            same[start:] & (key_index <= query_index), scores[start:], masked_score
        )
        if start:
            earlier = jnp.where(same[:start], scores[:start], masked_score)
            scores = jnp.concatenate([earlier, last], axis=0)
        else:
            scores = last
        top = jnp.max(scores, axis=0, keepdims=True)
        raised = jnp.exp(scores - top)
        probs = raised * (1.0 / jnp.sum(raised, axis=0, keepdims=True))
        weights = probs.astype(jnp.bfloat16)
        mixed = jnp.dot(values[:, :count], weights, preferred_element_type=jnp.float32).astype(
            jnp.bfloat16
        )
        grad_block = grads[:, here]
        delta = jnp.sum(
            mixed.astype(jnp.float32) * grad_block.astype(jnp.float32), axis=0, keepdims=True
        )
        prob_grads = jnp.dot(value_rows[:count], grad_block, preferred_element_type=jnp.float32)
        score_grads = (probs * (prob_grads - delta)).astype(jnp.bfloat16)
        query_part = jnp.dot(keys[:, :count], score_grads, preferred_element_type=jnp.float32)
        key_part = jnp.dot(score_grads, query_rows[here], preferred_element_type=jnp.float32)
        value_part = jnp.dot(weights, grad_rows[here], preferred_element_type=jnp.float32)
        if start:
            key_sum[:start] += key_part[:start]
            value_sum[:start] += value_part[:start]
        key_sum[here] = key_part[start:]
        value_sum[here] = value_part[start:]
        part, inside = start // span, start % span
        mixed_ref[part, 0, :, inside : inside + block] = mixed
        back_ref[part, 0, 0, :, inside : inside + block] = (query_part * scale).astype(jnp.bfloat16)
    for part in range(parts):
        at = pl.ds(part * span, span)
        back_ref[part, 0, 1] = key_sum[at].T.astype(jnp.bfloat16)
        back_ref[part, 0, 2] = value_sum[at].T.astype(jnp.bfloat16)


def attend(by_heads, grad_heads, item_base, scale):
    parts, items, unused, head_size, span = by_heads.shape
    length = parts * span
    block = min(256, span)
    wide = pltpu.VMEM((head_size, length), jnp.bfloat16)
    tall = pltpu.VMEM((length, head_size), jnp.bfloat16)
    total = pltpu.VMEM((length, head_size), jnp.float32)
    return pl.pallas_call(
        functools.partial(attend_kernel, block, scale, lambda step: None),
        grid=(items,),
        in_specs=[
            pl.BlockSpec((parts, 1, 3, head_size, span), lambda i: (0, i, 0, 0, 0)),
            pl.BlockSpec((parts, 1, head_size, span), lambda i: (0, i, 0, 0)),
            pl.BlockSpec((1, 1, length), lambda i: (i, 0, 0)),
        ],
        out_specs=[
            pl.BlockSpec((parts, 1, 3, head_size, span), lambda i: (0, i, 0, 0, 0)),
            pl.BlockSpec((parts, 1, head_size, span), lambda i: (0, i, 0, 0)),
        ],
        out_shape=[
            jax.ShapeDtypeStruct(by_heads.shape, jnp.bfloat16),
            jax.ShapeDtypeStruct(grad_heads.shape, jnp.bfloat16),
        ],
        scratch_shapes=[wide, tall, wide, tall, wide, tall, wide, tall,
                        pltpu.VMEM((length, 128), jnp.float32), total, total],
        compiler_params=pltpu.CompilerParams(vmem_limit_bytes=48 * 1024 * 1024),
        cost_estimate=pl.CostEstimate(
            flops=7 * items * length * length * 256,
            bytes_accessed=4 * by_heads.size,
            transcendentals=items * length * length // 2,
        ),
    )(by_heads, grad_heads, item_base)


def sum_pair(share, axis):
    size = lax.axis_size(axis)
    if size == 2:
        other = lax.ppermute(share, axis, [(0, 1), (1, 0)])
        return share.astype(jnp.float32) + other.astype(jnp.float32)
    return lax.psum(share, axis).astype(jnp.float32)


def shards_general(
    block_input,
    positions,
    first_gain,
    first_shift,
    second_gain,
    second_shift,
    triple_weight,
    triple_bias,
    mixer_weight,
    output_bias,
    widen_weight,
    widen_bias,
    narrow_weight,
    cotangent,
):
    seqs, local_tokens, local_width = block_input.shape
    vectors = (first_gain, first_shift, second_gain, second_shift, output_bias, triple_bias, widen_bias)
    small = lax.all_gather(
        jnp.concatenate([vector.reshape(-1) for vector in vectors]), "fsdp", axis=0, tiled=False
    )
    groups = small.shape[0]
    pieces = []
    offset = 0
    for vector in vectors:
        pieces.append(small[:, offset : offset + vector.size].astype(jnp.float32))
        offset += vector.size
    gain_one, shift_one, gain_two, shift_two, bias_output = [
        piece.reshape(-1) for piece in pieces[:5]
    ]
    bias_triple = jnp.transpose(
        pieces[5].reshape((groups,) + triple_bias.shape), (1, 2, 0, 3)
    ).reshape(triple_bias.shape[0], triple_bias.shape[1], -1)
    bias_widen = jnp.transpose(
        pieces[6].reshape((groups,) + widen_bias.shape), (1, 0, 2)
    ).reshape(-1)
    all_positions = lax.all_gather(positions, "ctx", axis=1, tiled=True)
    whole_input = lax.all_gather(block_input, "tp", axis=2, tiled=True)
    weight_triple = lax.all_gather(triple_weight, "fsdp", axis=0, tiled=True)
    whole_cot = lax.all_gather(cotangent, "tp", axis=2, tiled=True)
    mixer_rows = mixer_weight.shape[0]
    joined = lax.all_gather(
        jnp.concatenate([mixer_weight, narrow_weight], axis=0), "fsdp", axis=1, tiled=True
    )
    weight_mixer, weight_narrow = joined[:mixer_rows], joined[mixer_rows:]
    weight_widen = lax.all_gather(widen_weight, "fsdp", axis=0, tiled=True)
    width = weight_triple.shape[0]
    heads_local, head_size = bias_triple.shape[1:]
    feature_start = lax.axis_index("tp") * local_width
    scale = head_size ** (-0.5)
    half = ROT // 2
    normed, inverse = normalize(whole_input.astype(jnp.float32))
    first_rows = (normed * gain_one + shift_one).astype(jnp.bfloat16)
    second_rows = (normed * gain_two + shift_two).astype(jnp.bfloat16)
    cosine, sine = rotary_tables(positions, ROT)
    weight_four = weight_triple.reshape(width, 3, heads_local, head_size)
    projected = jnp.einsum(
        "std,dchk->shckt", first_rows, weight_four, preferred_element_type=jnp.float32
    )
    projected = projected + jnp.transpose(bias_triple, (1, 0, 2))[None, :, :, :, None]
    turned = rotate_forward(projected[:, :, :2], cosine, sine, half)
    triple = jnp.concatenate([turned, projected[:, :, 2:]], axis=2).astype(jnp.bfloat16)
    parts = lax.axis_size("ctx")
    items = seqs * heads_local // parts
    by_heads = lax.all_to_all(
        triple.reshape(parts, items, 3, head_size, local_tokens),
        "ctx",
        split_axis=0,
        concat_axis=0,
        tiled=True,
    )
    mixer_four = weight_mixer.reshape(heads_local, head_size, width)
    mixed_grad = jnp.einsum(
        "ste,hke->shkt", whole_cot, mixer_four, preferred_element_type=jnp.float32
    ).astype(jnp.bfloat16)
    grad_heads = lax.all_to_all(
        mixed_grad.reshape(parts, items, head_size, local_tokens),
        "ctx",
        split_axis=0,
        concat_axis=0,
        tiled=True,
    )
    length = all_positions.shape[1]
    item_seq = (lax.axis_index("ctx") * items + jnp.arange(items, dtype=jnp.int32)) // heads_local
    base = (jnp.arange(length, dtype=jnp.int32)[None, :] - all_positions).astype(jnp.float32)
    item_base = jnp.take(base, item_seq, axis=0)[:, None, :]
    back_heads, mixed = attend(by_heads, grad_heads, item_base, scale)
    mixed_tokens = lax.all_to_all(
        mixed, "ctx", split_axis=0, concat_axis=0, tiled=True
    ).reshape(seqs, heads_local, head_size, local_tokens)
    back_float = (
        lax.all_to_all(back_heads, "ctx", split_axis=0, concat_axis=0, tiled=True)
        .reshape(seqs, heads_local, 3, head_size, local_tokens)
        .astype(jnp.float32)
    )
    widened = (
        jnp.einsum("std,df->stf", second_rows, weight_widen, preferred_element_type=jnp.float32)
        + bias_widen
    )
    activated_float, slope = gelu_parts(widened)
    activated = activated_float.astype(jnp.bfloat16)
    hidden_grad = (
        jnp.einsum("ste,fe->stf", whole_cot, weight_narrow, preferred_element_type=jnp.float32)
        * slope
    )
    widen_bias_grad = jnp.sum(hidden_grad, axis=(0, 1))
    hidden_rounded = hidden_grad.astype(jnp.bfloat16)
    narrow_grad = jnp.einsum(
        "stf,ste->fe", activated, whole_cot, preferred_element_type=jnp.float32
    ).astype(jnp.bfloat16)
    narrow_share = lax.psum_scatter(narrow_grad, "fsdp", scatter_dimension=1, tiled=True)
    widen_grad = jnp.einsum(
        "std,stf->df", second_rows, hidden_rounded, preferred_element_type=jnp.float32
    ).astype(jnp.bfloat16)
    widen_share = lax.psum_scatter(widen_grad, "fsdp", scatter_dimension=0, tiled=True)
    second_grad = jnp.einsum(
        "stf,df->std", hidden_rounded, weight_widen, preferred_element_type=jnp.float32
    ).astype(jnp.bfloat16)
    attention_part = jnp.einsum(
        "shkt,hke->ste", mixed_tokens, mixer_four, preferred_element_type=jnp.float32
    )
    branches = attention_part + jnp.einsum(
        "stf,fe->ste", activated, weight_narrow, preferred_element_type=jnp.float32
    )
    summed = lax.psum_scatter(
        branches.astype(jnp.bfloat16), "tp", scatter_dimension=2, tiled=True
    ).astype(jnp.float32)
    bias_slice = lax.dynamic_slice_in_dim(bias_output, feature_start, local_width, 0)
    block_output = (block_input.astype(jnp.float32) + summed + bias_slice).astype(jnp.bfloat16)
    mixer_grad = (
        jnp.einsum("shkt,ste->hke", mixed_tokens, whole_cot, preferred_element_type=jnp.float32)
        .reshape(weight_mixer.shape)
        .astype(jnp.bfloat16)
    )
    mixer_share = lax.psum_scatter(mixer_grad, "fsdp", scatter_dimension=1, tiled=True)
    unturned = rotate_back(back_float[:, :, :2], cosine, sine, half)
    projected_grad = jnp.concatenate([unturned, back_float[:, :, 2:]], axis=2)
    triple_bias_grad = jnp.transpose(jnp.sum(projected_grad, axis=(0, 4)), (1, 0, 2))
    projected_rounded = projected_grad.astype(jnp.bfloat16)
    first_grad = jnp.einsum(
        "shckt,dchk->std", projected_rounded, weight_four, preferred_element_type=jnp.float32
    ).astype(jnp.bfloat16)
    first_float = first_grad.astype(jnp.float32)
    second_float = second_grad.astype(jnp.float32)
    scaled = first_float * gain_one + second_float * gain_two
    scattered = lax.psum_scatter(
        scaled.astype(jnp.bfloat16), "tp", scatter_dimension=2, tiled=True
    ).astype(jnp.float32)
    row_sums = lax.psum(
        jnp.stack([jnp.sum(scaled, axis=-1), jnp.sum(scaled * normed, axis=-1)]), "tp"
    ) * (1.0 / width)
    triple_grad = (
        jnp.einsum(
            "std,shckt->dchk", first_rows, projected_rounded, preferred_element_type=jnp.float32
        )
        .reshape(weight_triple.shape)
        .astype(jnp.bfloat16)
    )
    triple_share = lax.psum_scatter(triple_grad, "fsdp", scatter_dimension=0, tiled=True)
    output_bias_grad = jnp.sum(whole_cot.astype(jnp.float32), axis=(0, 1))
    wide_sums = jnp.stack(
        [
            jnp.sum(first_float * normed, axis=(0, 1)),
            jnp.sum(first_float, axis=(0, 1)),
            jnp.sum(second_float * normed, axis=(0, 1)),
            jnp.sum(second_float, axis=(0, 1)),
            jnp.where(lax.axis_index("tp") == 0, output_bias_grad, 0.0),
        ]
    )
    wide_sums = lax.psum(wide_sums, ("fsdp", "ctx", "tp"))
    bias_sums = lax.psum(
        jnp.concatenate([triple_bias_grad.reshape(-1), widen_bias_grad]), ("fsdp", "ctx")
    )
    place = lax.axis_index("fsdp")
    vector_size = first_gain.shape[0]
    wide_sums = lax.dynamic_slice_in_dim(wide_sums, place * vector_size, vector_size, 1)
    triple_bias_out = lax.dynamic_slice_in_dim(
        bias_sums[: triple_bias_grad.size].reshape(triple_bias_grad.shape),
        place * triple_bias.shape[2],
        triple_bias.shape[2],
        2,
    )
    widen_bias_out = lax.dynamic_slice_in_dim(
        bias_sums[triple_bias_grad.size :].reshape(widen_bias.shape[0], -1),
        place * widen_bias.shape[1],
        widen_bias.shape[1],
        1,
    )
    own_normed = lax.dynamic_slice_in_dim(normed, feature_start, local_width, 2)
    input_grad = (
        cotangent.astype(jnp.float32)
        + inverse * (scattered - row_sums[0][..., None] - own_normed * row_sums[1][..., None])
    ).astype(jnp.bfloat16)
    return (
        block_output,
        input_grad,
        wide_sums[0],
        wide_sums[1],
        wide_sums[2],
        wide_sums[3],
        sum_pair(triple_share, "ctx"),
        triple_bias_out,
        sum_pair(mixer_share, "ctx"),
        wide_sums[4],
        sum_pair(widen_share, "ctx"),
        widen_bias_out,
        sum_pair(narrow_share, "ctx"),
    )


class Copies:
    def __init__(self, send, recv, local):
        self.send, self.recv, self.local = send, recv, local
        self.remotes = self.locals = 0

    def remote(self, source, target, device):
        index = self.remotes
        self.remotes += 1
        return pltpu.make_async_remote_copy(
            src_ref=source, dst_ref=target, send_sem=self.send.at[index], recv_sem=self.recv.at[index],
            device_id=device, device_id_type=pl.DeviceIdType.MESH,
        )

    def here(self, source, target):
        index = self.locals
        self.locals += 1
        return pltpu.make_async_copy(source, target, self.local.at[index])


def sem_shapes(remotes, local_copies):
    return [pltpu.SemaphoreType.DMA((remotes,)), pltpu.SemaphoreType.DMA((remotes,)),
            pltpu.SemaphoreType.DMA((local_copies,))]


def places(groups):
    z, c, t = lax.axis_index("fsdp"), lax.axis_index("ctx"), lax.axis_index("tp")
    near = t + 1 - 2 * lax.rem(t, 2)
    far = lax.rem(t + 2, 4)
    return z, c, t, near, far


def greet(devices):
    barrier = pltpu.get_barrier_semaphore()
    for device in devices:
        pl.semaphore_signal(barrier, inc=1, device_id=device, device_id_type=pl.DeviceIdType.MESH)
    pl.semaphore_wait(barrier, len(devices))


def aligned(index, step):
    return pl.ds(pl.multiple_of(index * step, step), step)


class Spread:
    def __init__(self, groups, copies, shards, wholes, by_rows):
        z, c, t, _, _ = places(groups)
        self.groups, self.shards, self.wholes, self.by_rows = groups, shards, wholes, by_rows
        self.keeps, self.shares, self.relays = [], [], []
        for a in range(len(shards)):
            shares, relays = [], []
            for k in range(1, groups):
                origin = lax.rem(z + groups - k, groups)
                shares.append(copies.remote(
                    self.half(a, c), self.part(a, z, c), (lax.rem(z + k, groups), c, t)))
                relays.append(copies.remote(self.part(a, origin, c), self.part(a, origin, c), (z, 1 - c, t)))
            self.shares.append(shares)
            self.relays.append(relays)
            self.keeps.append(copies.here(shards[a], self.whole_of(a, z)))

    def half(self, a, half):
        return self.shards[a].at[aligned(half, self.shards[a].shape[0] // 2)]

    def whole_of(self, a, group):
        if self.by_rows[a]:
            return self.wholes[a].at[aligned(group, self.shards[a].shape[0])]
        return self.wholes[a].at[:, aligned(group, self.shards[a].shape[1])]

    def part(self, a, group, half):
        rows, columns = self.shards[a].shape
        if self.by_rows[a]:
            return self.wholes[a].at[aligned(group * 2 + half, rows // 2)]
        return self.wholes[a].at[aligned(half, rows // 2), aligned(group, columns)]

    def start(self, a):
        for share in self.shares[a]:
            share.start()
        self.keeps[a].start()

    def relay(self, a, k):
        self.shares[a][k].wait_recv()
        self.relays[a][k].start()

    def arrive(self, a):
        self.keeps[a].wait()
        for relay in self.relays[a]:
            relay.wait_recv()

    def finish(self):
        for a in range(len(self.shards)):
            for share, relay in zip(self.shares[a], self.relays[a]):
                share.wait_send()
                relay.wait_send()


def front_kernel(groups, x_in, c_in, pos_in, widen_in, triple_in, mixer_in, vec_in,
                 c_out, pos_out, widen_out, triple_out, mixer_out, vec_out,
                 normed_out, first_out, second_out, active_out, slope_out, narrow_out, stats_out, sums_out,
                 x_all, c_all, widen_all, vec_all, normed, first, second, active, slope, narrow_grad, vec_float,
                 send, recv, local):
    z, c, t, near, far = places(groups)
    copies = Copies(send, recv, local)
    y_peer, near_peer, far_peer = (z, 1 - c, t), (z, c, near), (z, c, far)
    ring = [lax.rem(z + k, groups) for k in range(1, groups)]
    greet([y_peer, near_peer, far_peer] + [(peer, c, t) for peer in ring])
    span, width = x_in.shape[1:]
    length, whole = x_all.shape
    started = []

    def start(copy):
        copy.start()
        started.append(copy)
        return copy

    def block(ref, half, feature):
        return ref.at[aligned(half, span), aligned(feature, width)]

    cross = 3 - t
    tensors = ((x_in, x_all), (c_in, c_all))
    stays = [copies.here(pos_in.at[c], pos_out.at[c]), copies.here(vec_in, vec_all.at[z])]
    for copy in stays:
        copy.start()
    own = [copies.here(source.at[c], block(target, c, t)) for source, target in tensors]
    swaps = [copies.remote(source.at[1 - c], block(target, c, t), y_peer) for source, target in tensors]
    firsts = [
        [copies.remote(source.at[c], block(target, c, t), far_peer),
         copies.remote(source.at[c], block(target, c, t), near_peer)]
        for source, target in tensors
    ]
    weights = Spread(groups, copies, (widen_in, triple_in, mixer_in), (widen_all, triple_out, mixer_out),
                     (True, True, False))
    start(swaps[0])
    start(firsts[0][0])
    start(firsts[0][1])
    small = [start(copies.remote(vec_in, vec_all.at[z], (peer, c, t))) for peer in ring]
    position_swap = start(copies.remote(pos_in.at[1 - c], pos_out.at[c], y_peer))
    weights.start(0)
    for copy in own:
        copy.start()
    start(firsts[1][1])
    weights.start(1)
    weights.start(2)

    def second_half(index):
        swaps[index].wait_recv()
        other = block(tensors[index][1], 1 - c, t)
        return [start(copies.remote(other, other, far_peer)), start(copies.remote(other, other, near_peer))]

    def pass_on(index, pair, half):
        pair[0].wait_recv()
        there = block(tensors[index][1], half, far)
        return start(copies.remote(there, there, near_peer))

    step_rows = min(256, span)
    saves = []

    def save(source, target):
        copy = copies.here(source, target)
        copy.start()
        saves.append(copy)

    def row_vector(index):
        pieces = []
        for group in range(groups):
            for k in range(width_rows):
                at = index * width_rows + k
                pieces.append(vec_float[group, at : at + 1])
        return jnp.concatenate(pieces, axis=1)

    width_rows = whole // groups // 128

    def normalise(half):
        gain_one, shift_one, gain_two, shift_two = [row_vector(index) for index in range(4)]

        @pl.loop(0, span // step_rows)
        def _(step):
            at = pl.ds(pl.multiple_of(half * span + step * step_rows, step_rows), step_rows)
            rows = x_all[at].astype(jnp.float32)
            mean = jnp.mean(rows, axis=-1, keepdims=True)
            centred = rows - mean
            inverse = lax.rsqrt(jnp.mean(centred * centred, axis=-1, keepdims=True) + norm_eps)
            unit = centred * inverse
            normed[at] = unit.astype(jnp.bfloat16)
            first[at] = (unit * gain_one + shift_one).astype(jnp.bfloat16)
            second[at] = (unit * gain_two + shift_two).astype(jnp.bfloat16)
            stats_out[0:1, at] = jnp.broadcast_to(mean, (step_rows, 128)).T[0:1]
            stats_out[1:2, at] = jnp.broadcast_to(inverse, (step_rows, 128)).T[0:1]

        for source, target in ((normed, normed_out), (first, first_out), (second, second_out)):
            save(source.at[aligned(half, span)], target.at[aligned(half, span)])

    seconds_x = second_half(0)
    relayed = [pass_on(0, firsts[0], c)]
    start(firsts[1][0])
    for copy in small:
        copy.wait_recv()
    for copy in stays:
        copy.wait()
    vec_float[...] = vec_all[...].astype(jnp.float32)
    save(vec_all, vec_out)
    firsts[0][1].wait_recv()
    own[0].wait()
    relayed[0].wait_recv()
    normalise(c)
    weights.relay(0, 0)
    for k in range(1, groups - 1):
        weights.relay(0, k)
    start(swaps[1])
    relayed.append(pass_on(0, seconds_x, 1 - c))
    seconds_x[1].wait_recv()
    relayed[1].wait_recv()
    normalise(1 - c)
    for k in range(groups - 1):
        weights.relay(1, k)
    weights.arrive(0)
    save(widen_all, widen_out)
    relayed.append(pass_on(1, firsts[1], c))
    bias_at = 5 * width_rows
    bias_pieces = []
    hidden = widen_all.shape[1]
    for row in range(hidden // 128):
        piece = vec_float[0, bias_at + row : bias_at + row + 1]
        for group in range(1, groups):
            piece = piece + vec_float[group, bias_at + row : bias_at + row + 1]
        bias_pieces.append(piece)
    bias = jnp.concatenate(bias_pieces, axis=1)

    def widen(half):
        @pl.loop(0, span // step_rows)
        def _(step):
            at = pl.ds(pl.multiple_of(half * span + step * step_rows, step_rows), step_rows)
            widened = jnp.dot(second[at], widen_all[...], preferred_element_type=jnp.float32) + bias
            value, gradient = gelu_parts(widened)
            active[at] = value.astype(jnp.bfloat16)
            slope[at] = gradient.astype(jnp.bfloat16)

        save(active.at[aligned(half, span)], active_out.at[aligned(half, span)])
        save(slope.at[aligned(half, span)], slope_out.at[aligned(half, span)])

    widen(c)
    seconds_c = second_half(1)
    widen(1 - c)
    for k in range(groups - 1):
        weights.relay(2, k)
    relayed.append(pass_on(1, seconds_c, 1 - c))
    own[1].wait()
    firsts[1][1].wait_recv()
    seconds_c[1].wait_recv()
    for copy in relayed[2:]:
        copy.wait_recv()
    save(c_all, c_out)
    tile = min(256, hidden)
    for at in range(0, hidden, tile):
        narrow_grad[at : at + tile] = lax.dot_general(
            active[:, at : at + tile], c_all[...], (((0,), (0,)), ((), ())), preferred_element_type=jnp.float32
        ).astype(jnp.bfloat16)
    save(narrow_grad, narrow_out)

    sums_out[...] = jnp.zeros_like(sums_out)

    @pl.loop(0, length // step_rows)
    def _(step):
        at = pl.ds(pl.multiple_of(step * step_rows, step_rows), step_rows)
        sums_out[0:1] += jnp.sum(c_all[at].astype(jnp.float32), axis=0, keepdims=True)

    weights.arrive(1)
    weights.arrive(2)
    position_swap.wait_recv()
    for copy in started:
        copy.wait_send()
    weights.finish()
    for copy in saves:
        copy.wait()


def front(groups, block_input, cotangent, positions, widen_weight, triple_weight, mixer_weight, vectors):
    seqs, span, width = block_input.shape
    length, whole = seqs * span, width * 4
    hidden = widen_weight.shape[1]
    any_space = pl.BlockSpec(memory_space=pl.ANY)
    in_vmem = pl.BlockSpec(memory_space=pltpu.VMEM)
    bf16, f32 = jnp.bfloat16, jnp.float32
    tokens = jax.ShapeDtypeStruct((length, whole), bf16)
    units = jax.ShapeDtypeStruct((length, hidden), bf16)
    vec_shape = (groups,) + vectors.shape
    return pl.pallas_call(
        functools.partial(front_kernel, groups),
        in_specs=[any_space] * 7,
        out_specs=[any_space] * 12 + [in_vmem] * 2,
        out_shape=[
            tokens,
            jax.ShapeDtypeStruct(positions.shape, positions.dtype),
            jax.ShapeDtypeStruct((whole, hidden), bf16),
            jax.ShapeDtypeStruct((whole, triple_weight.shape[1]), bf16),
            jax.ShapeDtypeStruct((mixer_weight.shape[0], whole), bf16),
            jax.ShapeDtypeStruct(vec_shape, bf16),
            tokens, tokens, tokens, units, units,
            jax.ShapeDtypeStruct((hidden, whole), bf16),
            jax.ShapeDtypeStruct((8, length), f32),
            jax.ShapeDtypeStruct((8, whole), f32),
        ],
        scratch_shapes=[
            pltpu.VMEM((length, whole), bf16),
            pltpu.VMEM((length, whole), bf16),
            pltpu.VMEM((whole, hidden), bf16),
            pltpu.VMEM(vec_shape, bf16),
            pltpu.VMEM((length, whole), bf16),
            pltpu.VMEM((length, whole), bf16),
            pltpu.VMEM((length, whole), bf16),
            pltpu.VMEM((length, hidden), bf16),
            pltpu.VMEM((length, hidden), bf16),
            pltpu.VMEM((hidden, whole), bf16),
            pltpu.VMEM(vec_shape, f32),
        ] + sem_shapes(15 + 7 * (groups - 1), 24),
        compiler_params=pltpu.CompilerParams(
            collective_id=0, has_side_effects=True, vmem_limit_bytes=52 * 1024 * 1024
        ),
        name="front",
    )(block_input, cotangent, positions, widen_weight, triple_weight, mixer_weight, vectors)


class Reduce:
    def __init__(self, groups, copies, arrays, outs, by_rows, owns, others, sums, inbox, done):
        self.groups, self.copies, self.arrays, self.outs, self.by_rows = groups, copies, arrays, outs, by_rows
        self.owns, self.others, self.sums, self.inbox, self.done = owns, others, sums, inbox, done
        self.z, self.c, self.t, _, _ = places(groups)
        self.y_peer = (self.z, 1 - self.c, self.t)
        self.order = list(range(1, groups)) + [0]
        self.loads, self.swaps, self.sends, self.backs, self.keeps = [], [], [], [], []

    def piece(self, a, group, half):
        array = self.arrays[a]
        if self.by_rows[a]:
            return array.at[aligned(group * 2 + half, array.shape[0] // (2 * self.groups))]
        return array.at[aligned(half, array.shape[0] // 2), aligned(group, array.shape[1] // self.groups)]

    def out_half(self, a, half):
        return self.outs[a].at[aligned(half, self.outs[a].shape[0] // 2)]

    def make(self):
        for a in range(len(self.arrays)):
            loads, swaps, sends = [], [], []
            for slot, k in enumerate(self.order):
                group = lax.rem(self.z + k, self.groups)
                loads.append(self.copies.here(self.piece(a, group, self.c), self.owns[a].at[slot]))
                swaps.append(self.copies.remote(self.piece(a, group, 1 - self.c), self.others[a].at[slot], self.y_peer))
                if k:
                    sends.append(self.copies.remote(
                        self.sums[a].at[slot], self.inbox[a].at[slot], (group, self.c, self.t)))
            self.loads.append(loads)
            self.swaps.append(swaps)
            self.sends.append(sends)
            self.backs.append(self.copies.remote(self.done[a], self.out_half(a, self.c), self.y_peer))
            self.keeps.append(self.copies.here(self.done[a], self.out_half(a, self.c)))

    def start(self, a):
        for swap, load in zip(self.swaps[a], self.loads[a]):
            swap.start()
            load.start()

    def add(self, a, slot):
        self.loads[a][slot].wait()
        self.swaps[a][slot].wait_recv()
        total = self.owns[a][slot].astype(jnp.float32) + self.others[a][slot].astype(jnp.float32)
        self.sums[a][slot] = total.astype(jnp.bfloat16)
        if slot < self.groups - 1:
            self.sends[a][slot].start()

    def total(self, a):
        total = self.sums[a][self.groups - 1].astype(jnp.float32)
        for slot in range(self.groups - 1):
            self.sends[a][slot].wait_recv()
            total = total + self.inbox[a][slot].astype(jnp.float32)
        self.done[a][...] = total.astype(jnp.bfloat16)
        self.backs[a].start()
        self.keeps[a].start()

    def finish(self):
        for a in range(len(self.arrays)):
            for swap in self.swaps[a]:
                swap.wait_send()
            for send in self.sends[a]:
                send.wait_send()
            self.backs[a].wait()
            self.keeps[a].wait()


def reduce_shapes(groups, shapes, by_rows):
    owns, others, sums, inbox, done, outs = [], [], [], [], [], []
    for (rows, columns), along in zip(shapes, by_rows):
        part = (rows // (2 * groups), columns) if along else (rows // 2, columns // groups)
        owns.append(pltpu.VMEM((groups,) + part, jnp.bfloat16))
        others.append(pltpu.VMEM((groups,) + part, jnp.bfloat16))
        sums.append(pltpu.VMEM((groups,) + part, jnp.bfloat16))
        inbox.append(pltpu.VMEM((groups - 1,) + part, jnp.bfloat16))
        done.append(pltpu.VMEM(part, jnp.bfloat16))
        outs.append(jax.ShapeDtypeStruct((2 * part[0], part[1]), jnp.bfloat16))
    return owns + others + sums + inbox + done, outs


def reduce_from(groups, copies, arrays, outs, by_rows, scratch):
    n = len(arrays)
    cut = [scratch[n * i : n * (i + 1)] for i in range(5)]
    made = Reduce(groups, copies, arrays, outs, by_rows, *cut)
    made.make()
    return made


def attend_reduce_kernel(block, scale, groups, items, qkv_ref, grad_ref, base_ref, grads_in, shard_in,
                         back_ref, mixed_ref, grads_out, whole_out, *refs):
    attention, refs = refs[:11], refs[11:]
    scratch, (send, recv, local) = refs[:-3], refs[-3:]
    item = pl.program_id(0)
    copies = Copies(send, recv, local)
    reduce = reduce_from(groups, copies, (grads_in,), (grads_out,), (False,), scratch)
    weights = Spread(groups, copies, (shard_in,), (whole_out,), (False,))
    blocks = grad_ref.shape[0] * grad_ref.shape[3] // block
    steps = [(i, b) for i in range(items) for b in range(blocks)]
    costs = [i * blocks * (blocks + 1) // 2 + b * (b + 1) // 2 for i, b in steps]
    total = items * blocks * (blocks + 1) // 2
    plan = {}

    def at_time(fraction, action, *args):
        at = max(k for k in range(len(steps)) if costs[k] <= total * fraction)
        plan.setdefault(steps[at], []).append(functools.partial(action, *args))

    for slot in range(groups):
        at_time(0.15 + 0.4 * slot / groups, reduce.add, 0, slot)
    for k in range(groups - 1):
        at_time(0.2 + 0.4 * k / groups, weights.relay, 0, k)
    at_time(0.85, reduce.total, 0)

    def begin():
        z, c, t, _, _ = places(groups)
        greet([(z, 1 - c, t)] + [(lax.rem(z + k, groups), c, t) for k in range(1, groups)])
        reduce.start(0)
        weights.start(0)

    pl.when(item == 0)(begin)

    def between(b):
        for i in range(items):
            for action in plan.get((i, b), ()):
                pl.when(item == i)(action)

    attend_kernel(block, scale, between, qkv_ref, grad_ref, base_ref, back_ref, mixed_ref, *attention)

    def end():
        reduce.finish()
        weights.arrive(0)
        weights.finish()

    pl.when(item == items - 1)(end)


def attend_reduce(by_heads, grad_heads, item_base, scale, groups, narrow_grad, narrow_weight):
    parts, items, unused, head_size, span = by_heads.shape
    length = parts * span
    block = min(256, span)
    wide = pltpu.VMEM((head_size, length), jnp.bfloat16)
    tall = pltpu.VMEM((length, head_size), jnp.bfloat16)
    total = pltpu.VMEM((length, head_size), jnp.float32)
    shapes, outs = reduce_shapes(groups, [narrow_grad.shape], (False,))
    any_space = pl.BlockSpec(memory_space=pl.ANY)
    return pl.pallas_call(
        functools.partial(attend_reduce_kernel, block, scale, groups, items),
        grid=(items,),
        in_specs=[
            pl.BlockSpec((parts, 1, 3, head_size, span), lambda i: (0, i, 0, 0, 0)),
            pl.BlockSpec((parts, 1, head_size, span), lambda i: (0, i, 0, 0)),
            pl.BlockSpec((1, 1, length), lambda i: (i, 0, 0)),
            any_space,
            any_space,
        ],
        out_specs=[
            pl.BlockSpec((parts, 1, 3, head_size, span), lambda i: (0, i, 0, 0, 0)),
            pl.BlockSpec((parts, 1, head_size, span), lambda i: (0, i, 0, 0)),
            any_space,
            any_space,
        ],
        out_shape=[
            jax.ShapeDtypeStruct(by_heads.shape, jnp.bfloat16),
            jax.ShapeDtypeStruct(grad_heads.shape, jnp.bfloat16),
        ] + outs + [
            jax.ShapeDtypeStruct((narrow_weight.shape[0], narrow_weight.shape[1] * groups), jnp.bfloat16)
        ],
        scratch_shapes=[wide, tall, wide, tall, wide, tall, wide, tall,
                        pltpu.VMEM((length, 128), jnp.float32), total, total]
        + shapes + sem_shapes(2 * groups + 2 * (groups - 1), groups + 2),
        compiler_params=pltpu.CompilerParams(
            collective_id=1, has_side_effects=True, vmem_limit_bytes=48 * 1024 * 1024
        ),
        cost_estimate=pl.CostEstimate(
            flops=7 * items * length * length * 256,
            bytes_accessed=4 * by_heads.size,
            transcendentals=items * length * length // 2,
        ),
        name="attend_reduce",
    )(by_heads, grad_heads, item_base, narrow_grad, narrow_weight)


class ReduceWhole:
    def __init__(self, groups, copies, arrays, outs, by_rows, scratch):
        z, c, t, _, _ = places(groups)
        n = len(arrays)
        self.groups, self.outs = groups, outs
        self.owns, self.inbox, self.mine, self.theirs = [scratch[n * i : n * (i + 1)] for i in range(4)]
        self.loads, self.sends, self.swaps = [], [], []

        def piece(a, group):
            array = arrays[a]
            if by_rows[a]:
                return array.at[aligned(group, array.shape[0] // groups)]
            return array.at[:, aligned(group, array.shape[1] // groups)]

        for a in range(n):
            self.loads.append(copies.here(piece(a, z), self.owns[a]))
            sends = []
            for k in range(1, groups):
                group = lax.rem(z + k, groups)
                sends.append(copies.remote(piece(a, group), self.inbox[a].at[k - 1], (group, c, t)))
            self.sends.append(sends)
            self.swaps.append(copies.remote(self.mine[a], self.theirs[a], (z, 1 - c, t)))

    def start(self):
        for load, sends in zip(self.loads, self.sends):
            for send in sends:
                send.start()
            load.start()

    def total(self):
        for a, sends in enumerate(self.sends):
            self.loads[a].wait()
            total = self.owns[a][...].astype(jnp.float32)
            for k, send in enumerate(sends):
                send.wait_recv()
                total = total + self.inbox[a][k].astype(jnp.float32)
            self.mine[a][...] = total.astype(jnp.bfloat16)
            self.swaps[a].start()

    def finish(self):
        for a, swap in enumerate(self.swaps):
            swap.wait()
            self.outs[a][...] = self.mine[a][...].astype(jnp.float32) + self.theirs[a][...].astype(jnp.float32)
            for send in self.sends[a]:
                send.wait_send()


def reduce_whole_shapes(groups, shapes, by_rows):
    parts = [(rows // groups, columns) if along else (rows, columns // groups)
             for (rows, columns), along in zip(shapes, by_rows)]
    scratch = [pltpu.VMEM(part, jnp.bfloat16) for part in parts]
    scratch += [pltpu.VMEM((groups - 1,) + part, jnp.bfloat16) for part in parts]
    scratch += [pltpu.VMEM(part, jnp.bfloat16) for part in parts] * 2
    return scratch, [jax.ShapeDtypeStruct(part, jnp.float32) for part in parts]


def back_kernel(groups, mixed_in, mixer_in, active_in, narrow_in, c_in, slope_in, second_in, turned_in, triple_in,
                widen_in, normed_in, gains, norm_stats, front_sums, triple_bias_in, triple_grad_in, mixer_grad_in,
                out_ref, grad_ref, stats_out, widen_share, wide_out, bias_out, triple_share, mixer_share,
                mixed, mixer, active, narrow, c_all, hidden, second, turned, triple, widen, normed,
                out_part, grad_part, near_box, far_box, widen_grad, wide_sum, bias_sum,
                row_box, row_sum, wide_box, wide_two, wide_three, bias_two, bias_three, *refs):
    scratch, (send, recv, local) = refs[:-3], refs[-3:]
    z, c, t, near, far = places(groups)
    copies = Copies(send, recv, local)
    y_peer = (z, 1 - c, t)
    near_peer, far_peer, cross_peer = (z, c, near), (z, c, far), (z, c, 3 - t)
    ring = [lax.rem(z + k, groups) for k in range(1, groups)]
    span, width = out_ref.shape[1:]
    length, whole = c_all.shape
    quarter = span // 2
    step_rows = min(256, quarter)
    f32, bf16 = jnp.float32, jnp.bfloat16
    loads = []
    for source, target in (
        (mixed_in, mixed), (mixer_in, mixer), (active_in, active), (narrow_in, narrow), (c_in, c_all),
        (slope_in, hidden), (second_in, second), (turned_in, turned), (triple_in, triple), (widen_in, widen),
        (normed_in, normed),
    ):
        load = copies.here(source, target)
        load.start()
        loads.append(load)
    greet([y_peer, near_peer, far_peer, cross_peer] + [(peer, c, t) for peer in ring])
    started, finals, keeps = [], [], []

    def start(copy):
        copy.start()
        started.append(copy)
        return copy

    whole_scratch, half_scratch = scratch[:8], scratch[8:]
    attention_sums = ReduceWhole(
        groups, copies, (triple_grad_in, mixer_grad_in), (triple_share, mixer_share), (True, False), whole_scratch
    )
    attention_sums.start()
    widen_sums = reduce_from(groups, copies, (widen_grad,), (widen_share,), (True,), half_scratch)
    parts = (out_part, grad_part)
    halves = (1 - c, c)
    nears = [[], []]
    fars = [[], []]

    def send_near(index, turn):
        rows = aligned(halves[turn], span)
        part = parts[index]
        nears[index].append([
            start(copies.remote(
                part.at[rows, aligned(3 - t, width)], near_box.at[index, 0, rows], near_peer)),
            start(copies.remote(
                part.at[rows, aligned(near, width)], near_box.at[index, 1, rows], near_peer)),
        ])

    def rows_of(turn, step):
        return pl.ds(pl.multiple_of(halves[turn] * span + step * quarter, quarter), quarter)

    def send_far(index, turn):
        nears[index][turn][0].wait_recv()
        part = parts[index]
        for step in range(2):
            rows = rows_of(turn, step)
            total = part[rows, aligned(far, width)].astype(f32) + near_box[index, 0, rows].astype(f32)
            part[rows, aligned(far, width)] = total.astype(bf16)
            fars[index].append(start(copies.remote(
                part.at[rows, aligned(far, width)], far_box.at[index, rows], far_peer)))

    def close(index, turn, target):
        nears[index][turn][1].wait_recv()
        part = parts[index]
        for step in range(2):
            rows = rows_of(turn, step)
            fars[index][2 * turn + step].wait_recv()
            done = part.at[rows, aligned(t, width)]
            total = (
                part[rows, aligned(t, width)].astype(f32)
                + near_box[index, 1, rows].astype(f32)
                + far_box[index, rows].astype(f32)
            )
            part[rows, aligned(t, width)] = total.astype(bf16)
            place = target.at[c, pl.ds(step * quarter, quarter)]
            if turn == 0:
                finals.append(start(copies.remote(done, place, y_peer)))
            else:
                keep = copies.here(done, place)
                keep.start()
                keeps.append(keep)

    def loop(turn, body):
        @pl.loop(0, span // step_rows)
        def _(step):
            body(pl.ds(pl.multiple_of(halves[turn] * span + step * step_rows, step_rows), step_rows))

    for load in loads[:4]:
        load.wait()

    def branches(at):
        total = lax.dot_general(mixed[:, at], mixer[...], (((0,), (0,)), ((), ())), preferred_element_type=f32)
        total = total + jnp.dot(active[at], narrow[...], preferred_element_type=f32)
        out_part[at] = total.astype(bf16)

    for turn in range(2):
        loop(turn, branches)
        send_near(0, turn)
    for load in loads[4:6]:
        load.wait()
    bias_sum[...] = jnp.zeros_like(bias_sum)
    bias_sum[1:2] = triple_bias_in[...]

    def hidden_grads(at):
        grads = lax.dot_general(c_all[at], narrow[...], (((1,), (1,)), ((), ())), preferred_element_type=f32)
        grads = grads * hidden[at].astype(f32)
        bias_sum[0:1] += jnp.sum(grads, axis=0, keepdims=True)
        hidden[at] = grads.astype(bf16)

    loop(0, hidden_grads)
    send_far(0, 0)
    loop(1, hidden_grads)
    send_far(0, 1)
    loads[6].wait()
    depth = widen_grad.shape[0]
    tile = min(256, depth)
    for at in range(0, depth, tile):
        widen_grad[at : at + tile] = lax.dot_general(
            second[:, at : at + tile], hidden[...], (((0,), (0,)), ((), ())), preferred_element_type=f32
        ).astype(bf16)
    widen_sums.start(0)
    bias_two[c] = bias_sum[...]
    bias_swap = start(copies.remote(bias_two.at[c], bias_two.at[c], y_peer))
    for load in loads[7:]:
        load.wait()
    wide_sum[...] = front_sums[...]
    gain_one, gain_two = gains[0:1], gains[1:2]

    def norm_grads(at):
        unit = normed[at].astype(f32)
        one = lax.dot_general(turned[:, at], triple[...], (((0,), (1,)), ((), ())), preferred_element_type=f32)
        wide_sum[0:1] += jnp.sum(one * unit, axis=0, keepdims=True)
        wide_sum[1:2] += jnp.sum(one, axis=0, keepdims=True)
        two = lax.dot_general(hidden[at], widen[...], (((1,), (1,)), ((), ())), preferred_element_type=f32)
        wide_sum[2:3] += jnp.sum(two * unit, axis=0, keepdims=True)
        wide_sum[3:4] += jnp.sum(two, axis=0, keepdims=True)
        scaled = one * gain_one + two * gain_two
        grad_part[at] = scaled.astype(bf16)
        rows = scaled.shape[0]
        total = jnp.sum(scaled, axis=-1, keepdims=True) * (1.0 / whole)
        along = jnp.sum(scaled * unit, axis=-1, keepdims=True) * (1.0 / whole)
        row_box[t, 0:1, at] = jnp.broadcast_to(total, (rows, 128)).T[0:1]
        row_box[t, 1:2, at] = jnp.broadcast_to(along, (rows, 128)).T[0:1]

    loop(0, norm_grads)
    send_near(1, 0)
    loop(1, norm_grads)
    send_near(1, 1)
    wide_box[t] = wide_sum[...]
    tp_peers = [(t + k) - 4 * ((t + k) // 4) for k in range(1, 4)]
    tp_sent = [start(copies.remote(row_box.at[t], row_box.at[t], (z, c, peer))) for peer in tp_peers]
    tp_sent += [start(copies.remote(wide_box.at[t], wide_box.at[t], (z, c, peer))) for peer in tp_peers]
    send_far(1, 0)
    close(0, 0, out_ref)
    send_far(1, 1)
    for slot in range(groups):
        widen_sums.add(0, slot)
    close(0, 1, out_ref)
    for copy in tp_sent:
        copy.wait_recv()
    row_sum[0:2] = row_box[0] + row_box[1] + row_box[2] + row_box[3]
    row_sum[2:4] = norm_stats[0:2]
    finals.append(start(copies.remote(row_sum.at[:, aligned(1 - c, span)], stats_out.at[c], y_peer)))
    keeps.append(copies.here(row_sum.at[:, aligned(c, span)], stats_out.at[c]))
    keeps[-1].start()
    wide_two[c] = wide_box[0] + wide_box[1] + wide_box[2] + wide_box[3]
    wide_swap = start(copies.remote(wide_two.at[c], wide_two.at[c], y_peer))
    bias_swap.wait_recv()
    bias_three[z] = bias_two[0] + bias_two[1]
    sums_sent = [start(copies.remote(bias_three.at[z], bias_three.at[z], (peer, c, t))) for peer in ring]
    attention_sums.total()
    wide_swap.wait_recv()
    wide_three[z] = wide_two[0] + wide_two[1]
    sums_sent += [start(copies.remote(wide_three.at[z], wide_three.at[z], (peer, c, t))) for peer in ring]
    close(1, 0, grad_ref)
    for copy in sums_sent:
        copy.wait_recv()
    bias_total, wide_total = bias_three[0], wide_three[0]
    for group in range(1, groups):
        bias_total = bias_total + bias_three[group]
        wide_total = wide_total + wide_three[group]
    bias_out[...] = bias_total
    wide_out[...] = wide_total
    widen_sums.total(0)
    close(1, 1, grad_ref)
    attention_sums.finish()
    for copy in finals:
        copy.wait_recv()
    for copy in started:
        copy.wait_send()
    for copy in keeps:
        copy.wait()
    widen_sums.finish()


def back(groups, mixed, mixer_weight, active, narrow_weight, c_rows, slope, second, turned, triple_weight, widen_weight,
         normed, gains, norm_stats, front_sums, triple_bias_row, triple_grad, mixer_grad):
    length, whole = c_rows.shape
    hidden = active.shape[1]
    width, span = whole // 4, length // 2
    any_space = pl.BlockSpec(memory_space=pl.ANY)
    in_vmem = pl.BlockSpec(memory_space=pltpu.VMEM)
    bf16, f32 = jnp.bfloat16, jnp.float32
    whole_scratch, whole_outs = reduce_whole_shapes(groups, [triple_grad.shape, mixer_grad.shape], (True, False))
    half_scratch, half_outs = reduce_shapes(groups, [(whole, hidden)], (True,))
    residents = (mixed, mixer_weight, active, narrow_weight, c_rows, slope, second, turned, triple_weight, widen_weight,
                 normed)
    wide, bias = (8, whole), (8, max(hidden, triple_bias_row.shape[1]))
    return pl.pallas_call(
        functools.partial(back_kernel, groups),
        in_specs=[any_space] * 11 + [in_vmem] * 4 + [any_space] * 2,
        out_specs=[any_space] * 4 + [in_vmem] * 4,
        out_shape=[
            jax.ShapeDtypeStruct((2, span, width), bf16),
            jax.ShapeDtypeStruct((2, span, width), bf16),
            jax.ShapeDtypeStruct((2, 4, span), f32),
        ] + half_outs + [
            jax.ShapeDtypeStruct(wide, f32),
            jax.ShapeDtypeStruct(bias, f32),
        ] + whole_outs,
        scratch_shapes=[pltpu.VMEM(array.shape, bf16) for array in residents] + [
            pltpu.VMEM((length, whole), bf16),
            pltpu.VMEM((length, whole), bf16),
            pltpu.VMEM((2, 2, length, width), bf16),
            pltpu.VMEM((2, length, width), bf16),
            pltpu.VMEM((whole, hidden), bf16),
            pltpu.VMEM(wide, f32),
            pltpu.VMEM(bias, f32),
            pltpu.VMEM((4, 2, length), f32),
            pltpu.VMEM((4, length), f32),
            pltpu.VMEM((4,) + wide, f32),
            pltpu.VMEM((2,) + wide, f32),
            pltpu.VMEM((groups,) + wide, f32),
            pltpu.VMEM((2,) + bias, f32),
            pltpu.VMEM((groups,) + bias, f32),
        ] + whole_scratch + half_scratch + sem_shapes(
            32 + 2 * (groups - 1) + 2 * groups + 2 * groups, 20 + groups + 3),
        compiler_params=pltpu.CompilerParams(
            collective_id=2, has_side_effects=True, vmem_limit_bytes=60 * 1024 * 1024
        ),
        name="back",
    )(*residents, gains, norm_stats, front_sums, triple_bias_row, triple_grad, mixer_grad)


def shards_sequence(
    block_input,
    positions,
    first_gain,
    first_shift,
    second_gain,
    second_shift,
    triple_weight,
    triple_bias,
    mixer_weight,
    output_bias,
    widen_weight,
    widen_bias,
    narrow_weight,
    cotangent,
):
    seqs, span, local_width = block_input.shape
    length = seqs * span
    groups = lax.axis_size("fsdp")
    hidden_rows, hidden_part = widen_bias.shape
    vectors = (first_gain, first_shift, second_gain, second_shift, output_bias)
    placed = lax.dynamic_update_slice_in_dim(
        jnp.zeros((hidden_rows, hidden_part * groups), jnp.bfloat16), widen_bias,
        lax.axis_index("fsdp") * hidden_part, 1,
    )
    flat = jnp.concatenate([vector for vector in vectors] + [placed.reshape(-1), triple_bias.reshape(-1)])
    padded = -(-flat.size // 4096) * 4096
    packed = jnp.pad(flat, (0, padded - flat.size)).reshape(-1, 128)
    (cot_rows, places_out, weight_widen, weight_triple, weight_mixer, small, normed_rows, first_rows, second_rows,
     activated, slope, narrow_grad, norm_stats, front_sums) = front(
        groups, block_input, cotangent, positions.reshape(seqs, span // 128, 128), widen_weight,
        triple_weight.reshape(triple_weight.shape[0], -1), mixer_weight, packed,
    )
    small = small.reshape(groups, -1)
    pieces = []
    offset = 0
    for vector in vectors + (placed, triple_bias):
        pieces.append(small[:, offset : offset + vector.size].astype(jnp.float32))
        offset += vector.size
    gain_one, shift_one, gain_two, shift_two, bias_output = [piece.reshape(-1) for piece in pieces[:5]]
    bias_triple = jnp.transpose(
        pieces[6].reshape((groups,) + triple_bias.shape), (1, 2, 0, 3)
    ).reshape(triple_bias.shape[0], triple_bias.shape[1], -1)
    width = weight_triple.shape[0]
    heads_local, head_size = bias_triple.shape[1:]
    scale = head_size ** (-0.5)
    half = ROT // 2
    all_positions = places_out.reshape(1, length)
    cosine, sine = rotary_tables(all_positions, ROT)
    weight_four = weight_triple.reshape(width, 3, heads_local, head_size)
    projected = jnp.einsum(
        "std,dchk->shckt", first_rows[None], weight_four, preferred_element_type=jnp.float32
    )
    projected = projected + jnp.transpose(bias_triple, (1, 0, 2))[None, :, :, :, None]
    turned = rotate_forward(projected[:, :, :2], cosine, sine, half)
    triple = jnp.concatenate([turned, projected[:, :, 2:]], axis=2).astype(jnp.bfloat16)
    mixer_four = weight_mixer.reshape(heads_local, head_size, width)
    mixed_grad = jnp.einsum(
        "ste,hke->shkt", cot_rows[None], mixer_four, preferred_element_type=jnp.float32
    ).astype(jnp.bfloat16)
    base = (jnp.arange(length, dtype=jnp.int32)[None, :] - all_positions).astype(jnp.float32)
    item_base = jnp.broadcast_to(base[:, None, :], (heads_local, 1, length))
    back_heads, mixed, narrow_share, weight_narrow = attend_reduce(
        triple, mixed_grad, item_base, scale, groups, narrow_grad, narrow_weight
    )
    mixer_rows = mixed.reshape(heads_local * head_size, length)
    back_float = back_heads[0].astype(jnp.float32)
    unturned = rotate_back(back_float[:, :2], cosine[0], sine[0], half)
    projected_grad = jnp.concatenate([unturned, back_float[:, 2:]], axis=1)
    triple_bias_grad = jnp.transpose(jnp.sum(projected_grad, axis=3), (1, 0, 2))
    turned_back = jnp.transpose(projected_grad, (1, 0, 2, 3)).reshape(-1, length).astype(jnp.bfloat16)
    triple_grad = jnp.einsum(
        "td,ct->dc", first_rows, turned_back, preferred_element_type=jnp.float32
    ).astype(jnp.bfloat16)
    mixer_grad = jnp.dot(mixer_rows, cot_rows, preferred_element_type=jnp.float32).astype(jnp.bfloat16)
    row = triple_bias_grad.reshape(1, -1)
    bias_width = max(activated.shape[1], row.shape[1])
    row = jnp.pad(row, ((0, 0), (0, bias_width - row.shape[1])))
    zero = jnp.zeros((width,), jnp.float32)
    first_sums = jnp.stack(
        [zero] * 4 + [jnp.where(lax.axis_index("tp") == 0, front_sums[0], 0.0)] + [zero] * 3
    )
    summed, scattered, row_stats, widen_share, wide_sums, bias_sums, triple_share, mixer_share = back(
        groups, mixer_rows, weight_mixer, activated, weight_narrow, cot_rows, slope, second_rows, turned_back,
        weight_triple, weight_widen, normed_rows, jnp.stack([gain_one, gain_two]), norm_stats, first_sums, row,
        triple_grad, mixer_grad,
    )
    feature_start = lax.axis_index("tp") * local_width
    bias_slice = lax.dynamic_slice_in_dim(bias_output, feature_start, local_width, 0)
    own_rows = block_input.astype(jnp.float32)
    block_output = (own_rows + summed.astype(jnp.float32) + bias_slice).astype(jnp.bfloat16)
    own_normed = (own_rows - row_stats[:, 2, :, None]) * row_stats[:, 3, :, None]
    input_grad = (
        cotangent.astype(jnp.float32)
        + row_stats[:, 3, :, None]
        * (scattered.astype(jnp.float32) - row_stats[:, 0, :, None] - own_normed * row_stats[:, 1, :, None])
    ).astype(jnp.bfloat16)
    place = lax.axis_index("fsdp")
    vector_size = first_gain.shape[0]
    wide_sums = lax.dynamic_slice_in_dim(wide_sums, place * vector_size, vector_size, 1)
    triple_bias_out = lax.dynamic_slice_in_dim(
        bias_sums[1, : triple_bias_grad.size].reshape(triple_bias_grad.shape),
        place * triple_bias.shape[2],
        triple_bias.shape[2],
        2,
    )
    widen_bias_out = lax.dynamic_slice_in_dim(
        bias_sums[0, : activated.shape[1]].reshape(hidden_rows, -1), place * hidden_part, hidden_part, 1
    )
    return (
        block_output,
        input_grad,
        wide_sums[0],
        wide_sums[1],
        wide_sums[2],
        wide_sums[3],
        triple_share.reshape(triple_weight.shape),
        triple_bias_out,
        mixer_share,
        wide_sums[4],
        widen_share.astype(jnp.float32),
        widen_bias_out,
        narrow_share.astype(jnp.float32),
    )


def shards(block_input, *others):
    seqs = block_input.shape[0]
    if seqs == 2 and lax.axis_size("ctx") == 2 and lax.axis_size("tp") == 4 and lax.axis_size("fsdp") > 1:
        return shards_sequence(block_input, *others)
    return shards_general(block_input, *others)


def solution(mesh):
    in_specs = (
        P("fsdp", "ctx", "tp"),
        P("fsdp", "ctx"),
        P("fsdp"),
        P("fsdp"),
        P("fsdp"),
        P("fsdp"),
        P("fsdp", None, "tp"),
        P(None, "tp", "fsdp"),
        P("tp", "fsdp"),
        P("fsdp"),
        P("fsdp", "tp"),
        P("tp", "fsdp"),
        P("tp", "fsdp"),
        P("fsdp", "ctx", "tp"),
    )
    out_specs = (
        P("fsdp", "ctx", "tp"),
        P("fsdp", "ctx", "tp"),
        P("fsdp"),
        P("fsdp"),
        P("fsdp"),
        P("fsdp"),
        P("fsdp", None, "tp"),
        P(None, "tp", "fsdp"),
        P("tp", "fsdp"),
        P("fsdp"),
        P("fsdp", "tp"),
        P("tp", "fsdp"),
        P("tp", "fsdp"),
    )
    return jax.shard_map(shards, mesh=mesh, in_specs=in_specs, out_specs=out_specs, check_vma=False)
```

```python
import functools
import math

import jax
import jax.numpy as jnp
from jax import lax
from jax.experimental import pallas as pl
from jax.experimental.pallas import tpu as pltpu
from jax.sharding import PartitionSpec as P

ROT = 16


norm_eps = 1e-05
masked_score = -1e30


def normalize(rows):
    centred = rows - jnp.mean(rows, axis=-1, keepdims=True)
    inverse = lax.rsqrt(jnp.mean(centred * centred, axis=-1, keepdims=True) + norm_eps)
    return (centred * inverse, inverse)


def gelu_parts(widened):
    cumulative = 0.5 * (1.0 + lax.erf(widened * (1.0 / math.sqrt(2.0))))
    density = jnp.exp(-0.5 * widened * widened) * (1.0 / math.sqrt(2.0 * math.pi))
    return (widened * cumulative, cumulative + widened * density)


def rotary_tables(positions, rotary):
    half = rotary // 2
    freqs = jnp.exp(jnp.arange(half, dtype=jnp.float32) * (-2.0 * math.log(10000.0) / rotary))
    angles = positions.astype(jnp.float32)[:, None, :] * freqs[None, :, None]
    return (jnp.cos(angles)[:, None, None], jnp.sin(angles)[:, None, None])


def rotate_forward(block, cosine, sine, half):
    first = block[..., :half, :]
    second = block[..., half : 2 * half, :]
    return jnp.concatenate(
        [first * cosine - second * sine, second * cosine + first * sine, block[..., 2 * half :, :]],
        axis=-2,
    )


def rotate_back(block, cosine, sine, half):
    first = block[..., :half, :]
    second = block[..., half : 2 * half, :]
    return jnp.concatenate(
        [first * cosine + second * sine, second * cosine - first * sine, block[..., 2 * half :, :]],
        axis=-2,
    )


def attend_kernel(block, scale, qkv_ref, grad_ref, base_ref, back_ref, mixed_ref,
                  queries, query_rows, keys, key_rows, values, value_rows, grads, grad_rows,
                  base_rows, key_sum, value_sum):
    parts, head_size, span = grad_ref.shape[0], grad_ref.shape[2], grad_ref.shape[3]
    length = parts * span
    for part in range(parts):
        at = pl.ds(part * span, span)
        queries[:, at] = (qkv_ref[part, 0, 0].astype(jnp.float32) * scale).astype(jnp.bfloat16)
        keys[:, at] = qkv_ref[part, 0, 1]
        values[:, at] = qkv_ref[part, 0, 2]
        grads[:, at] = grad_ref[part, 0]
    for source, target in (
        (queries, query_rows),
        (keys, key_rows),
        (values, value_rows),
        (grads, grad_rows),
    ):
        target[...] = source[...].astype(jnp.float32).T.astype(jnp.bfloat16)
    base_row = base_ref[0]
    base_rows[...] = jnp.broadcast_to(base_row, (128, length)).T
    for start in range(0, length, block):
        count = start + block
        here = slice(start, count)
        scores = jnp.dot(key_rows[:count], queries[:, here], preferred_element_type=jnp.float32)
        wide_base = jnp.concatenate([base_rows[:count]] * (block // 128), axis=1)
        same = wide_base == base_row[:, here]
        key_index = lax.broadcasted_iota(jnp.int32, (block, block), 0)
        query_index = lax.broadcasted_iota(jnp.int32, (block, block), 1)
        last = jnp.where(
            same[start:] & (key_index <= query_index), scores[start:], masked_score
        )
        if start:
            earlier = jnp.where(same[:start], scores[:start], masked_score)
            scores = jnp.concatenate([earlier, last], axis=0)
        else:
            scores = last
        top = jnp.max(scores, axis=0, keepdims=True)
        raised = jnp.exp(scores - top)
        probs = raised * (1.0 / jnp.sum(raised, axis=0, keepdims=True))
        weights = probs.astype(jnp.bfloat16)
        mixed = jnp.dot(values[:, :count], weights, preferred_element_type=jnp.float32).astype(
            jnp.bfloat16
        )
        grad_block = grads[:, here]
        delta = jnp.sum(
            mixed.astype(jnp.float32) * grad_block.astype(jnp.float32), axis=0, keepdims=True
        )
        prob_grads = jnp.dot(value_rows[:count], grad_block, preferred_element_type=jnp.float32)
        score_grads = (probs * (prob_grads - delta)).astype(jnp.bfloat16)
        query_part = jnp.dot(keys[:, :count], score_grads, preferred_element_type=jnp.float32)
        key_part = jnp.dot(score_grads, query_rows[here], preferred_element_type=jnp.float32)
        value_part = jnp.dot(weights, grad_rows[here], preferred_element_type=jnp.float32)
        if start:
            key_sum[:start] += key_part[:start]
            value_sum[:start] += value_part[:start]
        key_sum[here] = key_part[start:]
        value_sum[here] = value_part[start:]
        part, inside = start // span, start % span
        mixed_ref[part, 0, :, inside : inside + block] = mixed
        back_ref[part, 0, 0, :, inside : inside + block] = (query_part * scale).astype(jnp.bfloat16)
    for part in range(parts):
        at = pl.ds(part * span, span)
        back_ref[part, 0, 1] = key_sum[at].T.astype(jnp.bfloat16)
        back_ref[part, 0, 2] = value_sum[at].T.astype(jnp.bfloat16)


def attend(by_heads, grad_heads, item_base, scale):
    parts, items, unused, head_size, span = by_heads.shape
    length = parts * span
    block = min(256, span)
    wide = pltpu.VMEM((head_size, length), jnp.bfloat16)
    tall = pltpu.VMEM((length, head_size), jnp.bfloat16)
    total = pltpu.VMEM((length, head_size), jnp.float32)
    return pl.pallas_call(
        functools.partial(attend_kernel, block, scale),
        grid=(items,),
        in_specs=[
            pl.BlockSpec((parts, 1, 3, head_size, span), lambda i: (0, i, 0, 0, 0)),
            pl.BlockSpec((parts, 1, head_size, span), lambda i: (0, i, 0, 0)),
            pl.BlockSpec((1, 1, length), lambda i: (i, 0, 0)),
        ],
        out_specs=[
            pl.BlockSpec((parts, 1, 3, head_size, span), lambda i: (0, i, 0, 0, 0)),
            pl.BlockSpec((parts, 1, head_size, span), lambda i: (0, i, 0, 0)),
        ],
        out_shape=[
            jax.ShapeDtypeStruct(by_heads.shape, jnp.bfloat16),
            jax.ShapeDtypeStruct(grad_heads.shape, jnp.bfloat16),
        ],
        scratch_shapes=[wide, tall, wide, tall, wide, tall, wide, tall,
                        pltpu.VMEM((length, 128), jnp.float32), total, total],
        compiler_params=pltpu.CompilerParams(vmem_limit_bytes=48 * 1024 * 1024),
        cost_estimate=pl.CostEstimate(
            flops=7 * items * length * length * 256,
            bytes_accessed=4 * by_heads.size,
            transcendentals=items * length * length // 2,
        ),
    )(by_heads, grad_heads, item_base)


def sum_pair(share, axis):
    size = lax.axis_size(axis)
    if size == 2:
        other = lax.ppermute(share, axis, [(0, 1), (1, 0)])
        return share.astype(jnp.float32) + other.astype(jnp.float32)
    return lax.psum(share, axis).astype(jnp.float32)


def shards_general(
    block_input,
    positions,
    first_gain,
    first_shift,
    second_gain,
    second_shift,
    triple_weight,
    triple_bias,
    mixer_weight,
    output_bias,
    widen_weight,
    widen_bias,
    narrow_weight,
    cotangent,
):
    seqs, local_tokens, local_width = block_input.shape
    vectors = (first_gain, first_shift, second_gain, second_shift, output_bias, triple_bias, widen_bias)
    small = lax.all_gather(
        jnp.concatenate([vector.reshape(-1) for vector in vectors]), "fsdp", axis=0, tiled=False
    )
    groups = small.shape[0]
    pieces = []
    offset = 0
    for vector in vectors:
        pieces.append(small[:, offset : offset + vector.size].astype(jnp.float32))
        offset += vector.size
    gain_one, shift_one, gain_two, shift_two, bias_output = [
        piece.reshape(-1) for piece in pieces[:5]
    ]
    bias_triple = jnp.transpose(
        pieces[5].reshape((groups,) + triple_bias.shape), (1, 2, 0, 3)
    ).reshape(triple_bias.shape[0], triple_bias.shape[1], -1)
    bias_widen = jnp.transpose(
        pieces[6].reshape((groups,) + widen_bias.shape), (1, 0, 2)
    ).reshape(-1)
    all_positions = lax.all_gather(positions, "ctx", axis=1, tiled=True)
    whole_input = lax.all_gather(block_input, "tp", axis=2, tiled=True)
    weight_triple = lax.all_gather(triple_weight, "fsdp", axis=0, tiled=True)
    whole_cot = lax.all_gather(cotangent, "tp", axis=2, tiled=True)
    mixer_rows = mixer_weight.shape[0]
    joined = lax.all_gather(
        jnp.concatenate([mixer_weight, narrow_weight], axis=0), "fsdp", axis=1, tiled=True
    )
    weight_mixer, weight_narrow = joined[:mixer_rows], joined[mixer_rows:]
    weight_widen = lax.all_gather(widen_weight, "fsdp", axis=0, tiled=True)
    width = weight_triple.shape[0]
    heads_local, head_size = bias_triple.shape[1:]
    feature_start = lax.axis_index("tp") * local_width
    scale = head_size ** (-0.5)
    half = ROT // 2
    normed, inverse = normalize(whole_input.astype(jnp.float32))
    first_rows = (normed * gain_one + shift_one).astype(jnp.bfloat16)
    second_rows = (normed * gain_two + shift_two).astype(jnp.bfloat16)
    cosine, sine = rotary_tables(positions, ROT)
    weight_four = weight_triple.reshape(width, 3, heads_local, head_size)
    projected = jnp.einsum(
        "std,dchk->shckt", first_rows, weight_four, preferred_element_type=jnp.float32
    )
    projected = projected + jnp.transpose(bias_triple, (1, 0, 2))[None, :, :, :, None]
    turned = rotate_forward(projected[:, :, :2], cosine, sine, half)
    triple = jnp.concatenate([turned, projected[:, :, 2:]], axis=2).astype(jnp.bfloat16)
    parts = lax.axis_size("ctx")
    items = seqs * heads_local // parts
    by_heads = lax.all_to_all(
        triple.reshape(parts, items, 3, head_size, local_tokens),
        "ctx",
        split_axis=0,
        concat_axis=0,
        tiled=True,
    )
    mixer_four = weight_mixer.reshape(heads_local, head_size, width)
    mixed_grad = jnp.einsum(
        "ste,hke->shkt", whole_cot, mixer_four, preferred_element_type=jnp.float32
    ).astype(jnp.bfloat16)
    grad_heads = lax.all_to_all(
        mixed_grad.reshape(parts, items, head_size, local_tokens),
        "ctx",
        split_axis=0,
        concat_axis=0,
        tiled=True,
    )
    length = all_positions.shape[1]
    item_seq = (lax.axis_index("ctx") * items + jnp.arange(items, dtype=jnp.int32)) // heads_local
    base = (jnp.arange(length, dtype=jnp.int32)[None, :] - all_positions).astype(jnp.float32)
    item_base = jnp.take(base, item_seq, axis=0)[:, None, :]
    back_heads, mixed = attend(by_heads, grad_heads, item_base, scale)
    mixed_tokens = lax.all_to_all(
        mixed, "ctx", split_axis=0, concat_axis=0, tiled=True
    ).reshape(seqs, heads_local, head_size, local_tokens)
    back_float = (
        lax.all_to_all(back_heads, "ctx", split_axis=0, concat_axis=0, tiled=True)
        .reshape(seqs, heads_local, 3, head_size, local_tokens)
        .astype(jnp.float32)
    )
    widened = (
        jnp.einsum("std,df->stf", second_rows, weight_widen, preferred_element_type=jnp.float32)
        + bias_widen
    )
    activated_float, slope = gelu_parts(widened)
    activated = activated_float.astype(jnp.bfloat16)
    hidden_grad = (
        jnp.einsum("ste,fe->stf", whole_cot, weight_narrow, preferred_element_type=jnp.float32)
        * slope
    )
    widen_bias_grad = jnp.sum(hidden_grad, axis=(0, 1))
    hidden_rounded = hidden_grad.astype(jnp.bfloat16)
    narrow_grad = jnp.einsum(
        "stf,ste->fe", activated, whole_cot, preferred_element_type=jnp.float32
    ).astype(jnp.bfloat16)
    narrow_share = lax.psum_scatter(narrow_grad, "fsdp", scatter_dimension=1, tiled=True)
    widen_grad = jnp.einsum(
        "std,stf->df", second_rows, hidden_rounded, preferred_element_type=jnp.float32
    ).astype(jnp.bfloat16)
    widen_share = lax.psum_scatter(widen_grad, "fsdp", scatter_dimension=0, tiled=True)
    second_grad = jnp.einsum(
        "stf,df->std", hidden_rounded, weight_widen, preferred_element_type=jnp.float32
    ).astype(jnp.bfloat16)
    attention_part = jnp.einsum(
        "shkt,hke->ste", mixed_tokens, mixer_four, preferred_element_type=jnp.float32
    )
    branches = attention_part + jnp.einsum(
        "stf,fe->ste", activated, weight_narrow, preferred_element_type=jnp.float32
    )
    summed = lax.psum_scatter(
        branches.astype(jnp.bfloat16), "tp", scatter_dimension=2, tiled=True
    ).astype(jnp.float32)
    bias_slice = lax.dynamic_slice_in_dim(bias_output, feature_start, local_width, 0)
    block_output = (block_input.astype(jnp.float32) + summed + bias_slice).astype(jnp.bfloat16)
    mixer_grad = (
        jnp.einsum("shkt,ste->hke", mixed_tokens, whole_cot, preferred_element_type=jnp.float32)
        .reshape(weight_mixer.shape)
        .astype(jnp.bfloat16)
    )
    mixer_share = lax.psum_scatter(mixer_grad, "fsdp", scatter_dimension=1, tiled=True)
    unturned = rotate_back(back_float[:, :, :2], cosine, sine, half)
    projected_grad = jnp.concatenate([unturned, back_float[:, :, 2:]], axis=2)
    triple_bias_grad = jnp.transpose(jnp.sum(projected_grad, axis=(0, 4)), (1, 0, 2))
    projected_rounded = projected_grad.astype(jnp.bfloat16)
    first_grad = jnp.einsum(
        "shckt,dchk->std", projected_rounded, weight_four, preferred_element_type=jnp.float32
    ).astype(jnp.bfloat16)
    first_float = first_grad.astype(jnp.float32)
    second_float = second_grad.astype(jnp.float32)
    scaled = first_float * gain_one + second_float * gain_two
    scattered = lax.psum_scatter(
        scaled.astype(jnp.bfloat16), "tp", scatter_dimension=2, tiled=True
    ).astype(jnp.float32)
    row_sums = lax.psum(
        jnp.stack([jnp.sum(scaled, axis=-1), jnp.sum(scaled * normed, axis=-1)]), "tp"
    ) * (1.0 / width)
    triple_grad = (
        jnp.einsum(
            "std,shckt->dchk", first_rows, projected_rounded, preferred_element_type=jnp.float32
        )
        .reshape(weight_triple.shape)
        .astype(jnp.bfloat16)
    )
    triple_share = lax.psum_scatter(triple_grad, "fsdp", scatter_dimension=0, tiled=True)
    output_bias_grad = jnp.sum(whole_cot.astype(jnp.float32), axis=(0, 1))
    wide_sums = jnp.stack(
        [
            jnp.sum(first_float * normed, axis=(0, 1)),
            jnp.sum(first_float, axis=(0, 1)),
            jnp.sum(second_float * normed, axis=(0, 1)),
            jnp.sum(second_float, axis=(0, 1)),
            jnp.where(lax.axis_index("tp") == 0, output_bias_grad, 0.0),
        ]
    )
    wide_sums = lax.psum(wide_sums, ("fsdp", "ctx", "tp"))
    bias_sums = lax.psum(
        jnp.concatenate([triple_bias_grad.reshape(-1), widen_bias_grad]), ("fsdp", "ctx")
    )
    place = lax.axis_index("fsdp")
    vector_size = first_gain.shape[0]
    wide_sums = lax.dynamic_slice_in_dim(wide_sums, place * vector_size, vector_size, 1)
    triple_bias_out = lax.dynamic_slice_in_dim(
        bias_sums[: triple_bias_grad.size].reshape(triple_bias_grad.shape),
        place * triple_bias.shape[2],
        triple_bias.shape[2],
        2,
    )
    widen_bias_out = lax.dynamic_slice_in_dim(
        bias_sums[triple_bias_grad.size :].reshape(widen_bias.shape[0], -1),
        place * widen_bias.shape[1],
        widen_bias.shape[1],
        1,
    )
    own_normed = lax.dynamic_slice_in_dim(normed, feature_start, local_width, 2)
    input_grad = (
        cotangent.astype(jnp.float32)
        + inverse * (scattered - row_sums[0][..., None] - own_normed * row_sums[1][..., None])
    ).astype(jnp.bfloat16)
    return (
        block_output,
        input_grad,
        wide_sums[0],
        wide_sums[1],
        wide_sums[2],
        wide_sums[3],
        sum_pair(triple_share, "ctx"),
        triple_bias_out,
        sum_pair(mixer_share, "ctx"),
        wide_sums[4],
        sum_pair(widen_share, "ctx"),
        widen_bias_out,
        sum_pair(narrow_share, "ctx"),
    )


class Copies:
    def __init__(self, send, recv, local):
        self.send, self.recv, self.local = send, recv, local
        self.remotes = self.locals = 0

    def remote(self, source, target, device):
        index = self.remotes
        self.remotes += 1
        return pltpu.make_async_remote_copy(
            src_ref=source, dst_ref=target, send_sem=self.send.at[index], recv_sem=self.recv.at[index],
            device_id=device, device_id_type=pl.DeviceIdType.MESH,
        )

    def here(self, source, target):
        index = self.locals
        self.locals += 1
        return pltpu.make_async_copy(source, target, self.local.at[index])


def sem_shapes(remotes, local_copies):
    return [pltpu.SemaphoreType.DMA((remotes,)), pltpu.SemaphoreType.DMA((remotes,)),
            pltpu.SemaphoreType.DMA((local_copies,))]


def places(groups):
    z, c, t = lax.axis_index("fsdp"), lax.axis_index("ctx"), lax.axis_index("tp")
    near = t + 1 - 2 * lax.rem(t, 2)
    far = lax.rem(t + 2, 4)
    return z, c, t, near, far


def greet(devices):
    barrier = pltpu.get_barrier_semaphore()
    for device in devices:
        pl.semaphore_signal(barrier, inc=1, device_id=device, device_id_type=pl.DeviceIdType.MESH)
    pl.semaphore_wait(barrier, len(devices))


def aligned(index, step):
    return pl.ds(pl.multiple_of(index * step, step), step)


class Spread:
    def __init__(self, groups, copies, shards, wholes, by_rows):
        z, c, t, _, _ = places(groups)
        self.groups, self.shards, self.wholes, self.by_rows = groups, shards, wholes, by_rows
        self.keeps, self.shares, self.relays = [], [], []
        for a in range(len(shards)):
            shares, relays = [], []
            for k in range(1, groups):
                origin = lax.rem(z + groups - k, groups)
                shares.append(copies.remote(
                    self.half(a, c), self.part(a, z, c), (lax.rem(z + k, groups), c, t)))
                relays.append(copies.remote(self.part(a, origin, c), self.part(a, origin, c), (z, 1 - c, t)))
            self.shares.append(shares)
            self.relays.append(relays)
            self.keeps.append(copies.here(shards[a], self.whole_of(a, z)))

    def half(self, a, half):
        if len(self.shards[a].shape) == 3:
            return self.shards[a].at[:, aligned(half, self.shards[a].shape[1] // 2)]
        return self.shards[a].at[aligned(half, self.shards[a].shape[0] // 2)]

    def whole_of(self, a, group):
        if len(self.shards[a].shape) == 3:
            return self.wholes[a].at[:, aligned(group, self.shards[a].shape[1])]
        if self.by_rows[a]:
            return self.wholes[a].at[aligned(group, self.shards[a].shape[0])]
        return self.wholes[a].at[:, aligned(group, self.shards[a].shape[1])]

    def part(self, a, group, half):
        if len(self.shards[a].shape) == 3:
            return self.wholes[a].at[:, aligned(group * 2 + half, self.shards[a].shape[1] // 2)]
        rows, columns = self.shards[a].shape
        if self.by_rows[a]:
            return self.wholes[a].at[aligned(group * 2 + half, rows // 2)]
        return self.wholes[a].at[aligned(half, rows // 2), aligned(group, columns)]

    def start(self, a):
        for share in self.shares[a]:
            share.start()
        self.keeps[a].start()

    def relay(self, a, k):
        self.shares[a][k].wait_recv()
        self.relays[a][k].start()

    def arrive(self, a):
        self.keeps[a].wait()
        for relay in self.relays[a]:
            relay.wait_recv()

    def finish(self):
        for a in range(len(self.shards)):
            for share, relay in zip(self.shares[a], self.relays[a]):
                share.wait_send()
                relay.wait_send()


def front_kernel(groups, half_rotary, x_in, c_in, pos_in, turn_in, widen_in, triple_in, mixer_in, vec_in,
                 c_out, pos_out, turn_out, widen_out, triple_out, mixer_out, vec_out,
                 normed_out, first_out, second_out, active_out, slope_out, narrow_out, heads_out, mixed_grad_out,
                 stats_out, sums_out,
                 x_all, c_all, turn_all, widen_all, triple_all, mixer_all, vec_all, normed, first, second, active, slope,
                 narrow_grad, heads, mixed_grad, vec_float, send, recv, local):
    z, c, t, near, far = places(groups)
    copies = Copies(send, recv, local)
    y_peer, near_peer, far_peer = (z, 1 - c, t), (z, c, near), (z, c, far)
    ring = [lax.rem(z + k, groups) for k in range(1, groups)]
    greet([y_peer, near_peer, far_peer] + [(peer, c, t) for peer in ring])
    span, width = x_in.shape[1:]
    length, whole = x_all.shape
    started = []

    def start(copy):
        copy.start()
        started.append(copy)
        return copy

    def block(ref, half, feature):
        return ref.at[aligned(half, span), aligned(feature, width)]

    cross = 3 - t
    tensors = ((x_in, x_all), (c_in, c_all))
    stays = [copies.here(pos_in.at[c], pos_out.at[c]), copies.here(vec_in, vec_all.at[z]),
             copies.here(turn_in.at[c], turn_all.at[:, aligned(c, span)])]
    for copy in stays:
        copy.start()
    own = [copies.here(source.at[c], block(target, c, t)) for source, target in tensors]
    swaps = [copies.remote(source.at[1 - c], block(target, c, t), y_peer) for source, target in tensors]
    firsts = [
        [copies.remote(source.at[c], block(target, c, t), far_peer),
         copies.remote(source.at[c], block(target, c, t), near_peer)]
        for source, target in tensors
    ]
    weights = Spread(groups, copies, (widen_in, triple_in, mixer_in), (widen_all, triple_all, mixer_all),
                     (True, True, False))
    start(swaps[0])
    start(firsts[0][0])
    start(firsts[0][1])
    small = [start(copies.remote(vec_in, vec_all.at[z], (peer, c, t))) for peer in ring]
    position_swap = start(copies.remote(pos_in.at[1 - c], pos_out.at[c], y_peer))
    turn_swap = start(copies.remote(turn_in.at[1 - c], turn_all.at[:, aligned(c, span)], y_peer))
    weights.start(0)
    for copy in own:
        copy.start()
    start(firsts[1][1])
    weights.start(1)
    weights.start(2)

    def second_half(index):
        swaps[index].wait_recv()
        other = block(tensors[index][1], 1 - c, t)
        return [start(copies.remote(other, other, far_peer)), start(copies.remote(other, other, near_peer))]

    def pass_on(index, pair, half):
        pair[0].wait_recv()
        there = block(tensors[index][1], half, far)
        return start(copies.remote(there, there, near_peer))

    step_rows = min(256, span)
    saves = []

    def save(source, target):
        copy = copies.here(source, target)
        copy.start()
        saves.append(copy)

    def row_vector(index):
        pieces = []
        for group in range(groups):
            for k in range(width_rows):
                at = index * width_rows + k
                pieces.append(vec_float[group, at : at + 1])
        return jnp.concatenate(pieces, axis=1)

    width_rows = whole // groups // 128

    def normalise(half):
        gain_one, shift_one, gain_two, shift_two = [row_vector(index) for index in range(4)]

        @pl.loop(0, span // step_rows)
        def _(step):
            at = pl.ds(pl.multiple_of(half * span + step * step_rows, step_rows), step_rows)
            rows = x_all[at].astype(jnp.float32)
            mean = jnp.mean(rows, axis=-1, keepdims=True)
            centred = rows - mean
            inverse = lax.rsqrt(jnp.mean(centred * centred, axis=-1, keepdims=True) + norm_eps)
            unit = centred * inverse
            normed[at] = unit.astype(jnp.bfloat16)
            first[at] = (unit * gain_one + shift_one).astype(jnp.bfloat16)
            second[at] = (unit * gain_two + shift_two).astype(jnp.bfloat16)
            stats_out[0:1, at] = jnp.broadcast_to(mean, (step_rows, 128)).T[0:1]
            stats_out[1:2, at] = jnp.broadcast_to(inverse, (step_rows, 128)).T[0:1]

        for source, target in ((normed, normed_out), (first, first_out), (second, second_out)):
            save(source.at[aligned(half, span)], target.at[aligned(half, span)])

    seconds_x = second_half(0)
    relayed = [pass_on(0, firsts[0], c)]
    start(firsts[1][0])
    for copy in small:
        copy.wait_recv()
    for copy in stays:
        copy.wait()
    vec_float[...] = vec_all[...].astype(jnp.float32)
    save(vec_all, vec_out)
    firsts[0][1].wait_recv()
    own[0].wait()
    relayed[0].wait_recv()
    normalise(c)
    weights.relay(0, 0)
    for k in range(1, groups - 1):
        weights.relay(0, k)
    start(swaps[1])
    relayed.append(pass_on(0, seconds_x, 1 - c))
    seconds_x[1].wait_recv()
    relayed[1].wait_recv()
    normalise(1 - c)
    for k in range(groups - 1):
        weights.relay(1, k)
    weights.arrive(0)
    save(widen_all, widen_out)
    relayed.append(pass_on(1, firsts[1], c))
    hidden = widen_all.shape[1]

    def placed_vector(first_row, count):
        pieces = []
        for at in range(first_row, first_row + count):
            piece = vec_float[0, at : at + 1]
            for group in range(1, groups):
                piece = piece + vec_float[group, at : at + 1]
            pieces.append(piece)
        return jnp.concatenate(pieces, axis=1)

    bias = placed_vector(5 * width_rows, hidden // 128)
    columns = triple_all.shape[2]
    bias_row = 5 * width_rows + hidden // 128
    triple_bias = [placed_vector(bias_row + k * (columns // 128), columns // 128) for k in range(3)]
    head_size = heads.shape[2]

    def project(half):
        @pl.loop(0, span // step_rows)
        def _(step):
            at = pl.ds(pl.multiple_of(half * span + step * step_rows, step_rows), step_rows)
            cosine, sine = turn_all[0:half_rotary, at], turn_all[half_rotary : 2 * half_rotary, at]
            for k in range(3):
                block = jnp.dot(first[at], triple_all[k], preferred_element_type=jnp.float32) + triple_bias[k]
                block = block.T
                for head in range(columns // head_size):
                    part = block[head * head_size : (head + 1) * head_size]
                    if k < 2:
                        one, two = part[:half_rotary], part[half_rotary : 2 * half_rotary]
                        part = jnp.concatenate(
                            [one * cosine - two * sine, two * cosine + one * sine, part[2 * half_rotary :]], axis=0
                        )
                    heads[k, head, :, at] = part.astype(jnp.bfloat16)

    def widen(half):
        @pl.loop(0, span // step_rows)
        def _(step):
            at = pl.ds(pl.multiple_of(half * span + step * step_rows, step_rows), step_rows)
            widened = jnp.dot(second[at], widen_all[...], preferred_element_type=jnp.float32) + bias
            value, gradient = gelu_parts(widened)
            active[at] = value.astype(jnp.bfloat16)
            slope[at] = gradient.astype(jnp.bfloat16)

        save(active.at[aligned(half, span)], active_out.at[aligned(half, span)])
        save(slope.at[aligned(half, span)], slope_out.at[aligned(half, span)])

    widen(c)
    seconds_c = second_half(1)
    widen(1 - c)
    for k in range(groups - 1):
        weights.relay(2, k)
    weights.arrive(1)
    save(triple_all, triple_out)
    position_swap.wait_recv()
    turn_swap.wait_recv()
    save(turn_all, turn_out)
    project(c)
    relayed.append(pass_on(1, seconds_c, 1 - c))
    project(1 - c)
    save(heads, heads_out)
    weights.arrive(2)
    save(mixer_all, mixer_out)
    own[1].wait()
    firsts[1][1].wait_recv()
    seconds_c[1].wait_recv()
    for copy in relayed[2:]:
        copy.wait_recv()
    save(c_all, c_out)

    @pl.loop(0, length // step_rows)
    def _(step):
        at = pl.ds(pl.multiple_of(step * step_rows, step_rows), step_rows)
        mixed_grad[:, at] = lax.dot_general(
            mixer_all[...], c_all[at], (((1,), (1,)), ((), ())), preferred_element_type=jnp.float32
        ).astype(jnp.bfloat16)

    save(mixed_grad, mixed_grad_out)
    tile = min(256, hidden)
    for at in range(0, hidden, tile):
        narrow_grad[at : at + tile] = lax.dot_general(
            active[:, at : at + tile], c_all[...], (((0,), (0,)), ((), ())), preferred_element_type=jnp.float32
        ).astype(jnp.bfloat16)
    save(narrow_grad, narrow_out)

    sums_out[...] = jnp.zeros_like(sums_out)

    @pl.loop(0, length // step_rows)
    def _(step):
        at = pl.ds(pl.multiple_of(step * step_rows, step_rows), step_rows)
        sums_out[0:1] += jnp.sum(c_all[at].astype(jnp.float32), axis=0, keepdims=True)

    for copy in started:
        copy.wait_send()
    weights.finish()
    for copy in saves:
        copy.wait()


def front(groups, half_rotary, head_size, block_input, cotangent, positions, turns, widen_weight, triple_weight,
          mixer_weight, vectors):
    seqs, span, width = block_input.shape
    length, whole = seqs * span, width * 4
    hidden, columns = widen_weight.shape[1], triple_weight.shape[2]
    any_space = pl.BlockSpec(memory_space=pl.ANY)
    in_vmem = pl.BlockSpec(memory_space=pltpu.VMEM)
    bf16, f32 = jnp.bfloat16, jnp.float32
    vec_shape = (groups,) + vectors.shape
    triple_shape = (3, whole, columns)
    turn_shape = (turns.shape[1], length)
    heads_shape = (3, columns // head_size, head_size, length)
    shapes = [
        ((length, whole), bf16), (turn_shape, f32), ((whole, hidden), bf16), (triple_shape, bf16),
        ((columns, whole), bf16), (vec_shape, bf16), ((length, whole), bf16), ((length, whole), bf16),
        ((length, whole), bf16), ((length, hidden), bf16), ((length, hidden), bf16), ((hidden, whole), bf16),
        (heads_shape, bf16), ((columns, length), bf16),
    ]
    outs = [jax.ShapeDtypeStruct(*shape) for shape in shapes]
    return pl.pallas_call(
        functools.partial(front_kernel, groups, half_rotary),
        in_specs=[any_space] * 8,
        out_specs=[any_space] * 15 + [in_vmem] * 2,
        out_shape=outs[:1] + [jax.ShapeDtypeStruct(positions.shape, positions.dtype)] + outs[1:] + [
            jax.ShapeDtypeStruct((8, length), f32),
            jax.ShapeDtypeStruct((8, whole), f32),
        ],
        scratch_shapes=[pltpu.VMEM((length, whole), bf16)] + [pltpu.VMEM(*shape) for shape in shapes] + [
            pltpu.VMEM(vec_shape, f32),
        ] + sem_shapes(16 + 7 * (groups - 1), 32),
        compiler_params=pltpu.CompilerParams(
            collective_id=0, has_side_effects=True, vmem_limit_bytes=58 * 1024 * 1024
        ),
        name="front",
    )(block_input, cotangent, positions, turns, widen_weight, triple_weight, mixer_weight, vectors)


class Reduce:
    def __init__(self, groups, copies, arrays, outs, by_rows, owns, others, sums, inbox, done):
        self.groups, self.copies, self.arrays, self.outs, self.by_rows = groups, copies, arrays, outs, by_rows
        self.owns, self.others, self.sums, self.inbox, self.done = owns, others, sums, inbox, done
        self.z, self.c, self.t, _, _ = places(groups)
        self.y_peer = (self.z, 1 - self.c, self.t)
        self.order = list(range(1, groups)) + [0]
        self.loads, self.swaps, self.sends, self.backs, self.keeps = [], [], [], [], []

    def piece(self, a, group, half):
        array = self.arrays[a]
        if self.by_rows[a]:
            return array.at[aligned(group * 2 + half, array.shape[0] // (2 * self.groups))]
        return array.at[aligned(half, array.shape[0] // 2), aligned(group, array.shape[1] // self.groups)]

    def out_half(self, a, half):
        return self.outs[a].at[aligned(half, self.outs[a].shape[0] // 2)]

    def make(self):
        for a in range(len(self.arrays)):
            loads, swaps, sends = [], [], []
            for slot, k in enumerate(self.order):
                group = lax.rem(self.z + k, self.groups)
                loads.append(self.copies.here(self.piece(a, group, self.c), self.owns[a].at[slot]))
                swaps.append(self.copies.remote(self.piece(a, group, 1 - self.c), self.others[a].at[slot], self.y_peer))
                if k:
                    sends.append(self.copies.remote(
                        self.sums[a].at[slot], self.inbox[a].at[slot], (group, self.c, self.t)))
            self.loads.append(loads)
            self.swaps.append(swaps)
            self.sends.append(sends)
            self.backs.append(self.copies.remote(self.done[a], self.out_half(a, self.c), self.y_peer))
            self.keeps.append(self.copies.here(self.done[a], self.out_half(a, self.c)))

    def start(self, a):
        for swap, load in zip(self.swaps[a], self.loads[a]):
            swap.start()
            load.start()

    def add(self, a, slot):
        self.loads[a][slot].wait()
        self.swaps[a][slot].wait_recv()
        total = self.owns[a][slot].astype(jnp.float32) + self.others[a][slot].astype(jnp.float32)
        self.sums[a][slot] = total.astype(jnp.bfloat16)
        if slot < self.groups - 1:
            self.sends[a][slot].start()

    def total(self, a):
        total = self.sums[a][self.groups - 1].astype(jnp.float32)
        for slot in range(self.groups - 1):
            self.sends[a][slot].wait_recv()
            total = total + self.inbox[a][slot].astype(jnp.float32)
        self.done[a][...] = total.astype(jnp.bfloat16)
        self.backs[a].start()
        self.keeps[a].start()

    def finish(self):
        for a in range(len(self.arrays)):
            for swap in self.swaps[a]:
                swap.wait_send()
            for send in self.sends[a]:
                send.wait_send()
            self.backs[a].wait()
            self.keeps[a].wait()


def reduce_shapes(groups, shapes, by_rows):
    owns, others, sums, inbox, done, outs = [], [], [], [], [], []
    for (rows, columns), along in zip(shapes, by_rows):
        part = (rows // (2 * groups), columns) if along else (rows // 2, columns // groups)
        owns.append(pltpu.VMEM((groups,) + part, jnp.bfloat16))
        others.append(pltpu.VMEM((groups,) + part, jnp.bfloat16))
        sums.append(pltpu.VMEM((groups,) + part, jnp.bfloat16))
        inbox.append(pltpu.VMEM((groups - 1,) + part, jnp.bfloat16))
        done.append(pltpu.VMEM(part, jnp.bfloat16))
        outs.append(jax.ShapeDtypeStruct((2 * part[0], part[1]), jnp.bfloat16))
    return owns + others + sums + inbox + done, outs


def reduce_from(groups, copies, arrays, outs, by_rows, scratch):
    n = len(arrays)
    cut = [scratch[n * i : n * (i + 1)] for i in range(5)]
    made = Reduce(groups, copies, arrays, outs, by_rows, *cut)
    made.make()
    return made


def attend_sequence(block, scale, half_rotary, qkv_ref, grad_ref, hot_ref, turn_ref, back_ref, mixed_ref, bias_ref,
                    queries, key_rows, value_rows, key_sum, value_sum):
    head_size, length = grad_ref.shape[1:]
    f32, bf16 = jnp.float32, jnp.bfloat16
    hot = hot_ref[...]
    blank = jnp.zeros_like(hot)
    queries[...] = jnp.concatenate(
        [qkv_ref[0, 0].astype(f32) * scale, (1.0 - hot) * masked_score, blank], axis=0
    ).astype(bf16)
    key_rows[...] = jnp.concatenate([qkv_ref[1, 0].astype(f32), hot, blank], axis=0).T.astype(bf16)
    value_rows[...] = qkv_ref[2, 0].astype(f32).T.astype(bf16)
    keys, values, grads = qkv_ref.at[1, 0], qkv_ref.at[2, 0], grad_ref.at[0]
    last_dims = (((1,), (1,)), ((), ()))

    def unturn(grad, at):
        rounded = grad.astype(bf16).astype(f32)
        cosine, sine = turn_ref[0:half_rotary, at], turn_ref[half_rotary : 2 * half_rotary, at]
        one, two = rounded[:half_rotary], rounded[half_rotary : 2 * half_rotary]
        return jnp.concatenate(
            [one * cosine + two * sine, two * cosine - one * sine, rounded[2 * half_rotary :]], axis=0
        )

    query_bias = jnp.zeros((head_size, 1), f32)
    for start in range(0, length, block):
        count = start + block
        here = slice(start, count)
        scores = jnp.dot(key_rows[:count], queries[:, here], preferred_element_type=f32)
        key_index = lax.broadcasted_iota(jnp.int32, (block, block), 0)
        query_index = lax.broadcasted_iota(jnp.int32, (block, block), 1)
        last = jnp.where(key_index <= query_index, scores[start:], masked_score)
        scores = jnp.concatenate([scores[:start], last], axis=0) if start else last
        top = jnp.max(scores, axis=0, keepdims=True)
        raised = jnp.exp(scores - top)
        inverse = 1.0 / jnp.sum(raised, axis=0, keepdims=True)
        weights = raised.astype(bf16)
        mixed = (jnp.dot(values[:, :count], weights, preferred_element_type=f32) * inverse).astype(bf16)
        scaled = grads[:, here].astype(f32) * inverse
        delta = jnp.sum(mixed.astype(f32) * scaled, axis=0, keepdims=True)
        scaled = scaled.astype(bf16)
        prob_grads = jnp.dot(value_rows[:count], scaled, preferred_element_type=f32)
        score_grads = (raised * (prob_grads - delta)).astype(bf16)
        query_part = jnp.dot(keys[:, :count], score_grads, preferred_element_type=f32)
        key_part = lax.dot_general(queries[:head_size, here], score_grads, last_dims, preferred_element_type=f32)
        value_part = lax.dot_general(scaled, weights, last_dims, preferred_element_type=f32)
        if start:
            key_sum[:, :start] += key_part[:, :start]
            value_sum[:, :start] += value_part[:, :start]
        key_sum[:, here] = key_part[:, start:]
        value_sum[:, here] = value_part[:, start:]
        mixed_ref[0, :, here] = mixed
        turned = unturn(query_part * scale, here)
        query_bias = query_bias + jnp.sum(turned, axis=1, keepdims=True)
        back_ref[0, 0, :, here] = turned.astype(bf16)
    turned = unturn(key_sum[...], slice(0, length))
    back_ref[1, 0] = turned.astype(bf16)
    rounded = value_sum[...].astype(bf16)
    back_ref[2, 0] = rounded
    bias_ref[0, 0] = jnp.broadcast_to(query_bias, (head_size, 128))
    bias_ref[1, 0] = jnp.broadcast_to(jnp.sum(turned, axis=1, keepdims=True), (head_size, 128))
    bias_ref[2, 0] = jnp.broadcast_to(jnp.sum(rounded.astype(f32), axis=1, keepdims=True), (head_size, 128))


def attend_reduce_kernel(block, scale, half_rotary, groups, items, qkv_ref, grad_ref, hot_ref, turn_ref, grads_in,
                         shard_in, back_ref, mixed_ref, bias_ref, grads_out, whole_out, *refs):
    attention, refs = refs[:5], refs[5:]
    scratch, (send, recv, local) = refs[:-3], refs[-3:]
    item = pl.program_id(0)
    copies = Copies(send, recv, local)
    reduce = reduce_from(groups, copies, (grads_in,), (grads_out,), (False,), scratch)
    weights = Spread(groups, copies, (shard_in,), (whole_out,), (False,))
    plan = [[] for _ in range(items + 1)]
    for slot in range(groups):
        plan[min(items, 1 + (slot * (items - 1) + 1) // groups)].append(functools.partial(reduce.add, 0, slot))
    for k in range(groups - 1):
        plan[min(items, 1 + k)].append(functools.partial(weights.relay, 0, k))
    plan[items].append(functools.partial(reduce.total, 0))

    def run(actions):
        for action in actions:
            action()

    def begin():
        z, c, t, _, _ = places(groups)
        greet([(z, 1 - c, t)] + [(lax.rem(z + k, groups), c, t) for k in range(1, groups)])
        reduce.start(0)
        weights.start(0)

    pl.when(item == 0)(begin)
    for i in range(1, items):
        if plan[i]:
            pl.when(item == i)(functools.partial(run, plan[i]))

    attend_sequence(block, scale, half_rotary, qkv_ref, grad_ref, hot_ref, turn_ref, back_ref, mixed_ref, bias_ref,
                    *attention)

    def end():
        run(plan[items])
        reduce.finish()
        weights.arrive(0)
        weights.finish()

    pl.when(item == items - 1)(end)


def attend_reduce(heads, grad_heads, hot, turns, scale, half_rotary, groups, narrow_grad, narrow_weight):
    _, items, head_size, length = heads.shape
    block = min(512, length)
    bf16, f32 = jnp.bfloat16, jnp.float32
    deep = head_size + 2 * hot.shape[0]
    shapes, outs = reduce_shapes(groups, [narrow_grad.shape], (False,))
    any_space = pl.BlockSpec(memory_space=pl.ANY)
    return pl.pallas_call(
        functools.partial(attend_reduce_kernel, block, scale, half_rotary, groups, items),
        grid=(items,),
        in_specs=[
            pl.BlockSpec((3, 1, head_size, length), lambda i: (0, i, 0, 0)),
            pl.BlockSpec((1, head_size, length), lambda i: (i, 0, 0)),
            pl.BlockSpec(hot.shape, lambda i: (0, 0)),
            pl.BlockSpec(turns.shape, lambda i: (0, 0)),
            any_space,
            any_space,
        ],
        out_specs=[
            pl.BlockSpec((3, 1, head_size, length), lambda i: (0, i, 0, 0)),
            pl.BlockSpec((1, head_size, length), lambda i: (i, 0, 0)),
            pl.BlockSpec((3, 1, head_size, 128), lambda i: (0, i, 0, 0)),
            any_space,
            any_space,
        ],
        out_shape=[
            jax.ShapeDtypeStruct(heads.shape, bf16),
            jax.ShapeDtypeStruct(grad_heads.shape, bf16),
            jax.ShapeDtypeStruct((3, items, head_size, 128), f32),
        ] + outs + [
            jax.ShapeDtypeStruct((narrow_weight.shape[0], narrow_weight.shape[1] * groups), bf16)
        ],
        scratch_shapes=[
            pltpu.VMEM((deep, length), bf16),
            pltpu.VMEM((length, deep), bf16),
            pltpu.VMEM((length, head_size), bf16),
            pltpu.VMEM((head_size, length), f32),
            pltpu.VMEM((head_size, length), f32),
        ] + shapes + sem_shapes(2 * groups + 2 * (groups - 1), groups + 2),
        compiler_params=pltpu.CompilerParams(
            collective_id=1, has_side_effects=True, vmem_limit_bytes=56 * 1024 * 1024
        ),
        cost_estimate=pl.CostEstimate(
            flops=7 * items * length * length * 256,
            bytes_accessed=4 * heads.size,
            transcendentals=items * length * length // 2,
        ),
        name="attend_reduce",
    )(heads, grad_heads, hot, turns, narrow_grad, narrow_weight)


class ReduceWhole:
    def __init__(self, groups, copies, arrays, outs, by_rows, scratch):
        z, c, t, _, _ = places(groups)
        n = len(arrays)
        self.groups, self.outs = groups, outs
        self.owns, self.inbox, self.mine, self.theirs = [scratch[n * i : n * (i + 1)] for i in range(4)]
        self.loads, self.sends, self.swaps = [], [], []

        def piece(a, group):
            array = arrays[a]
            if by_rows[a]:
                return array.at[aligned(group, array.shape[0] // groups)]
            return array.at[:, aligned(group, array.shape[1] // groups)]

        for a in range(n):
            self.loads.append(copies.here(piece(a, z), self.owns[a]))
            sends = []
            for k in range(1, groups):
                group = lax.rem(z + k, groups)
                sends.append(copies.remote(piece(a, group), self.inbox[a].at[k - 1], (group, c, t)))
            self.sends.append(sends)
            self.swaps.append(copies.remote(self.mine[a], self.theirs[a], (z, 1 - c, t)))

    def start(self):
        for load, sends in zip(self.loads, self.sends):
            for send in sends:
                send.start()
            load.start()

    def total(self):
        for a, sends in enumerate(self.sends):
            self.loads[a].wait()
            total = self.owns[a][...].astype(jnp.float32)
            for k, send in enumerate(sends):
                send.wait_recv()
                total = total + self.inbox[a][k].astype(jnp.float32)
            self.mine[a][...] = total.astype(jnp.bfloat16)
            self.swaps[a].start()

    def finish(self):
        for a, swap in enumerate(self.swaps):
            swap.wait()
            total = self.mine[a][...].astype(jnp.float32) + self.theirs[a][...].astype(jnp.float32)
            if len(self.outs[a].shape) == 3:
                rows = total.shape[0] // 3
                for k in range(3):
                    self.outs[a][k] = total[k * rows : (k + 1) * rows].T
            else:
                self.outs[a][...] = total
            for send in self.sends[a]:
                send.wait_send()


def reduce_whole_shapes(groups, shapes, by_rows):
    parts = [(rows // groups, columns) if along else (rows, columns // groups)
             for (rows, columns), along in zip(shapes, by_rows)]
    scratch = [pltpu.VMEM(part, jnp.bfloat16) for part in parts]
    scratch += [pltpu.VMEM((groups - 1,) + part, jnp.bfloat16) for part in parts]
    scratch += [pltpu.VMEM(part, jnp.bfloat16) for part in parts] * 2
    return scratch, [jax.ShapeDtypeStruct(part, jnp.float32) for part in parts]


def back_kernel(groups, turned_in, first_in, mixed_in, c_in, mixer_in, active_in, narrow_in, slope_in, second_in,
                triple_in, widen_in, normed_in, gains, norm_stats, front_sums, triple_bias_in,
                out_ref, grad_ref, stats_out, widen_share, wide_out, bias_out, triple_share, mixer_share,
                turned, grad_part, mixed, c_all, mixer, active, narrow, hidden, second, triple, widen, normed,
                out_part, triple_grad, mixer_grad, near_box, far_box, widen_grad, wide_sum, bias_sum,
                row_box, row_sum, wide_box, wide_two, wide_three, bias_two, bias_three, *refs):
    scratch, (send, recv, local) = refs[:-3], refs[-3:]
    z, c, t, near, far = places(groups)
    copies = Copies(send, recv, local)
    y_peer = (z, 1 - c, t)
    near_peer, far_peer, cross_peer = (z, c, near), (z, c, far), (z, c, 3 - t)
    ring = [lax.rem(z + k, groups) for k in range(1, groups)]
    span, width = out_ref.shape[1:]
    length, whole = c_all.shape
    quarter = span // 2
    step_rows = min(256, quarter)
    f32, bf16 = jnp.float32, jnp.bfloat16
    loads = []
    for source, target in (
        (turned_in, turned), (first_in, grad_part), (mixed_in, mixed), (c_in, c_all), (mixer_in, mixer),
        (active_in, active), (narrow_in, narrow), (slope_in, hidden), (second_in, second), (triple_in, triple),
        (widen_in, widen), (normed_in, normed),
    ):
        load = copies.here(source, target)
        load.start()
        loads.append(load)
    greet([y_peer, near_peer, far_peer, cross_peer] + [(peer, c, t) for peer in ring])
    started, finals, keeps = [], [], []

    def start(copy):
        copy.start()
        started.append(copy)
        return copy

    whole_scratch, half_scratch = scratch[:8], scratch[8:]
    attention_sums = ReduceWhole(
        groups, copies, (triple_grad, mixer_grad), (triple_share, mixer_share), (False, False), whole_scratch
    )
    widen_sums = reduce_from(groups, copies, (widen_grad,), (widen_share,), (True,), half_scratch)
    parts = (out_part, grad_part)
    halves = (1 - c, c)
    nears = [[], []]
    fars = [[], []]

    def send_near(index, turn):
        rows = aligned(halves[turn], span)
        part = parts[index]
        nears[index].append([
            start(copies.remote(
                part.at[rows, aligned(3 - t, width)], near_box.at[index, 0, rows], near_peer)),
            start(copies.remote(
                part.at[rows, aligned(near, width)], near_box.at[index, 1, rows], near_peer)),
        ])

    def rows_of(turn, step):
        return pl.ds(pl.multiple_of(halves[turn] * span + step * quarter, quarter), quarter)

    def send_far(index, turn):
        nears[index][turn][0].wait_recv()
        part = parts[index]
        for step in range(2):
            rows = rows_of(turn, step)
            total = part[rows, aligned(far, width)].astype(f32) + near_box[index, 0, rows].astype(f32)
            part[rows, aligned(far, width)] = total.astype(bf16)
            fars[index].append(start(copies.remote(
                part.at[rows, aligned(far, width)], far_box.at[index, rows], far_peer)))

    def close(index, turn, target):
        nears[index][turn][1].wait_recv()
        part = parts[index]
        for step in range(2):
            rows = rows_of(turn, step)
            fars[index][2 * turn + step].wait_recv()
            done = part.at[rows, aligned(t, width)]
            total = (
                part[rows, aligned(t, width)].astype(f32)
                + near_box[index, 1, rows].astype(f32)
                + far_box[index, rows].astype(f32)
            )
            part[rows, aligned(t, width)] = total.astype(bf16)
            place = target.at[c, pl.ds(step * quarter, quarter)]
            if turn == 0:
                finals.append(start(copies.remote(done, place, y_peer)))
            else:
                keep = copies.here(done, place)
                keep.start()
                keeps.append(keep)

    def loop(turn, body):
        @pl.loop(0, span // step_rows)
        def _(step):
            body(pl.ds(pl.multiple_of(halves[turn] * span + step * step_rows, step_rows), step_rows))

    for load in loads[:4]:
        load.wait()
    columns = mixer.shape[0]
    for k in range(3):
        rows = slice(k * columns, (k + 1) * columns)
        triple_grad[rows] = jnp.dot(turned[rows], grad_part[...], preferred_element_type=f32).astype(bf16)
    mixer_grad[...] = jnp.dot(mixed[...], c_all[...], preferred_element_type=f32).astype(bf16)
    attention_sums.start()
    for load in loads[4:7]:
        load.wait()

    def branches(at):
        total = lax.dot_general(mixed[:, at], mixer[...], (((0,), (0,)), ((), ())), preferred_element_type=f32)
        total = total + jnp.dot(active[at], narrow[...], preferred_element_type=f32)
        out_part[at] = total.astype(bf16)

    for turn in range(2):
        loop(turn, branches)
        send_near(0, turn)
    loads[7].wait()
    bias_sum[...] = jnp.zeros_like(bias_sum)
    bias_sum[1:2] = triple_bias_in[...]

    def hidden_grads(at):
        grads = lax.dot_general(c_all[at], narrow[...], (((1,), (1,)), ((), ())), preferred_element_type=f32)
        grads = grads * hidden[at].astype(f32)
        bias_sum[0:1] += jnp.sum(grads, axis=0, keepdims=True)
        hidden[at] = grads.astype(bf16)

    loop(0, hidden_grads)
    send_far(0, 0)
    loop(1, hidden_grads)
    send_far(0, 1)
    loads[8].wait()
    depth = widen_grad.shape[0]
    tile = min(256, depth)
    for at in range(0, depth, tile):
        widen_grad[at : at + tile] = lax.dot_general(
            second[:, at : at + tile], hidden[...], (((0,), (0,)), ((), ())), preferred_element_type=f32
        ).astype(bf16)
    widen_sums.start(0)
    bias_two[c] = bias_sum[...]
    bias_swap = start(copies.remote(bias_two.at[c], bias_two.at[c], y_peer))
    for load in loads[9:]:
        load.wait()
    wide_sum[...] = front_sums[...]
    gain_one, gain_two = gains[0:1], gains[1:2]

    def norm_grads(at):
        unit = normed[at].astype(f32)
        one = sum(
            lax.dot_general(turned[k * columns : (k + 1) * columns, at], triple[k], (((0,), (1,)), ((), ())),
                            preferred_element_type=f32)
            for k in range(3)
        )
        wide_sum[0:1] += jnp.sum(one * unit, axis=0, keepdims=True)
        wide_sum[1:2] += jnp.sum(one, axis=0, keepdims=True)
        two = lax.dot_general(hidden[at], widen[...], (((1,), (1,)), ((), ())), preferred_element_type=f32)
        wide_sum[2:3] += jnp.sum(two * unit, axis=0, keepdims=True)
        wide_sum[3:4] += jnp.sum(two, axis=0, keepdims=True)
        scaled = one * gain_one + two * gain_two
        grad_part[at] = scaled.astype(bf16)
        rows = scaled.shape[0]
        total = jnp.sum(scaled, axis=-1, keepdims=True) * (1.0 / whole)
        along = jnp.sum(scaled * unit, axis=-1, keepdims=True) * (1.0 / whole)
        row_box[t, 0:1, at] = jnp.broadcast_to(total, (rows, 128)).T[0:1]
        row_box[t, 1:2, at] = jnp.broadcast_to(along, (rows, 128)).T[0:1]

    loop(0, norm_grads)
    send_near(1, 0)
    loop(1, norm_grads)
    send_near(1, 1)
    wide_box[t] = wide_sum[...]
    tp_peers = [(t + k) - 4 * ((t + k) // 4) for k in range(1, 4)]
    tp_sent = [start(copies.remote(row_box.at[t], row_box.at[t], (z, c, peer))) for peer in tp_peers]
    tp_sent += [start(copies.remote(wide_box.at[t], wide_box.at[t], (z, c, peer))) for peer in tp_peers]
    send_far(1, 0)
    close(0, 0, out_ref)
    send_far(1, 1)
    for slot in range(groups):
        widen_sums.add(0, slot)
    close(0, 1, out_ref)
    for copy in tp_sent:
        copy.wait_recv()
    row_sum[0:2] = row_box[0] + row_box[1] + row_box[2] + row_box[3]
    row_sum[2:4] = norm_stats[0:2]
    finals.append(start(copies.remote(row_sum.at[:, aligned(1 - c, span)], stats_out.at[c], y_peer)))
    keeps.append(copies.here(row_sum.at[:, aligned(c, span)], stats_out.at[c]))
    keeps[-1].start()
    wide_two[c] = wide_box[0] + wide_box[1] + wide_box[2] + wide_box[3]
    wide_swap = start(copies.remote(wide_two.at[c], wide_two.at[c], y_peer))
    bias_swap.wait_recv()
    bias_three[z] = bias_two[0] + bias_two[1]
    sums_sent = [start(copies.remote(bias_three.at[z], bias_three.at[z], (peer, c, t))) for peer in ring]
    attention_sums.total()
    wide_swap.wait_recv()
    wide_three[z] = wide_two[0] + wide_two[1]
    sums_sent += [start(copies.remote(wide_three.at[z], wide_three.at[z], (peer, c, t))) for peer in ring]
    close(1, 0, grad_ref)
    for copy in sums_sent:
        copy.wait_recv()
    bias_total, wide_total = bias_three[0], wide_three[0]
    for group in range(1, groups):
        bias_total = bias_total + bias_three[group]
        wide_total = wide_total + wide_three[group]
    bias_out[...] = bias_total
    wide_out[...] = wide_total
    widen_sums.total(0)
    close(1, 1, grad_ref)
    attention_sums.finish()
    for copy in finals:
        copy.wait_recv()
    for copy in started:
        copy.wait_send()
    for copy in keeps:
        copy.wait()
    widen_sums.finish()


def back(groups, turned, first, mixed, c_rows, mixer_weight, active, narrow_weight, slope, second, triple_weight,
         widen_weight, normed, gains, norm_stats, front_sums, triple_bias_row):
    length, whole = c_rows.shape
    hidden = active.shape[1]
    width, span = whole // 4, length // 2
    columns = mixed.shape[0]
    any_space = pl.BlockSpec(memory_space=pl.ANY)
    in_vmem = pl.BlockSpec(memory_space=pltpu.VMEM)
    bf16, f32 = jnp.bfloat16, jnp.float32
    grads = [(3 * columns, whole), (columns, whole)]
    whole_scratch, whole_outs = reduce_whole_shapes(groups, grads, (False, False))
    whole_outs[0] = jax.ShapeDtypeStruct((3, whole // groups, columns), f32)
    half_scratch, half_outs = reduce_shapes(groups, [(whole, hidden)], (True,))
    residents = (turned, first, mixed, c_rows, mixer_weight, active, narrow_weight, slope, second, triple_weight,
                 widen_weight, normed)
    wide, bias = (8, whole), (8, max(hidden, triple_bias_row.shape[1]))
    return pl.pallas_call(
        functools.partial(back_kernel, groups),
        in_specs=[any_space] * 12 + [in_vmem] * 4,
        out_specs=[any_space] * 4 + [in_vmem] * 4,
        out_shape=[
            jax.ShapeDtypeStruct((2, span, width), bf16),
            jax.ShapeDtypeStruct((2, span, width), bf16),
            jax.ShapeDtypeStruct((2, 4, span), f32),
        ] + half_outs + [
            jax.ShapeDtypeStruct(wide, f32),
            jax.ShapeDtypeStruct(bias, f32),
        ] + whole_outs,
        scratch_shapes=[pltpu.VMEM(array.shape, bf16) for array in residents] + [
            pltpu.VMEM((length, whole), bf16),
            pltpu.VMEM(grads[0], bf16),
            pltpu.VMEM(grads[1], bf16),
            pltpu.VMEM((2, 2, length, width), bf16),
            pltpu.VMEM((2, length, width), bf16),
            pltpu.VMEM((whole, hidden), bf16),
            pltpu.VMEM(wide, f32),
            pltpu.VMEM(bias, f32),
            pltpu.VMEM((4, 2, length), f32),
            pltpu.VMEM((4, length), f32),
            pltpu.VMEM((4,) + wide, f32),
            pltpu.VMEM((2,) + wide, f32),
            pltpu.VMEM((groups,) + wide, f32),
            pltpu.VMEM((2,) + bias, f32),
            pltpu.VMEM((groups,) + bias, f32),
        ] + whole_scratch + half_scratch + sem_shapes(
            32 + 2 * (groups - 1) + 2 * groups + 2 * groups, 20 + groups + 3),
        compiler_params=pltpu.CompilerParams(
            collective_id=2, has_side_effects=True, vmem_limit_bytes=62 * 1024 * 1024
        ),
        name="back",
    )(*residents, gains, norm_stats, front_sums, triple_bias_row)


def shards_sequence(
    block_input,
    positions,
    first_gain,
    first_shift,
    second_gain,
    second_shift,
    triple_weight,
    triple_bias,
    mixer_weight,
    output_bias,
    widen_weight,
    widen_bias,
    narrow_weight,
    cotangent,
):
    seqs, span, local_width = block_input.shape
    length = seqs * span
    groups = lax.axis_size("fsdp")
    hidden_rows, hidden_part = widen_bias.shape
    heads_local, bias_part = triple_bias.shape[1:]
    head_size = bias_part * groups
    place = lax.axis_index("fsdp")
    here = jnp.arange(groups) == place
    placed_widen = jnp.where(here[None, :, None], widen_bias[:, None, :], 0)
    placed_triple = jnp.where(here[None, None, :, None], triple_bias[:, :, None, :], 0)
    vectors = (first_gain, first_shift, second_gain, second_shift, output_bias)
    flat = jnp.concatenate(
        [vector.reshape(-1) for vector in vectors + (placed_widen, placed_triple)]
    )
    padded = -(-flat.size // 2048) * 2048
    packed = jnp.pad(flat, (0, padded - flat.size)).reshape(-1, 128)
    cosine, sine = rotary_tables(positions, ROT)
    turns = jnp.concatenate([cosine[:, 0, 0], sine[:, 0, 0]], axis=1)
    (cot_rows, places_out, turn_rows, weight_widen, weight_triple, weight_mixer, small, normed_rows, first_rows,
     second_rows, activated, slope, narrow_grad, heads, mixed_grad, norm_stats, front_sums) = front(
        groups, ROT // 2, head_size, block_input, cotangent, positions.reshape(seqs, span // 128, 128), turns,
        widen_weight, jnp.transpose(triple_weight, (1, 0, 2)), mixer_weight, packed,
    )
    width = weight_widen.shape[0]
    small = small.reshape(groups, -1)
    vector_size = first_gain.shape[0]
    gain_one, _, gain_two, _, bias_output = [
        small[:, at * vector_size : (at + 1) * vector_size].astype(jnp.float32).reshape(-1) for at in range(5)
    ]
    begun = (places_out.reshape(length // 128, 128) == 0).astype(jnp.float32)
    lanes, token_rows = jnp.arange(128), jnp.arange(length // 128)
    count = jnp.dot(begun, (lanes[:, None] <= lanes[None, :]).astype(jnp.float32))
    before = jnp.dot((token_rows[None, :] < token_rows[:, None]).astype(jnp.float32), begun)
    documents = (count + jnp.sum(before, axis=1, keepdims=True)).reshape(1, length) - 1.0
    hot = (documents == jnp.arange(8, dtype=jnp.float32)[:, None]).astype(jnp.float32)
    turned_back, mixed, bias_lanes, narrow_share, weight_narrow = attend_reduce(
        heads, mixed_grad.reshape(heads_local, head_size, length), hot, turn_rows, head_size ** (-0.5), ROT // 2,
        groups, narrow_grad, narrow_weight,
    )
    row = bias_lanes[..., 0].reshape(1, -1)
    bias_width = max(activated.shape[1], row.shape[1])
    row = jnp.pad(row, ((0, 0), (0, bias_width - row.shape[1])))
    zero = jnp.zeros((width,), jnp.float32)
    first_sums = jnp.stack(
        [zero] * 4 + [jnp.where(lax.axis_index("tp") == 0, front_sums[0], 0.0)] + [zero] * 3
    )
    summed, scattered, row_stats, widen_share, wide_sums, bias_sums, triple_share, mixer_share = back(
        groups, turned_back.reshape(-1, length), first_rows, mixed.reshape(-1, length), cot_rows, weight_mixer, activated,
        weight_narrow, slope, second_rows, weight_triple, weight_widen, normed_rows, jnp.stack([gain_one, gain_two]),
        norm_stats, first_sums, row,
    )
    feature_start = lax.axis_index("tp") * local_width
    bias_slice = lax.dynamic_slice_in_dim(bias_output, feature_start, local_width, 0)
    own_rows = block_input.astype(jnp.float32)
    block_output = (own_rows + summed.astype(jnp.float32) + bias_slice).astype(jnp.bfloat16)
    own_normed = (own_rows - row_stats[:, 2, :, None]) * row_stats[:, 3, :, None]
    input_grad = (
        cotangent.astype(jnp.float32)
        + row_stats[:, 3, :, None]
        * (scattered.astype(jnp.float32) - row_stats[:, 0, :, None] - own_normed * row_stats[:, 1, :, None])
    ).astype(jnp.bfloat16)
    wide_sums = lax.dynamic_slice_in_dim(wide_sums, place * vector_size, vector_size, 1)
    triple_bias_out = lax.dynamic_slice_in_dim(
        bias_sums[1, : 3 * heads_local * head_size].reshape(3, heads_local, head_size),
        place * triple_bias.shape[2],
        triple_bias.shape[2],
        2,
    )
    widen_bias_out = lax.dynamic_slice_in_dim(
        bias_sums[0, : activated.shape[1]].reshape(hidden_rows, -1), place * hidden_part, hidden_part, 1
    )
    return (
        block_output,
        input_grad,
        wide_sums[0],
        wide_sums[1],
        wide_sums[2],
        wide_sums[3],
        jnp.transpose(triple_share, (1, 0, 2)),
        triple_bias_out,
        mixer_share,
        wide_sums[4],
        widen_share.astype(jnp.float32),
        widen_bias_out,
        narrow_share.astype(jnp.float32),
    )


def shards(block_input, *others):
    seqs = block_input.shape[0]
    if seqs == 2 and lax.axis_size("ctx") == 2 and lax.axis_size("tp") == 4 and lax.axis_size("fsdp") > 1:
        return shards_sequence(block_input, *others)
    return shards_general(block_input, *others)


def solution(mesh):
    in_specs = (
        P("fsdp", "ctx", "tp"),
        P("fsdp", "ctx"),
        P("fsdp"),
        P("fsdp"),
        P("fsdp"),
        P("fsdp"),
        P("fsdp", None, "tp"),
        P(None, "tp", "fsdp"),
        P("tp", "fsdp"),
        P("fsdp"),
        P("fsdp", "tp"),
        P("tp", "fsdp"),
        P("tp", "fsdp"),
        P("fsdp", "ctx", "tp"),
    )
    out_specs = (
        P("fsdp", "ctx", "tp"),
        P("fsdp", "ctx", "tp"),
        P("fsdp"),
        P("fsdp"),
        P("fsdp"),
        P("fsdp"),
        P("fsdp", None, "tp"),
        P(None, "tp", "fsdp"),
        P("tp", "fsdp"),
        P("fsdp"),
        P("fsdp", "tp"),
        P("tp", "fsdp"),
        P("tp", "fsdp"),
    )
    return jax.shard_map(shards, mesh=mesh, in_specs=in_specs, out_specs=out_specs, check_vma=False)
```

```python
import functools
import math

import jax
import jax.numpy as jnp
from jax import lax
from jax.experimental import pallas as pl
from jax.experimental.pallas import tpu as pltpu
from jax.sharding import PartitionSpec as P

ROT = 16


norm_eps = 1e-05
masked_score = -1e30


def normalize(rows):
    centred = rows - jnp.mean(rows, axis=-1, keepdims=True)
    inverse = lax.rsqrt(jnp.mean(centred * centred, axis=-1, keepdims=True) + norm_eps)
    return (centred * inverse, inverse)


def gelu_parts(widened):
    cumulative = 0.5 * (1.0 + lax.erf(widened * (1.0 / math.sqrt(2.0))))
    density = jnp.exp(-0.5 * widened * widened) * (1.0 / math.sqrt(2.0 * math.pi))
    return (widened * cumulative, cumulative + widened * density)


def rotary_tables(positions, rotary):
    half = rotary // 2
    freqs = jnp.exp(jnp.arange(half, dtype=jnp.float32) * (-2.0 * math.log(10000.0) / rotary))
    angles = positions.astype(jnp.float32)[:, None, :] * freqs[None, :, None]
    return (jnp.cos(angles)[:, None, None], jnp.sin(angles)[:, None, None])


def rotate_forward(block, cosine, sine, half):
    first = block[..., :half, :]
    second = block[..., half : 2 * half, :]
    return jnp.concatenate(
        [first * cosine - second * sine, second * cosine + first * sine, block[..., 2 * half :, :]],
        axis=-2,
    )


def rotate_back(block, cosine, sine, half):
    first = block[..., :half, :]
    second = block[..., half : 2 * half, :]
    return jnp.concatenate(
        [first * cosine + second * sine, second * cosine - first * sine, block[..., 2 * half :, :]],
        axis=-2,
    )


def attend_kernel(block, scale, qkv_ref, grad_ref, base_ref, back_ref, mixed_ref,
                  queries, query_rows, keys, key_rows, values, value_rows, grads, grad_rows,
                  base_rows, key_sum, value_sum):
    parts, head_size, span = grad_ref.shape[0], grad_ref.shape[2], grad_ref.shape[3]
    length = parts * span
    for part in range(parts):
        at = pl.ds(part * span, span)
        queries[:, at] = (qkv_ref[part, 0, 0].astype(jnp.float32) * scale).astype(jnp.bfloat16)
        keys[:, at] = qkv_ref[part, 0, 1]
        values[:, at] = qkv_ref[part, 0, 2]
        grads[:, at] = grad_ref[part, 0]
    for source, target in (
        (queries, query_rows),
        (keys, key_rows),
        (values, value_rows),
        (grads, grad_rows),
    ):
        target[...] = source[...].astype(jnp.float32).T.astype(jnp.bfloat16)
    base_row = base_ref[0]
    base_rows[...] = jnp.broadcast_to(base_row, (128, length)).T
    for start in range(0, length, block):
        count = start + block
        here = slice(start, count)
        scores = jnp.dot(key_rows[:count], queries[:, here], preferred_element_type=jnp.float32)
        wide_base = jnp.concatenate([base_rows[:count]] * (block // 128), axis=1)
        same = wide_base == base_row[:, here]
        key_index = lax.broadcasted_iota(jnp.int32, (block, block), 0)
        query_index = lax.broadcasted_iota(jnp.int32, (block, block), 1)
        last = jnp.where(
            same[start:] & (key_index <= query_index), scores[start:], masked_score
        )
        if start:
            earlier = jnp.where(same[:start], scores[:start], masked_score)
            scores = jnp.concatenate([earlier, last], axis=0)
        else:
            scores = last
        top = jnp.max(scores, axis=0, keepdims=True)
        raised = jnp.exp(scores - top)
        probs = raised * (1.0 / jnp.sum(raised, axis=0, keepdims=True))
        weights = probs.astype(jnp.bfloat16)
        mixed = jnp.dot(values[:, :count], weights, preferred_element_type=jnp.float32).astype(
            jnp.bfloat16
        )
        grad_block = grads[:, here]
        delta = jnp.sum(
            mixed.astype(jnp.float32) * grad_block.astype(jnp.float32), axis=0, keepdims=True
        )
        prob_grads = jnp.dot(value_rows[:count], grad_block, preferred_element_type=jnp.float32)
        score_grads = (probs * (prob_grads - delta)).astype(jnp.bfloat16)
        query_part = jnp.dot(keys[:, :count], score_grads, preferred_element_type=jnp.float32)
        key_part = jnp.dot(score_grads, query_rows[here], preferred_element_type=jnp.float32)
        value_part = jnp.dot(weights, grad_rows[here], preferred_element_type=jnp.float32)
        if start:
            key_sum[:start] += key_part[:start]
            value_sum[:start] += value_part[:start]
        key_sum[here] = key_part[start:]
        value_sum[here] = value_part[start:]
        part, inside = start // span, start % span
        mixed_ref[part, 0, :, inside : inside + block] = mixed
        back_ref[part, 0, 0, :, inside : inside + block] = (query_part * scale).astype(jnp.bfloat16)
    for part in range(parts):
        at = pl.ds(part * span, span)
        back_ref[part, 0, 1] = key_sum[at].T.astype(jnp.bfloat16)
        back_ref[part, 0, 2] = value_sum[at].T.astype(jnp.bfloat16)


def attend(by_heads, grad_heads, item_base, scale):
    parts, items, unused, head_size, span = by_heads.shape
    length = parts * span
    block = min(256, span)
    wide = pltpu.VMEM((head_size, length), jnp.bfloat16)
    tall = pltpu.VMEM((length, head_size), jnp.bfloat16)
    total = pltpu.VMEM((length, head_size), jnp.float32)
    return pl.pallas_call(
        functools.partial(attend_kernel, block, scale),
        grid=(items,),
        in_specs=[
            pl.BlockSpec((parts, 1, 3, head_size, span), lambda i: (0, i, 0, 0, 0)),
            pl.BlockSpec((parts, 1, head_size, span), lambda i: (0, i, 0, 0)),
            pl.BlockSpec((1, 1, length), lambda i: (i, 0, 0)),
        ],
        out_specs=[
            pl.BlockSpec((parts, 1, 3, head_size, span), lambda i: (0, i, 0, 0, 0)),
            pl.BlockSpec((parts, 1, head_size, span), lambda i: (0, i, 0, 0)),
        ],
        out_shape=[
            jax.ShapeDtypeStruct(by_heads.shape, jnp.bfloat16),
            jax.ShapeDtypeStruct(grad_heads.shape, jnp.bfloat16),
        ],
        scratch_shapes=[wide, tall, wide, tall, wide, tall, wide, tall,
                        pltpu.VMEM((length, 128), jnp.float32), total, total],
        compiler_params=pltpu.CompilerParams(vmem_limit_bytes=48 * 1024 * 1024),
        cost_estimate=pl.CostEstimate(
            flops=7 * items * length * length * 256,
            bytes_accessed=4 * by_heads.size,
            transcendentals=items * length * length // 2,
        ),
    )(by_heads, grad_heads, item_base)


def sum_pair(share, axis):
    size = lax.axis_size(axis)
    if size == 2:
        other = lax.ppermute(share, axis, [(0, 1), (1, 0)])
        return share.astype(jnp.float32) + other.astype(jnp.float32)
    return lax.psum(share, axis).astype(jnp.float32)


def shards_general(
    block_input,
    positions,
    first_gain,
    first_shift,
    second_gain,
    second_shift,
    triple_weight,
    triple_bias,
    mixer_weight,
    output_bias,
    widen_weight,
    widen_bias,
    narrow_weight,
    cotangent,
):
    seqs, local_tokens, local_width = block_input.shape
    vectors = (first_gain, first_shift, second_gain, second_shift, output_bias, triple_bias, widen_bias)
    small = lax.all_gather(
        jnp.concatenate([vector.reshape(-1) for vector in vectors]), "fsdp", axis=0, tiled=False
    )
    groups = small.shape[0]
    pieces = []
    offset = 0
    for vector in vectors:
        pieces.append(small[:, offset : offset + vector.size].astype(jnp.float32))
        offset += vector.size
    gain_one, shift_one, gain_two, shift_two, bias_output = [
        piece.reshape(-1) for piece in pieces[:5]
    ]
    bias_triple = jnp.transpose(
        pieces[5].reshape((groups,) + triple_bias.shape), (1, 2, 0, 3)
    ).reshape(triple_bias.shape[0], triple_bias.shape[1], -1)
    bias_widen = jnp.transpose(
        pieces[6].reshape((groups,) + widen_bias.shape), (1, 0, 2)
    ).reshape(-1)
    all_positions = lax.all_gather(positions, "ctx", axis=1, tiled=True)
    whole_input = lax.all_gather(block_input, "tp", axis=2, tiled=True)
    weight_triple = lax.all_gather(triple_weight, "fsdp", axis=0, tiled=True)
    whole_cot = lax.all_gather(cotangent, "tp", axis=2, tiled=True)
    mixer_rows = mixer_weight.shape[0]
    joined = lax.all_gather(
        jnp.concatenate([mixer_weight, narrow_weight], axis=0), "fsdp", axis=1, tiled=True
    )
    weight_mixer, weight_narrow = joined[:mixer_rows], joined[mixer_rows:]
    weight_widen = lax.all_gather(widen_weight, "fsdp", axis=0, tiled=True)
    width = weight_triple.shape[0]
    heads_local, head_size = bias_triple.shape[1:]
    feature_start = lax.axis_index("tp") * local_width
    scale = head_size ** (-0.5)
    half = ROT // 2
    normed, inverse = normalize(whole_input.astype(jnp.float32))
    first_rows = (normed * gain_one + shift_one).astype(jnp.bfloat16)
    second_rows = (normed * gain_two + shift_two).astype(jnp.bfloat16)
    cosine, sine = rotary_tables(positions, ROT)
    weight_four = weight_triple.reshape(width, 3, heads_local, head_size)
    projected = jnp.einsum(
        "std,dchk->shckt", first_rows, weight_four, preferred_element_type=jnp.float32
    )
    projected = projected + jnp.transpose(bias_triple, (1, 0, 2))[None, :, :, :, None]
    turned = rotate_forward(projected[:, :, :2], cosine, sine, half)
    triple = jnp.concatenate([turned, projected[:, :, 2:]], axis=2).astype(jnp.bfloat16)
    parts = lax.axis_size("ctx")
    items = seqs * heads_local // parts
    by_heads = lax.all_to_all(
        triple.reshape(parts, items, 3, head_size, local_tokens),
        "ctx",
        split_axis=0,
        concat_axis=0,
        tiled=True,
    )
    mixer_four = weight_mixer.reshape(heads_local, head_size, width)
    mixed_grad = jnp.einsum(
        "ste,hke->shkt", whole_cot, mixer_four, preferred_element_type=jnp.float32
    ).astype(jnp.bfloat16)
    grad_heads = lax.all_to_all(
        mixed_grad.reshape(parts, items, head_size, local_tokens),
        "ctx",
        split_axis=0,
        concat_axis=0,
        tiled=True,
    )
    length = all_positions.shape[1]
    item_seq = (lax.axis_index("ctx") * items + jnp.arange(items, dtype=jnp.int32)) // heads_local
    base = (jnp.arange(length, dtype=jnp.int32)[None, :] - all_positions).astype(jnp.float32)
    item_base = jnp.take(base, item_seq, axis=0)[:, None, :]
    back_heads, mixed = attend(by_heads, grad_heads, item_base, scale)
    mixed_tokens = lax.all_to_all(
        mixed, "ctx", split_axis=0, concat_axis=0, tiled=True
    ).reshape(seqs, heads_local, head_size, local_tokens)
    back_float = (
        lax.all_to_all(back_heads, "ctx", split_axis=0, concat_axis=0, tiled=True)
        .reshape(seqs, heads_local, 3, head_size, local_tokens)
        .astype(jnp.float32)
    )
    widened = (
        jnp.einsum("std,df->stf", second_rows, weight_widen, preferred_element_type=jnp.float32)
        + bias_widen
    )
    activated_float, slope = gelu_parts(widened)
    activated = activated_float.astype(jnp.bfloat16)
    hidden_grad = (
        jnp.einsum("ste,fe->stf", whole_cot, weight_narrow, preferred_element_type=jnp.float32)
        * slope
    )
    widen_bias_grad = jnp.sum(hidden_grad, axis=(0, 1))
    hidden_rounded = hidden_grad.astype(jnp.bfloat16)
    narrow_grad = jnp.einsum(
        "stf,ste->fe", activated, whole_cot, preferred_element_type=jnp.float32
    ).astype(jnp.bfloat16)
    narrow_share = lax.psum_scatter(narrow_grad, "fsdp", scatter_dimension=1, tiled=True)
    widen_grad = jnp.einsum(
        "std,stf->df", second_rows, hidden_rounded, preferred_element_type=jnp.float32
    ).astype(jnp.bfloat16)
    widen_share = lax.psum_scatter(widen_grad, "fsdp", scatter_dimension=0, tiled=True)
    second_grad = jnp.einsum(
        "stf,df->std", hidden_rounded, weight_widen, preferred_element_type=jnp.float32
    ).astype(jnp.bfloat16)
    attention_part = jnp.einsum(
        "shkt,hke->ste", mixed_tokens, mixer_four, preferred_element_type=jnp.float32
    )
    branches = attention_part + jnp.einsum(
        "stf,fe->ste", activated, weight_narrow, preferred_element_type=jnp.float32
    )
    summed = lax.psum_scatter(
        branches.astype(jnp.bfloat16), "tp", scatter_dimension=2, tiled=True
    ).astype(jnp.float32)
    bias_slice = lax.dynamic_slice_in_dim(bias_output, feature_start, local_width, 0)
    block_output = (block_input.astype(jnp.float32) + summed + bias_slice).astype(jnp.bfloat16)
    mixer_grad = (
        jnp.einsum("shkt,ste->hke", mixed_tokens, whole_cot, preferred_element_type=jnp.float32)
        .reshape(weight_mixer.shape)
        .astype(jnp.bfloat16)
    )
    mixer_share = lax.psum_scatter(mixer_grad, "fsdp", scatter_dimension=1, tiled=True)
    unturned = rotate_back(back_float[:, :, :2], cosine, sine, half)
    projected_grad = jnp.concatenate([unturned, back_float[:, :, 2:]], axis=2)
    triple_bias_grad = jnp.transpose(jnp.sum(projected_grad, axis=(0, 4)), (1, 0, 2))
    projected_rounded = projected_grad.astype(jnp.bfloat16)
    first_grad = jnp.einsum(
        "shckt,dchk->std", projected_rounded, weight_four, preferred_element_type=jnp.float32
    ).astype(jnp.bfloat16)
    first_float = first_grad.astype(jnp.float32)
    second_float = second_grad.astype(jnp.float32)
    scaled = first_float * gain_one + second_float * gain_two
    scattered = lax.psum_scatter(
        scaled.astype(jnp.bfloat16), "tp", scatter_dimension=2, tiled=True
    ).astype(jnp.float32)
    row_sums = lax.psum(
        jnp.stack([jnp.sum(scaled, axis=-1), jnp.sum(scaled * normed, axis=-1)]), "tp"
    ) * (1.0 / width)
    triple_grad = (
        jnp.einsum(
            "std,shckt->dchk", first_rows, projected_rounded, preferred_element_type=jnp.float32
        )
        .reshape(weight_triple.shape)
        .astype(jnp.bfloat16)
    )
    triple_share = lax.psum_scatter(triple_grad, "fsdp", scatter_dimension=0, tiled=True)
    output_bias_grad = jnp.sum(whole_cot.astype(jnp.float32), axis=(0, 1))
    wide_sums = jnp.stack(
        [
            jnp.sum(first_float * normed, axis=(0, 1)),
            jnp.sum(first_float, axis=(0, 1)),
            jnp.sum(second_float * normed, axis=(0, 1)),
            jnp.sum(second_float, axis=(0, 1)),
            jnp.where(lax.axis_index("tp") == 0, output_bias_grad, 0.0),
        ]
    )
    wide_sums = lax.psum(wide_sums, ("fsdp", "ctx", "tp"))
    bias_sums = lax.psum(
        jnp.concatenate([triple_bias_grad.reshape(-1), widen_bias_grad]), ("fsdp", "ctx")
    )
    place = lax.axis_index("fsdp")
    vector_size = first_gain.shape[0]
    wide_sums = lax.dynamic_slice_in_dim(wide_sums, place * vector_size, vector_size, 1)
    triple_bias_out = lax.dynamic_slice_in_dim(
        bias_sums[: triple_bias_grad.size].reshape(triple_bias_grad.shape),
        place * triple_bias.shape[2],
        triple_bias.shape[2],
        2,
    )
    widen_bias_out = lax.dynamic_slice_in_dim(
        bias_sums[triple_bias_grad.size :].reshape(widen_bias.shape[0], -1),
        place * widen_bias.shape[1],
        widen_bias.shape[1],
        1,
    )
    own_normed = lax.dynamic_slice_in_dim(normed, feature_start, local_width, 2)
    input_grad = (
        cotangent.astype(jnp.float32)
        + inverse * (scattered - row_sums[0][..., None] - own_normed * row_sums[1][..., None])
    ).astype(jnp.bfloat16)
    return (
        block_output,
        input_grad,
        wide_sums[0],
        wide_sums[1],
        wide_sums[2],
        wide_sums[3],
        sum_pair(triple_share, "ctx"),
        triple_bias_out,
        sum_pair(mixer_share, "ctx"),
        wide_sums[4],
        sum_pair(widen_share, "ctx"),
        widen_bias_out,
        sum_pair(narrow_share, "ctx"),
    )


class Copies:
    def __init__(self, send, recv, local):
        self.send, self.recv, self.local = send, recv, local
        self.remotes = self.locals = 0

    def remote(self, source, target, device):
        index = self.remotes
        self.remotes += 1
        return pltpu.make_async_remote_copy(
            src_ref=source, dst_ref=target, send_sem=self.send.at[index], recv_sem=self.recv.at[index],
            device_id=device, device_id_type=pl.DeviceIdType.MESH,
        )

    def here(self, source, target):
        index = self.locals
        self.locals += 1
        return pltpu.make_async_copy(source, target, self.local.at[index])


def sem_shapes(remotes, local_copies):
    return [pltpu.SemaphoreType.DMA((remotes,)), pltpu.SemaphoreType.DMA((remotes,)),
            pltpu.SemaphoreType.DMA((local_copies,))]


def places(groups):
    z, c, t = lax.axis_index("fsdp"), lax.axis_index("ctx"), lax.axis_index("tp")
    near = t + 1 - 2 * lax.rem(t, 2)
    far = lax.rem(t + 2, 4)
    return z, c, t, near, far


def greet(devices):
    barrier = pltpu.get_barrier_semaphore()
    for device in devices:
        pl.semaphore_signal(barrier, inc=1, device_id=device, device_id_type=pl.DeviceIdType.MESH)
    pl.semaphore_wait(barrier, len(devices))


def aligned(index, step):
    return pl.ds(pl.multiple_of(index * step, step), step)


def line_peers():
    z = lax.axis_index("fsdp")
    return z + 1 - 2 * lax.rem(z, 2), lax.rem(z + 2, 4), 3 - z


class Spread:
    def __init__(self, groups, copies, shards, wholes, by_rows, halved):
        z, c, t, _, _ = places(groups)
        beside, across, cross = line_peers()
        self.groups, self.shards, self.wholes, self.by_rows, self.halved = groups, shards, wholes, by_rows, halved
        self.keeps, self.shares, self.relays = [], [], []
        for a in range(len(shards)):
            def region(group):
                return self.part(a, group, c) if halved[a] else self.whole_of(a, group)

            own = self.half(a, c) if halved[a] else shards[a]
            self.shares.append([
                copies.remote(own, region(z), (across, c, t)),
                copies.remote(own, region(z), (beside, c, t)),
                copies.remote(region(across), region(across), (beside, c, t)),
            ])
            self.relays.append([
                copies.remote(region(origin), region(origin), (z, 1 - c, t)) for origin in (across, beside, cross)
            ] if halved[a] else [])
            self.keeps.append(copies.here(shards[a], self.whole_of(a, z)))

    def half(self, a, half):
        if len(self.shards[a].shape) == 3:
            return self.shards[a].at[:, aligned(half, self.shards[a].shape[1] // 2)]
        return self.shards[a].at[aligned(half, self.shards[a].shape[0] // 2)]

    def whole_of(self, a, group):
        if len(self.shards[a].shape) == 3:
            return self.wholes[a].at[:, aligned(group, self.shards[a].shape[1])]
        if self.by_rows[a]:
            return self.wholes[a].at[aligned(group, self.shards[a].shape[0])]
        return self.wholes[a].at[:, aligned(group, self.shards[a].shape[1])]

    def part(self, a, group, half):
        if len(self.shards[a].shape) == 3:
            return self.wholes[a].at[:, aligned(group * 2 + half, self.shards[a].shape[1] // 2)]
        rows, columns = self.shards[a].shape
        if self.by_rows[a]:
            return self.wholes[a].at[aligned(group * 2 + half, rows // 2)]
        return self.wholes[a].at[aligned(half, rows // 2), aligned(group, columns)]

    def start(self, a):
        self.shares[a][0].start()
        self.shares[a][1].start()
        self.keeps[a].start()

    def relay(self, a, k):
        self.shares[a][k].wait_recv()
        if k == 0:
            self.shares[a][2].start()
        if self.halved[a]:
            self.relays[a][k].start()

    def arrive(self, a):
        self.keeps[a].wait()
        for relay in self.relays[a]:
            relay.wait_recv()

    def finish(self):
        for a in range(len(self.shards)):
            for copy in self.shares[a] + self.relays[a]:
                copy.wait_send()


def front_kernel(groups, half_rotary, x_in, c_in, pos_in, turn_in, widen_in, triple_in, mixer_in, vec_in,
                 c_out, pos_out, turn_out, widen_out, triple_out, mixer_out, vec_out,
                 normed_out, first_out, second_out, active_out, slope_out, narrow_out, heads_out, mixed_grad_out,
                 stats_out, sums_out,
                 x_all, c_all, turn_all, widen_all, triple_all, mixer_all, vec_all, normed, first, second, active, slope,
                 narrow_grad, heads, mixed_grad, vec_float, send, recv, local):
    z, c, t, near, far = places(groups)
    copies = Copies(send, recv, local)
    y_peer, near_peer, far_peer = (z, 1 - c, t), (z, c, near), (z, c, far)
    ring = [lax.rem(z + k, groups) for k in range(1, groups)]
    greet([y_peer, near_peer, far_peer] + [(peer, c, t) for peer in ring])
    span, width = x_in.shape[1:]
    length, whole = x_all.shape
    started = []

    def start(copy):
        copy.start()
        started.append(copy)
        return copy

    def block(ref, half, feature):
        return ref.at[aligned(half, span), aligned(feature, width)]

    cross = 3 - t
    tensors = ((x_in, x_all), (c_in, c_all))
    stays = [copies.here(pos_in.at[c], pos_out.at[c]), copies.here(vec_in, vec_all.at[z]),
             copies.here(turn_in.at[c], turn_all.at[:, aligned(c, span)])]
    for copy in stays:
        copy.start()
    own = [copies.here(source.at[c], block(target, c, t)) for source, target in tensors]
    swaps = [copies.remote(source.at[1 - c], block(target, c, t), y_peer) for source, target in tensors]
    firsts = [
        [copies.remote(source.at[c], block(target, c, t), far_peer),
         copies.remote(source.at[c], block(target, c, t), near_peer)]
        for source, target in tensors
    ]
    weights = Spread(groups, copies, (widen_in, triple_in, mixer_in), (widen_all, triple_all, mixer_all),
                     (True, True, False), (True, False, True))
    start(swaps[0])
    start(firsts[0][0])
    start(firsts[0][1])
    small = [start(copies.remote(vec_in, vec_all.at[z], (peer, c, t))) for peer in ring]
    position_swap = start(copies.remote(pos_in.at[1 - c], pos_out.at[c], y_peer))
    turn_swap = start(copies.remote(turn_in.at[1 - c], turn_all.at[:, aligned(c, span)], y_peer))
    weights.start(0)
    for copy in own:
        copy.start()

    def second_half(index):
        swaps[index].wait_recv()
        other = block(tensors[index][1], 1 - c, t)
        return [start(copies.remote(other, other, far_peer)), start(copies.remote(other, other, near_peer))]

    def pass_on(index, pair, half):
        pair[0].wait_recv()
        there = block(tensors[index][1], half, far)
        return start(copies.remote(there, there, near_peer))

    step_rows = min(256, span)
    saves = []

    def save(source, target):
        copy = copies.here(source, target)
        copy.start()
        saves.append(copy)

    def row_vector(index):
        pieces = []
        for group in range(groups):
            for k in range(width_rows):
                at = index * width_rows + k
                pieces.append(vec_float[group, at : at + 1])
        return jnp.concatenate(pieces, axis=1)

    width_rows = whole // groups // 128

    def normalise(half):
        gain_one, shift_one, gain_two, shift_two = [row_vector(index) for index in range(4)]

        @pl.loop(0, span // step_rows)
        def _(step):
            at = pl.ds(pl.multiple_of(half * span + step * step_rows, step_rows), step_rows)
            rows = x_all[at].astype(jnp.float32)
            mean = jnp.mean(rows, axis=-1, keepdims=True)
            centred = rows - mean
            inverse = lax.rsqrt(jnp.mean(centred * centred, axis=-1, keepdims=True) + norm_eps)
            unit = centred * inverse
            normed[at] = unit.astype(jnp.bfloat16)
            first[at] = (unit * gain_one + shift_one).astype(jnp.bfloat16)
            second[at] = (unit * gain_two + shift_two).astype(jnp.bfloat16)
            stats_out[0:1, at] = jnp.broadcast_to(mean, (step_rows, 128)).T[0:1]
            stats_out[1:2, at] = jnp.broadcast_to(inverse, (step_rows, 128)).T[0:1]

        for source, target in ((normed, normed_out), (first, first_out), (second, second_out)):
            save(source.at[aligned(half, span)], target.at[aligned(half, span)])

    seconds_x = second_half(0)
    start(swaps[1])
    relayed = [pass_on(0, firsts[0], c)]
    for copy in small:
        copy.wait_recv()
    for copy in stays:
        copy.wait()
    vec_float[...] = vec_all[...].astype(jnp.float32)
    save(vec_all, vec_out)
    firsts[0][1].wait_recv()
    own[0].wait()
    relayed[0].wait_recv()
    normalise(c)
    weights.relay(0, 0)
    weights.relay(0, 1)
    weights.start(1)
    relayed.append(pass_on(0, seconds_x, 1 - c))
    start(firsts[1][0])
    start(firsts[1][1])
    seconds_x[1].wait_recv()
    relayed[1].wait_recv()
    normalise(1 - c)
    weights.relay(0, 2)
    seconds_c = second_half(1)
    weights.relay(1, 0)
    weights.start(2)
    weights.arrive(0)
    save(widen_all, widen_out)
    hidden = widen_all.shape[1]

    def placed_vector(first_row, count):
        pieces = []
        for at in range(first_row, first_row + count):
            piece = vec_float[0, at : at + 1]
            for group in range(1, groups):
                piece = piece + vec_float[group, at : at + 1]
            pieces.append(piece)
        return jnp.concatenate(pieces, axis=1)

    bias = placed_vector(5 * width_rows, hidden // 128)
    columns = triple_all.shape[2]
    bias_row = 5 * width_rows + hidden // 128
    triple_bias = [placed_vector(bias_row + k * (columns // 128), columns // 128) for k in range(3)]
    head_size = heads.shape[2]

    def project(half):
        @pl.loop(0, span // step_rows)
        def _(step):
            at = pl.ds(pl.multiple_of(half * span + step * step_rows, step_rows), step_rows)
            cosine, sine = turn_all[0:half_rotary, at], turn_all[half_rotary : 2 * half_rotary, at]
            for k in range(3):
                block = jnp.dot(first[at], triple_all[k], preferred_element_type=jnp.float32) + triple_bias[k]
                block = block.T
                for head in range(columns // head_size):
                    part = block[head * head_size : (head + 1) * head_size]
                    if k < 2:
                        one, two = part[:half_rotary], part[half_rotary : 2 * half_rotary]
                        part = jnp.concatenate(
                            [one * cosine - two * sine, two * cosine + one * sine, part[2 * half_rotary :]], axis=0
                        )
                    heads[k, head, :, at] = part.astype(jnp.bfloat16)

    def widen(half):
        @pl.loop(0, span // step_rows)
        def _(step):
            at = pl.ds(pl.multiple_of(half * span + step * step_rows, step_rows), step_rows)
            widened = jnp.dot(second[at], widen_all[...], preferred_element_type=jnp.float32) + bias
            value, gradient = gelu_parts(widened)
            active[at] = value.astype(jnp.bfloat16)
            slope[at] = gradient.astype(jnp.bfloat16)

        save(active.at[aligned(half, span)], active_out.at[aligned(half, span)])
        save(slope.at[aligned(half, span)], slope_out.at[aligned(half, span)])

    widen(c)
    weights.relay(1, 1)
    relayed.append(pass_on(1, firsts[1], c))
    widen(1 - c)
    weights.relay(1, 2)
    for k in range(2):
        weights.relay(2, k)
    weights.arrive(1)
    save(triple_all, triple_out)
    position_swap.wait_recv()
    turn_swap.wait_recv()
    save(turn_all, turn_out)
    project(c)
    weights.relay(2, 2)
    relayed.append(pass_on(1, seconds_c, 1 - c))
    project(1 - c)
    save(heads, heads_out)
    weights.arrive(2)
    save(mixer_all, mixer_out)
    own[1].wait()
    firsts[1][1].wait_recv()
    seconds_c[1].wait_recv()
    for copy in relayed[2:]:
        copy.wait_recv()
    save(c_all, c_out)

    @pl.loop(0, length // step_rows)
    def _(step):
        at = pl.ds(pl.multiple_of(step * step_rows, step_rows), step_rows)
        mixed_grad[:, at] = lax.dot_general(
            mixer_all[...], c_all[at], (((1,), (1,)), ((), ())), preferred_element_type=jnp.float32
        ).astype(jnp.bfloat16)

    save(mixed_grad, mixed_grad_out)
    tile = min(256, hidden)
    for at in range(0, hidden, tile):
        narrow_grad[at : at + tile] = lax.dot_general(
            active[:, at : at + tile], c_all[...], (((0,), (0,)), ((), ())), preferred_element_type=jnp.float32
        ).astype(jnp.bfloat16)
    save(narrow_grad, narrow_out)

    sums_out[...] = jnp.zeros_like(sums_out)

    @pl.loop(0, length // step_rows)
    def _(step):
        at = pl.ds(pl.multiple_of(step * step_rows, step_rows), step_rows)
        sums_out[0:1] += jnp.sum(c_all[at].astype(jnp.float32), axis=0, keepdims=True)

    for copy in started:
        copy.wait_send()
    weights.finish()
    for copy in saves:
        copy.wait()


def front(groups, half_rotary, head_size, block_input, cotangent, positions, turns, widen_weight, triple_weight,
          mixer_weight, vectors):
    seqs, span, width = block_input.shape
    length, whole = seqs * span, width * 4
    hidden, columns = widen_weight.shape[1], triple_weight.shape[2]
    any_space = pl.BlockSpec(memory_space=pl.ANY)
    in_vmem = pl.BlockSpec(memory_space=pltpu.VMEM)
    bf16, f32 = jnp.bfloat16, jnp.float32
    vec_shape = (groups,) + vectors.shape
    triple_shape = (3, whole, columns)
    turn_shape = (turns.shape[1], length)
    heads_shape = (3, columns // head_size, head_size, length)
    shapes = [
        ((length, whole), bf16), (turn_shape, f32), ((whole, hidden), bf16), (triple_shape, bf16),
        ((columns, whole), bf16), (vec_shape, bf16), ((length, whole), bf16), ((length, whole), bf16),
        ((length, whole), bf16), ((length, hidden), bf16), ((length, hidden), bf16), ((hidden, whole), bf16),
        (heads_shape, bf16), ((columns, length), bf16),
    ]
    outs = [jax.ShapeDtypeStruct(*shape) for shape in shapes]
    return pl.pallas_call(
        functools.partial(front_kernel, groups, half_rotary),
        in_specs=[any_space] * 8,
        out_specs=[any_space] * 15 + [in_vmem] * 2,
        out_shape=outs[:1] + [jax.ShapeDtypeStruct(positions.shape, positions.dtype)] + outs[1:] + [
            jax.ShapeDtypeStruct((8, length), f32),
            jax.ShapeDtypeStruct((8, whole), f32),
        ],
        scratch_shapes=[pltpu.VMEM((length, whole), bf16)] + [pltpu.VMEM(*shape) for shape in shapes] + [
            pltpu.VMEM(vec_shape, f32),
        ] + sem_shapes(16 + 7 * (groups - 1), 32),
        compiler_params=pltpu.CompilerParams(
            collective_id=0, has_side_effects=True, vmem_limit_bytes=58 * 1024 * 1024
        ),
        name="front",
    )(block_input, cotangent, positions, turns, widen_weight, triple_weight, mixer_weight, vectors)


class Reduce:
    def __init__(self, groups, copies, arrays, outs, by_rows, owns, others, sums, inbox, done):
        self.groups, self.copies, self.arrays, self.outs, self.by_rows = groups, copies, arrays, outs, by_rows
        self.owns, self.others, self.sums, self.inbox, self.done = owns, others, sums, inbox, done
        self.z, self.c, self.t, _, _ = places(groups)
        self.y_peer = (self.z, 1 - self.c, self.t)
        beside, across, cross = line_peers()
        self.order = [beside, cross, across, self.z]
        self.targets = [beside, beside, across]
        self.loads, self.swaps, self.sends, self.backs, self.keeps = [], [], [], [], []

    def piece(self, a, group, half):
        array = self.arrays[a]
        if self.by_rows[a]:
            return array.at[aligned(group * 2 + half, array.shape[0] // (2 * self.groups))]
        return array.at[aligned(half, array.shape[0] // 2), aligned(group, array.shape[1] // self.groups)]

    def out_half(self, a, half):
        return self.outs[a].at[aligned(half, self.outs[a].shape[0] // 2)]

    def make(self):
        for a in range(len(self.arrays)):
            loads, swaps, sends = [], [], []
            for slot, group in enumerate(self.order):
                loads.append(self.copies.here(self.piece(a, group, self.c), self.owns[a].at[slot]))
                swaps.append(self.copies.remote(self.piece(a, group, 1 - self.c), self.others[a].at[slot], self.y_peer))
                if slot < 3:
                    sends.append(self.copies.remote(
                        self.sums[a].at[slot], self.inbox[a].at[slot], (self.targets[slot], self.c, self.t)))
            self.loads.append(loads)
            self.swaps.append(swaps)
            self.sends.append(sends)
            self.backs.append(self.copies.remote(self.done[a], self.out_half(a, self.c), self.y_peer))
            self.keeps.append(self.copies.here(self.done[a], self.out_half(a, self.c)))

    def start(self, a):
        for swap, load in zip(self.swaps[a], self.loads[a]):
            swap.start()
            load.start()

    def add(self, a, slot):
        self.loads[a][slot].wait()
        self.swaps[a][slot].wait_recv()
        total = self.owns[a][slot].astype(jnp.float32) + self.others[a][slot].astype(jnp.float32)
        if slot == 2:
            self.sends[a][1].wait_recv()
            total = total + self.inbox[a][1].astype(jnp.float32)
        self.sums[a][slot] = total.astype(jnp.bfloat16)
        if slot < 3:
            self.sends[a][slot].start()

    def total(self, a):
        total = self.sums[a][3].astype(jnp.float32)
        for slot in (0, 2):
            self.sends[a][slot].wait_recv()
            total = total + self.inbox[a][slot].astype(jnp.float32)
        self.done[a][...] = total.astype(jnp.bfloat16)
        self.backs[a].start()
        self.keeps[a].start()

    def finish(self):
        for a in range(len(self.arrays)):
            for swap in self.swaps[a]:
                swap.wait_send()
            for send in self.sends[a]:
                send.wait_send()
            self.backs[a].wait()
            self.keeps[a].wait()


def reduce_shapes(groups, shapes, by_rows):
    owns, others, sums, inbox, done, outs = [], [], [], [], [], []
    for (rows, columns), along in zip(shapes, by_rows):
        part = (rows // (2 * groups), columns) if along else (rows // 2, columns // groups)
        owns.append(pltpu.VMEM((groups,) + part, jnp.bfloat16))
        others.append(pltpu.VMEM((groups,) + part, jnp.bfloat16))
        sums.append(pltpu.VMEM((groups,) + part, jnp.bfloat16))
        inbox.append(pltpu.VMEM((groups - 1,) + part, jnp.bfloat16))
        done.append(pltpu.VMEM(part, jnp.bfloat16))
        outs.append(jax.ShapeDtypeStruct((2 * part[0], part[1]), jnp.bfloat16))
    return owns + others + sums + inbox + done, outs


def reduce_from(groups, copies, arrays, outs, by_rows, scratch):
    n = len(arrays)
    cut = [scratch[n * i : n * (i + 1)] for i in range(5)]
    made = Reduce(groups, copies, arrays, outs, by_rows, *cut)
    made.make()
    return made


def attend_sequence(block, scale, half_rotary, qkv_ref, grad_ref, hot_ref, turn_ref, back_ref, mixed_ref, bias_ref,
                    turned_all, mixed_all, queries, key_rows, value_rows, key_sum, value_sum):
    head_size, length = grad_ref.shape[1:]
    item = pl.program_id(0)
    f32, bf16 = jnp.float32, jnp.bfloat16
    hot = hot_ref[...]
    blank = jnp.zeros_like(hot)
    queries[...] = jnp.concatenate(
        [qkv_ref[0, 0].astype(f32) * scale, (1.0 - hot) * masked_score, blank], axis=0
    ).astype(bf16)
    key_rows[...] = jnp.concatenate([qkv_ref[1, 0].astype(f32), hot, blank], axis=0).T.astype(bf16)
    value_rows[...] = qkv_ref[2, 0].astype(f32).T.astype(bf16)
    keys, values, grads = qkv_ref.at[1, 0], qkv_ref.at[2, 0], grad_ref.at[0]
    last_dims = (((1,), (1,)), ((), ()))

    def unturn(grad, at):
        rounded = grad.astype(bf16).astype(f32)
        cosine, sine = turn_ref[0:half_rotary, at], turn_ref[half_rotary : 2 * half_rotary, at]
        one, two = rounded[:half_rotary], rounded[half_rotary : 2 * half_rotary]
        return jnp.concatenate(
            [one * cosine + two * sine, two * cosine - one * sine, rounded[2 * half_rotary :]], axis=0
        )

    query_bias = jnp.zeros((head_size, 1), f32)
    for start in range(0, length, block):
        count = start + block
        here = slice(start, count)
        scores = jnp.dot(key_rows[:count], queries[:, here], preferred_element_type=f32)
        key_index = lax.broadcasted_iota(jnp.int32, (block, block), 0)
        query_index = lax.broadcasted_iota(jnp.int32, (block, block), 1)
        last = jnp.where(key_index <= query_index, scores[start:], masked_score)
        scores = jnp.concatenate([scores[:start], last], axis=0) if start else last
        top = jnp.max(scores, axis=0, keepdims=True)
        raised = jnp.exp(scores - top)
        inverse = 1.0 / jnp.sum(raised, axis=0, keepdims=True)
        weights = raised.astype(bf16)
        mixed = (jnp.dot(values[:, :count], weights, preferred_element_type=f32) * inverse).astype(bf16)
        scaled = grads[:, here].astype(f32) * inverse
        delta = jnp.sum(mixed.astype(f32) * scaled, axis=0, keepdims=True)
        scaled = scaled.astype(bf16)
        prob_grads = jnp.dot(value_rows[:count], scaled, preferred_element_type=f32)
        score_grads = (raised * (prob_grads - delta)).astype(bf16)
        query_part = jnp.dot(keys[:, :count], score_grads, preferred_element_type=f32)
        key_part = lax.dot_general(queries[:head_size, here], score_grads, last_dims, preferred_element_type=f32)
        value_part = lax.dot_general(scaled, weights, last_dims, preferred_element_type=f32)
        if start:
            key_sum[:, :start] += key_part[:, :start]
            value_sum[:, :start] += value_part[:, :start]
        key_sum[:, here] = key_part[:, start:]
        value_sum[:, here] = value_part[:, start:]
        mixed_ref[0, :, here] = mixed
        mixed_all[item, :, here] = mixed
        turned = unturn(query_part * scale, here)
        query_bias = query_bias + jnp.sum(turned, axis=1, keepdims=True)
        back_ref[0, 0, :, here] = turned.astype(bf16)
        turned_all[0, item, :, here] = turned.astype(bf16)
    turned = unturn(key_sum[...], slice(0, length))
    back_ref[1, 0] = turned.astype(bf16)
    turned_all[1, item] = turned.astype(bf16)
    rounded = value_sum[...].astype(bf16)
    back_ref[2, 0] = rounded
    turned_all[2, item] = rounded
    bias_ref[0, 0] = jnp.broadcast_to(query_bias, (head_size, 128))
    bias_ref[1, 0] = jnp.broadcast_to(jnp.sum(turned, axis=1, keepdims=True), (head_size, 128))
    bias_ref[2, 0] = jnp.broadcast_to(jnp.sum(rounded.astype(f32), axis=1, keepdims=True), (head_size, 128))


def attend_reduce_kernel(block, scale, half_rotary, groups, items, qkv_ref, grad_ref, hot_ref, turn_ref, grads_in,
                         shard_in, first_in, c_in, back_ref, mixed_ref, bias_ref, triple_grad, mixer_grad, grads_out,
                         whole_out, *refs):
    first, c_all, refs = refs[0], refs[1], refs[2:]
    attention, refs = refs[:7], refs[7:]
    scratch, (send, recv, local) = refs[:-3], refs[-3:]
    item = pl.program_id(0)
    copies = Copies(send, recv, local)
    reduce = reduce_from(groups, copies, (grads_in,), (grads_out,), (False,), scratch)
    weights = Spread(groups, copies, (shard_in,), (whole_out,), (False,), (True,))
    rows_loads = [copies.here(first_in, first), copies.here(c_in, c_all)]
    plan = [[] for _ in range(items + 1)]
    for slot in range(groups):
        plan[min(items, max(1, slot))].append(functools.partial(reduce.add, 0, slot))
    for k in range(groups - 1):
        plan[min(items, 1 + k)].append(functools.partial(weights.relay, 0, k))
    plan[items].append(functools.partial(reduce.total, 0))

    def run(actions):
        for action in actions:
            action()

    def begin():
        z, c, t, _, _ = places(groups)
        greet([(z, 1 - c, t)] + [(lax.rem(z + k, groups), c, t) for k in range(1, groups)])
        reduce.start(0)
        weights.start(0)
        for load in rows_loads:
            load.start()

    pl.when(item == 0)(begin)
    for i in range(1, items):
        if plan[i]:
            pl.when(item == i)(functools.partial(run, plan[i]))

    attend_sequence(block, scale, half_rotary, qkv_ref, grad_ref, hot_ref, turn_ref, back_ref, mixed_ref, bias_ref,
                    *attention)

    def end():
        run(plan[items])
        for load in rows_loads:
            load.wait()
        turned_all, mixed_all = attention[:2]
        columns = mixed_all.shape[0] * mixed_all.shape[1]
        for k in range(3):
            triple_grad[k * columns : (k + 1) * columns] = jnp.dot(
                turned_all[k].reshape(columns, -1), first[...], preferred_element_type=jnp.float32
            ).astype(jnp.bfloat16)
        mixer_grad[...] = jnp.dot(
            mixed_all[...].reshape(columns, -1), c_all[...], preferred_element_type=jnp.float32
        ).astype(jnp.bfloat16)
        reduce.finish()
        weights.arrive(0)
        weights.finish()

    pl.when(item == items - 1)(end)


def attend_reduce(heads, grad_heads, hot, turns, scale, half_rotary, groups, narrow_grad, narrow_weight, first, c_rows):
    _, items, head_size, length = heads.shape
    block = min(512, length)
    bf16, f32 = jnp.bfloat16, jnp.float32
    deep = head_size + 2 * hot.shape[0]
    whole = first.shape[1]
    grads = [(3 * items * head_size, whole), (items * head_size, whole)]
    shapes, outs = reduce_shapes(groups, [narrow_grad.shape], (False,))
    any_space = pl.BlockSpec(memory_space=pl.ANY)
    return pl.pallas_call(
        functools.partial(attend_reduce_kernel, block, scale, half_rotary, groups, items),
        grid=(items,),
        in_specs=[
            pl.BlockSpec((3, 1, head_size, length), lambda i: (0, i, 0, 0)),
            pl.BlockSpec((1, head_size, length), lambda i: (i, 0, 0)),
            pl.BlockSpec(hot.shape, lambda i: (0, 0)),
            pl.BlockSpec(turns.shape, lambda i: (0, 0)),
            any_space,
            any_space,
            any_space,
            any_space,
        ],
        out_specs=[
            pl.BlockSpec((3, 1, head_size, length), lambda i: (0, i, 0, 0)),
            pl.BlockSpec((1, head_size, length), lambda i: (i, 0, 0)),
            pl.BlockSpec((3, 1, head_size, 128), lambda i: (0, i, 0, 0)),
            pl.BlockSpec(grads[0], lambda i: (0, 0)),
            pl.BlockSpec(grads[1], lambda i: (0, 0)),
            any_space,
            any_space,
        ],
        out_shape=[
            jax.ShapeDtypeStruct(heads.shape, bf16),
            jax.ShapeDtypeStruct(grad_heads.shape, bf16),
            jax.ShapeDtypeStruct((3, items, head_size, 128), f32),
            jax.ShapeDtypeStruct(grads[0], bf16),
            jax.ShapeDtypeStruct(grads[1], bf16),
        ] + outs + [
            jax.ShapeDtypeStruct((narrow_weight.shape[0], narrow_weight.shape[1] * groups), bf16)
        ],
        scratch_shapes=[
            pltpu.VMEM(first.shape, bf16),
            pltpu.VMEM(c_rows.shape, bf16),
            pltpu.VMEM(heads.shape, bf16),
            pltpu.VMEM(grad_heads.shape, bf16),
            pltpu.VMEM((deep, length), bf16),
            pltpu.VMEM((length, deep), bf16),
            pltpu.VMEM((length, head_size), bf16),
            pltpu.VMEM((head_size, length), f32),
            pltpu.VMEM((head_size, length), f32),
        ] + shapes + sem_shapes(2 * groups + 2 * (groups - 1), groups + 4),
        compiler_params=pltpu.CompilerParams(
            collective_id=1, has_side_effects=True, vmem_limit_bytes=62 * 1024 * 1024
        ),
        cost_estimate=pl.CostEstimate(
            flops=7 * items * length * length * 256,
            bytes_accessed=4 * heads.size,
            transcendentals=items * length * length // 2,
        ),
        name="attend_reduce",
    )(heads, grad_heads, hot, turns, narrow_grad, narrow_weight, first, c_rows)


class ReduceWhole:
    def __init__(self, groups, copies, arrays, outs, by_rows, scratch):
        z, c, t, _, _ = places(groups)
        n = len(arrays)
        self.groups, self.outs = groups, outs
        self.owns, self.inbox, self.theirs = [scratch[n * i : n * (i + 1)] for i in range(3)]
        self.loads, self.sends, self.swaps = [], [], []
        beside, across, cross = line_peers()

        def piece(a, group):
            array = arrays[a]
            if by_rows[a]:
                return array.at[aligned(group, array.shape[0] // groups)]
            return array.at[:, aligned(group, array.shape[1] // groups)]

        for a in range(n):
            self.loads.append([copies.here(piece(a, group), self.owns[a].at[k]) for k, group in enumerate((z, across))])
            self.sends.append([
                copies.remote(piece(a, cross), self.inbox[a].at[0], (beside, c, t)),
                copies.remote(piece(a, beside), self.inbox[a].at[1], (beside, c, t)),
                copies.remote(self.owns[a].at[1], self.inbox[a].at[2], (across, c, t)),
            ])
            self.swaps.append(copies.remote(self.owns[a].at[0], self.theirs[a], (z, 1 - c, t)))

    def start(self):
        for loads, sends in zip(self.loads, self.sends):
            sends[0].start()
            loads[1].start()
        for loads, sends in zip(self.loads, self.sends):
            sends[1].start()
            loads[0].start()

    def middle(self):
        for a, sends in enumerate(self.sends):
            self.loads[a][1].wait()
            sends[0].wait_recv()
            total = self.owns[a][1].astype(jnp.float32) + self.inbox[a][0].astype(jnp.float32)
            self.owns[a][1] = total.astype(jnp.bfloat16)
            sends[2].start()

    def total(self):
        for a, sends in enumerate(self.sends):
            self.loads[a][0].wait()
            total = self.owns[a][0].astype(jnp.float32)
            for k in (1, 2):
                sends[k].wait_recv()
                total = total + self.inbox[a][k].astype(jnp.float32)
            self.owns[a][0] = total.astype(jnp.bfloat16)
            self.swaps[a].start()

    def finish(self):
        for a, swap in enumerate(self.swaps):
            swap.wait()
            total = self.owns[a][0].astype(jnp.float32) + self.theirs[a][...].astype(jnp.float32)
            if len(self.outs[a].shape) == 3:
                rows = total.shape[0] // 3
                for k in range(3):
                    self.outs[a][k] = total[k * rows : (k + 1) * rows].T
            else:
                self.outs[a][...] = total
            for send in self.sends[a]:
                send.wait_send()


def reduce_whole_shapes(groups, shapes, by_rows):
    parts = [(rows // groups, columns) if along else (rows, columns // groups)
             for (rows, columns), along in zip(shapes, by_rows)]
    scratch = [pltpu.VMEM((2,) + part, jnp.bfloat16) for part in parts]
    scratch += [pltpu.VMEM((3,) + part, jnp.bfloat16) for part in parts]
    scratch += [pltpu.VMEM(part, jnp.bfloat16) for part in parts]
    return scratch, [jax.ShapeDtypeStruct(part, jnp.float32) for part in parts]


def back_kernel(groups, turned_in, mixed_in, c_in, mixer_in, active_in, narrow_in, slope_in, second_in,
                triple_in, widen_in, normed_in, gains, norm_stats, front_sums, triple_bias_in,
                triple_grad, mixer_grad,
                out_ref, grad_ref, stats_out, widen_share, wide_out, bias_out, triple_share, mixer_share,
                turned, mixed, c_all, mixer, active, narrow, hidden, second, triple, widen, normed,
                out_part, grad_part, near_box, far_box, widen_grad, wide_sum, bias_sum,
                row_box, row_sum, wide_box, wide_two, wide_three, bias_two, bias_three, *refs):
    scratch, (send, recv, local) = refs[:-3], refs[-3:]
    z, c, t, near, far = places(groups)
    copies = Copies(send, recv, local)
    y_peer = (z, 1 - c, t)
    near_peer, far_peer, cross_peer = (z, c, near), (z, c, far), (z, c, 3 - t)
    ring = [lax.rem(z + k, groups) for k in range(1, groups)]
    span, width = out_ref.shape[1:]
    length, whole = c_all.shape
    quarter = span // 2
    step_rows = min(256, quarter)
    f32, bf16 = jnp.float32, jnp.bfloat16
    loads = []
    for source, target in (
        (mixed_in, mixed), (mixer_in, mixer), (active_in, active), (narrow_in, narrow), (c_in, c_all),
        (slope_in, hidden), (second_in, second), (turned_in, turned), (triple_in, triple), (widen_in, widen),
        (normed_in, normed),
    ):
        load = copies.here(source, target)
        load.start()
        loads.append(load)
    greet([y_peer, near_peer, far_peer, cross_peer] + [(peer, c, t) for peer in ring])
    started, finals, keeps = [], [], []

    def start(copy):
        copy.start()
        started.append(copy)
        return copy

    whole_scratch, half_scratch = scratch[:6], scratch[6:]
    attention_sums = ReduceWhole(
        groups, copies, (triple_grad, mixer_grad), (triple_share, mixer_share), (False, False), whole_scratch
    )
    widen_sums = reduce_from(groups, copies, (widen_grad,), (widen_share,), (True,), half_scratch)
    parts = (out_part, grad_part)
    halves = (1 - c, c)
    nears = [[], []]
    fars = [[], []]

    def send_near(index, turn):
        rows = aligned(halves[turn], span)
        part = parts[index]
        nears[index].append([
            start(copies.remote(
                part.at[rows, aligned(3 - t, width)], near_box.at[index, 0, rows], near_peer)),
            start(copies.remote(
                part.at[rows, aligned(near, width)], near_box.at[index, 1, rows], near_peer)),
        ])

    def rows_of(turn, step):
        return pl.ds(pl.multiple_of(halves[turn] * span + step * quarter, quarter), quarter)

    def send_far(index, turn):
        nears[index][turn][0].wait_recv()
        part = parts[index]
        for step in range(2):
            rows = rows_of(turn, step)
            total = part[rows, aligned(far, width)].astype(f32) + near_box[index, 0, rows].astype(f32)
            part[rows, aligned(far, width)] = total.astype(bf16)
            fars[index].append(start(copies.remote(
                part.at[rows, aligned(far, width)], far_box.at[index, rows], far_peer)))

    def close(index, turn, target):
        nears[index][turn][1].wait_recv()
        part = parts[index]
        for step in range(2):
            rows = rows_of(turn, step)
            fars[index][2 * turn + step].wait_recv()
            done = part.at[rows, aligned(t, width)]
            total = (
                part[rows, aligned(t, width)].astype(f32)
                + near_box[index, 1, rows].astype(f32)
                + far_box[index, rows].astype(f32)
            )
            part[rows, aligned(t, width)] = total.astype(bf16)
            place = target.at[c, pl.ds(step * quarter, quarter)]
            if turn == 0:
                finals.append(start(copies.remote(done, place, y_peer)))
            else:
                keep = copies.here(done, place)
                keep.start()
                keeps.append(keep)

    def loop(turn, body):
        @pl.loop(0, span // step_rows)
        def _(step):
            body(pl.ds(pl.multiple_of(halves[turn] * span + step * step_rows, step_rows), step_rows))

    attention_sums.start()
    columns = mixer.shape[0]
    for load in loads[:4]:
        load.wait()

    def branches(at):
        total = lax.dot_general(mixed[:, at], mixer[...], (((0,), (0,)), ((), ())), preferred_element_type=f32)
        total = total + jnp.dot(active[at], narrow[...], preferred_element_type=f32)
        out_part[at] = total.astype(bf16)

    for turn in range(2):
        loop(turn, branches)
        send_near(0, turn)
    for load in loads[4:6]:
        load.wait()
    bias_sum[...] = jnp.zeros_like(bias_sum)
    bias_sum[1:2] = triple_bias_in[...]

    def hidden_grads(at):
        grads = lax.dot_general(c_all[at], narrow[...], (((1,), (1,)), ((), ())), preferred_element_type=f32)
        grads = grads * hidden[at].astype(f32)
        bias_sum[0:1] += jnp.sum(grads, axis=0, keepdims=True)
        hidden[at] = grads.astype(bf16)

    loop(0, hidden_grads)
    send_far(0, 0)
    loop(1, hidden_grads)
    send_far(0, 1)
    loads[6].wait()
    depth = widen_grad.shape[0]
    tile = min(256, depth)
    for at in range(0, depth, tile):
        widen_grad[at : at + tile] = lax.dot_general(
            second[:, at : at + tile], hidden[...], (((0,), (0,)), ((), ())), preferred_element_type=f32
        ).astype(bf16)
    widen_sums.start(0)
    attention_sums.middle()
    bias_two[c] = bias_sum[...]
    bias_swap = start(copies.remote(bias_two.at[c], bias_two.at[c], y_peer))
    for load in loads[7:]:
        load.wait()
    wide_sum[...] = front_sums[...]
    gain_one, gain_two = gains[0:1], gains[1:2]

    def norm_grads(at):
        unit = normed[at].astype(f32)
        one = sum(
            lax.dot_general(turned[k * columns : (k + 1) * columns, at], triple[k], (((0,), (1,)), ((), ())),
                            preferred_element_type=f32)
            for k in range(3)
        )
        wide_sum[0:1] += jnp.sum(one * unit, axis=0, keepdims=True)
        wide_sum[1:2] += jnp.sum(one, axis=0, keepdims=True)
        two = lax.dot_general(hidden[at], widen[...], (((1,), (1,)), ((), ())), preferred_element_type=f32)
        wide_sum[2:3] += jnp.sum(two * unit, axis=0, keepdims=True)
        wide_sum[3:4] += jnp.sum(two, axis=0, keepdims=True)
        scaled = one * gain_one + two * gain_two
        grad_part[at] = scaled.astype(bf16)
        rows = scaled.shape[0]
        total = jnp.sum(scaled, axis=-1, keepdims=True) * (1.0 / whole)
        along = jnp.sum(scaled * unit, axis=-1, keepdims=True) * (1.0 / whole)
        row_box[t, 0:1, at] = jnp.broadcast_to(total, (rows, 128)).T[0:1]
        row_box[t, 1:2, at] = jnp.broadcast_to(along, (rows, 128)).T[0:1]

    loop(0, norm_grads)
    send_near(1, 0)
    loop(1, norm_grads)
    send_near(1, 1)
    wide_box[t] = wide_sum[...]
    tp_peers = [(t + k) - 4 * ((t + k) // 4) for k in range(1, 4)]
    tp_sent = [start(copies.remote(row_box.at[t], row_box.at[t], (z, c, peer))) for peer in tp_peers]
    tp_sent += [start(copies.remote(wide_box.at[t], wide_box.at[t], (z, c, peer))) for peer in tp_peers]
    send_far(1, 0)
    widen_sums.add(0, 0)
    close(0, 0, out_ref)
    send_far(1, 1)
    for slot in range(1, groups):
        widen_sums.add(0, slot)
    attention_sums.total()
    close(0, 1, out_ref)
    for copy in tp_sent:
        copy.wait_recv()
    row_sum[0:2] = row_box[0] + row_box[1] + row_box[2] + row_box[3]
    row_sum[2:4] = norm_stats[0:2]
    finals.append(start(copies.remote(row_sum.at[:, aligned(1 - c, span)], stats_out.at[c], y_peer)))
    keeps.append(copies.here(row_sum.at[:, aligned(c, span)], stats_out.at[c]))
    keeps[-1].start()
    wide_two[c] = wide_box[0] + wide_box[1] + wide_box[2] + wide_box[3]
    wide_swap = start(copies.remote(wide_two.at[c], wide_two.at[c], y_peer))
    bias_swap.wait_recv()
    bias_three[z] = bias_two[0] + bias_two[1]
    sums_sent = [start(copies.remote(bias_three.at[z], bias_three.at[z], (peer, c, t))) for peer in ring]
    wide_swap.wait_recv()
    wide_three[z] = wide_two[0] + wide_two[1]
    sums_sent += [start(copies.remote(wide_three.at[z], wide_three.at[z], (peer, c, t))) for peer in ring]
    close(1, 0, grad_ref)
    for copy in sums_sent:
        copy.wait_recv()
    bias_total, wide_total = bias_three[0], wide_three[0]
    for group in range(1, groups):
        bias_total = bias_total + bias_three[group]
        wide_total = wide_total + wide_three[group]
    bias_out[...] = bias_total
    wide_out[...] = wide_total
    widen_sums.total(0)
    close(1, 1, grad_ref)
    attention_sums.finish()
    for copy in finals:
        copy.wait_recv()
    for copy in started:
        copy.wait_send()
    for copy in keeps:
        copy.wait()
    widen_sums.finish()


def back(groups, turned, mixed, c_rows, mixer_weight, active, narrow_weight, slope, second, triple_weight,
         widen_weight, normed, gains, norm_stats, front_sums, triple_bias_row,
         triple_grad, mixer_grad):
    length, whole = c_rows.shape
    hidden = active.shape[1]
    width, span = whole // 4, length // 2
    columns = mixed.shape[0]
    any_space = pl.BlockSpec(memory_space=pl.ANY)
    in_vmem = pl.BlockSpec(memory_space=pltpu.VMEM)
    bf16, f32 = jnp.bfloat16, jnp.float32
    grads = [(3 * columns, whole), (columns, whole)]
    whole_scratch, whole_outs = reduce_whole_shapes(groups, grads, (False, False))
    whole_outs[0] = jax.ShapeDtypeStruct((3, whole // groups, columns), f32)
    half_scratch, half_outs = reduce_shapes(groups, [(whole, hidden)], (True,))
    residents = (turned, mixed, c_rows, mixer_weight, active, narrow_weight, slope, second, triple_weight,
                 widen_weight, normed)
    wide, bias = (8, whole), (8, max(hidden, triple_bias_row.shape[1]))
    return pl.pallas_call(
        functools.partial(back_kernel, groups),
        in_specs=[any_space] * 11 + [in_vmem] * 4 + [any_space] * 2,
        out_specs=[any_space] * 4 + [in_vmem] * 4,
        out_shape=[
            jax.ShapeDtypeStruct((2, span, width), bf16),
            jax.ShapeDtypeStruct((2, span, width), bf16),
            jax.ShapeDtypeStruct((2, 4, span), f32),
        ] + half_outs + [
            jax.ShapeDtypeStruct(wide, f32),
            jax.ShapeDtypeStruct(bias, f32),
        ] + whole_outs,
        scratch_shapes=[pltpu.VMEM(array.shape, bf16) for array in residents] + [
            pltpu.VMEM((length, whole), bf16),
            pltpu.VMEM((length, whole), bf16),
            pltpu.VMEM((2, 2, length, width), bf16),
            pltpu.VMEM((2, length, width), bf16),
            pltpu.VMEM((whole, hidden), bf16),
            pltpu.VMEM(wide, f32),
            pltpu.VMEM(bias, f32),
            pltpu.VMEM((4, 2, length), f32),
            pltpu.VMEM((4, length), f32),
            pltpu.VMEM((4,) + wide, f32),
            pltpu.VMEM((2,) + wide, f32),
            pltpu.VMEM((groups,) + wide, f32),
            pltpu.VMEM((2,) + bias, f32),
            pltpu.VMEM((groups,) + bias, f32),
        ] + whole_scratch + half_scratch + sem_shapes(
            32 + 2 * (groups - 1) + 2 * groups + 2 * groups, 20 + groups + 3),
        compiler_params=pltpu.CompilerParams(
            collective_id=2, has_side_effects=True, vmem_limit_bytes=62 * 1024 * 1024
        ),
        name="back",
    )(*residents, gains, norm_stats, front_sums, triple_bias_row, triple_grad, mixer_grad)


def shards_sequence(
    block_input,
    positions,
    first_gain,
    first_shift,
    second_gain,
    second_shift,
    triple_weight,
    triple_bias,
    mixer_weight,
    output_bias,
    widen_weight,
    widen_bias,
    narrow_weight,
    cotangent,
):
    seqs, span, local_width = block_input.shape
    length = seqs * span
    groups = lax.axis_size("fsdp")
    hidden_rows, hidden_part = widen_bias.shape
    heads_local, bias_part = triple_bias.shape[1:]
    head_size = bias_part * groups
    place = lax.axis_index("fsdp")
    here = jnp.arange(groups) == place
    placed_widen = jnp.where(here[None, :, None], widen_bias[:, None, :], 0)
    placed_triple = jnp.where(here[None, None, :, None], triple_bias[:, :, None, :], 0)
    vectors = (first_gain, first_shift, second_gain, second_shift, output_bias)
    index = jnp.arange(len(vectors), dtype=jnp.int32)[:, None, None]
    stacked = sum(
        jnp.where(index == at, vector.reshape(1, -1, 128), 0) for at, vector in enumerate(vectors)
    ).reshape(-1, 128)
    count = stacked.shape[0] + (placed_widen.size + placed_triple.size) // 128
    packed = jnp.concatenate([
        stacked, placed_widen.reshape(-1, 128), placed_triple.reshape(-1, 128),
        jnp.zeros((-count % 16, 128), jnp.bfloat16),
    ])
    cosine, sine = rotary_tables(positions, ROT)
    turns = jnp.concatenate([cosine[:, 0, 0], sine[:, 0, 0]], axis=1)
    (cot_rows, places_out, turn_rows, weight_widen, weight_triple, weight_mixer, small, normed_rows, first_rows,
     second_rows, activated, slope, narrow_grad, heads, mixed_grad, norm_stats, front_sums) = front(
        groups, ROT // 2, head_size, block_input, cotangent, positions.reshape(seqs, span // 128, 128), turns,
        widen_weight, jnp.transpose(triple_weight, (1, 0, 2)), mixer_weight, packed,
    )
    width = weight_widen.shape[0]
    small = small.reshape(groups, -1)
    vector_size = first_gain.shape[0]
    gain_one, _, gain_two, _, bias_output = [
        small[:, at * vector_size : (at + 1) * vector_size].astype(jnp.float32).reshape(-1) for at in range(5)
    ]
    begun = (places_out.reshape(length // 128, 128) == 0).astype(jnp.float32)
    lanes, token_rows = jnp.arange(128), jnp.arange(length // 128)
    count = jnp.dot(begun, (lanes[:, None] <= lanes[None, :]).astype(jnp.float32))
    before = jnp.dot((token_rows[None, :] < token_rows[:, None]).astype(jnp.float32), begun)
    documents = (count + jnp.sum(before, axis=1, keepdims=True)).reshape(1, length) - 1.0
    hot = (documents == jnp.arange(8, dtype=jnp.float32)[:, None]).astype(jnp.float32)
    turned_back, mixed, bias_lanes, triple_grad, mixer_grad, narrow_share, weight_narrow = attend_reduce(
        heads, mixed_grad.reshape(heads_local, head_size, length), hot, turn_rows, head_size ** (-0.5), ROT // 2,
        groups, narrow_grad, narrow_weight, first_rows, cot_rows,
    )
    row = bias_lanes[..., 0].reshape(1, -1)
    bias_width = max(activated.shape[1], row.shape[1])
    row = jnp.pad(row, ((0, 0), (0, bias_width - row.shape[1])))
    zero = jnp.zeros((width,), jnp.float32)
    first_sums = jnp.stack(
        [zero] * 4 + [jnp.where(lax.axis_index("tp") == 0, front_sums[0], 0.0)] + [zero] * 3
    )
    summed, scattered, row_stats, widen_share, wide_sums, bias_sums, triple_share, mixer_share = back(
        groups, turned_back.reshape(-1, length), mixed.reshape(-1, length), cot_rows, weight_mixer, activated,
        weight_narrow, slope, second_rows, weight_triple, weight_widen, normed_rows, jnp.stack([gain_one, gain_two]),
        norm_stats, first_sums, row, triple_grad, mixer_grad,
    )
    feature_start = lax.axis_index("tp") * local_width
    bias_slice = lax.dynamic_slice_in_dim(bias_output, feature_start, local_width, 0)
    own_rows = block_input.astype(jnp.float32)
    block_output = (own_rows + summed.astype(jnp.float32) + bias_slice).astype(jnp.bfloat16)
    own_normed = (own_rows - row_stats[:, 2, :, None]) * row_stats[:, 3, :, None]
    input_grad = (
        cotangent.astype(jnp.float32)
        + row_stats[:, 3, :, None]
        * (scattered.astype(jnp.float32) - row_stats[:, 0, :, None] - own_normed * row_stats[:, 1, :, None])
    ).astype(jnp.bfloat16)
    wide_sums = lax.dynamic_slice_in_dim(wide_sums, place * vector_size, vector_size, 1)
    triple_bias_out = lax.dynamic_slice_in_dim(
        bias_sums[1, : 3 * heads_local * head_size].reshape(3, heads_local, head_size),
        place * triple_bias.shape[2],
        triple_bias.shape[2],
        2,
    )
    widen_bias_out = lax.dynamic_slice_in_dim(
        bias_sums[0, : activated.shape[1]].reshape(hidden_rows, -1), place * hidden_part, hidden_part, 1
    )
    return (
        block_output,
        input_grad,
        wide_sums[0],
        wide_sums[1],
        wide_sums[2],
        wide_sums[3],
        jnp.transpose(triple_share, (1, 0, 2)),
        triple_bias_out,
        mixer_share,
        wide_sums[4],
        widen_share.astype(jnp.float32),
        widen_bias_out,
        narrow_share.astype(jnp.float32),
    )


def shards(block_input, *others):
    seqs = block_input.shape[0]
    if seqs == 2 and lax.axis_size("ctx") == 2 and lax.axis_size("tp") == 4 and lax.axis_size("fsdp") == 4:
        return shards_sequence(block_input, *others)
    return shards_general(block_input, *others)


def solution(mesh):
    in_specs = (
        P("fsdp", "ctx", "tp"),
        P("fsdp", "ctx"),
        P("fsdp"),
        P("fsdp"),
        P("fsdp"),
        P("fsdp"),
        P("fsdp", None, "tp"),
        P(None, "tp", "fsdp"),
        P("tp", "fsdp"),
        P("fsdp"),
        P("fsdp", "tp"),
        P("tp", "fsdp"),
        P("tp", "fsdp"),
        P("fsdp", "ctx", "tp"),
    )
    out_specs = (
        P("fsdp", "ctx", "tp"),
        P("fsdp", "ctx", "tp"),
        P("fsdp"),
        P("fsdp"),
        P("fsdp"),
        P("fsdp"),
        P("fsdp", None, "tp"),
        P(None, "tp", "fsdp"),
        P("tp", "fsdp"),
        P("fsdp"),
        P("fsdp", "tp"),
        P("tp", "fsdp"),
        P("tp", "fsdp"),
    )
    return jax.shard_map(shards, mesh=mesh, in_specs=in_specs, out_specs=out_specs, check_vma=False)
```

```python
import functools
import math

import jax
import jax.numpy as jnp
from jax import lax
from jax.experimental import pallas as pl
from jax.experimental.pallas import tpu as pltpu
from jax.sharding import PartitionSpec as P

ROT = 16


norm_eps = 1e-05
masked_score = -1e30


def normalize(rows):
    centred = rows - jnp.mean(rows, axis=-1, keepdims=True)
    inverse = lax.rsqrt(jnp.mean(centred * centred, axis=-1, keepdims=True) + norm_eps)
    return (centred * inverse, inverse)


def gelu_parts(widened):
    cumulative = 0.5 * (1.0 + lax.erf(widened * (1.0 / math.sqrt(2.0))))
    density = jnp.exp(-0.5 * widened * widened) * (1.0 / math.sqrt(2.0 * math.pi))
    return (widened * cumulative, cumulative + widened * density)


def rotary_tables(positions, rotary):
    half = rotary // 2
    freqs = jnp.exp(jnp.arange(half, dtype=jnp.float32) * (-2.0 * math.log(10000.0) / rotary))
    angles = positions.astype(jnp.float32)[:, None, :] * freqs[None, :, None]
    return (jnp.cos(angles)[:, None, None], jnp.sin(angles)[:, None, None])


def rotate_forward(block, cosine, sine, half):
    first = block[..., :half, :]
    second = block[..., half : 2 * half, :]
    return jnp.concatenate(
        [first * cosine - second * sine, second * cosine + first * sine, block[..., 2 * half :, :]],
        axis=-2,
    )


def rotate_back(block, cosine, sine, half):
    first = block[..., :half, :]
    second = block[..., half : 2 * half, :]
    return jnp.concatenate(
        [first * cosine + second * sine, second * cosine - first * sine, block[..., 2 * half :, :]],
        axis=-2,
    )


def attend_kernel(block, scale, qkv_ref, grad_ref, base_ref, back_ref, mixed_ref,
                  queries, query_rows, keys, key_rows, values, value_rows, grads, grad_rows,
                  base_rows, key_sum, value_sum):
    parts, head_size, span = grad_ref.shape[0], grad_ref.shape[2], grad_ref.shape[3]
    length = parts * span
    for part in range(parts):
        at = pl.ds(part * span, span)
        queries[:, at] = (qkv_ref[part, 0, 0].astype(jnp.float32) * scale).astype(jnp.bfloat16)
        keys[:, at] = qkv_ref[part, 0, 1]
        values[:, at] = qkv_ref[part, 0, 2]
        grads[:, at] = grad_ref[part, 0]
    for source, target in (
        (queries, query_rows),
        (keys, key_rows),
        (values, value_rows),
        (grads, grad_rows),
    ):
        target[...] = source[...].astype(jnp.float32).T.astype(jnp.bfloat16)
    base_row = base_ref[0]
    base_rows[...] = jnp.broadcast_to(base_row, (128, length)).T
    for start in range(0, length, block):
        count = start + block
        here = slice(start, count)
        scores = jnp.dot(key_rows[:count], queries[:, here], preferred_element_type=jnp.float32)
        wide_base = jnp.concatenate([base_rows[:count]] * (block // 128), axis=1)
        same = wide_base == base_row[:, here]
        key_index = lax.broadcasted_iota(jnp.int32, (block, block), 0)
        query_index = lax.broadcasted_iota(jnp.int32, (block, block), 1)
        last = jnp.where(
            same[start:] & (key_index <= query_index), scores[start:], masked_score
        )
        if start:
            earlier = jnp.where(same[:start], scores[:start], masked_score)
            scores = jnp.concatenate([earlier, last], axis=0)
        else:
            scores = last
        top = jnp.max(scores, axis=0, keepdims=True)
        raised = jnp.exp(scores - top)
        probs = raised * (1.0 / jnp.sum(raised, axis=0, keepdims=True))
        weights = probs.astype(jnp.bfloat16)
        mixed = jnp.dot(values[:, :count], weights, preferred_element_type=jnp.float32).astype(
            jnp.bfloat16
        )
        grad_block = grads[:, here]
        delta = jnp.sum(
            mixed.astype(jnp.float32) * grad_block.astype(jnp.float32), axis=0, keepdims=True
        )
        prob_grads = jnp.dot(value_rows[:count], grad_block, preferred_element_type=jnp.float32)
        score_grads = (probs * (prob_grads - delta)).astype(jnp.bfloat16)
        query_part = jnp.dot(keys[:, :count], score_grads, preferred_element_type=jnp.float32)
        key_part = jnp.dot(score_grads, query_rows[here], preferred_element_type=jnp.float32)
        value_part = jnp.dot(weights, grad_rows[here], preferred_element_type=jnp.float32)
        if start:
            key_sum[:start] += key_part[:start]
            value_sum[:start] += value_part[:start]
        key_sum[here] = key_part[start:]
        value_sum[here] = value_part[start:]
        part, inside = start // span, start % span
        mixed_ref[part, 0, :, inside : inside + block] = mixed
        back_ref[part, 0, 0, :, inside : inside + block] = (query_part * scale).astype(jnp.bfloat16)
    for part in range(parts):
        at = pl.ds(part * span, span)
        back_ref[part, 0, 1] = key_sum[at].T.astype(jnp.bfloat16)
        back_ref[part, 0, 2] = value_sum[at].T.astype(jnp.bfloat16)


def attend(by_heads, grad_heads, item_base, scale):
    parts, items, unused, head_size, span = by_heads.shape
    length = parts * span
    block = min(256, span)
    wide = pltpu.VMEM((head_size, length), jnp.bfloat16)
    tall = pltpu.VMEM((length, head_size), jnp.bfloat16)
    total = pltpu.VMEM((length, head_size), jnp.float32)
    return pl.pallas_call(
        functools.partial(attend_kernel, block, scale),
        grid=(items,),
        in_specs=[
            pl.BlockSpec((parts, 1, 3, head_size, span), lambda i: (0, i, 0, 0, 0)),
            pl.BlockSpec((parts, 1, head_size, span), lambda i: (0, i, 0, 0)),
            pl.BlockSpec((1, 1, length), lambda i: (i, 0, 0)),
        ],
        out_specs=[
            pl.BlockSpec((parts, 1, 3, head_size, span), lambda i: (0, i, 0, 0, 0)),
            pl.BlockSpec((parts, 1, head_size, span), lambda i: (0, i, 0, 0)),
        ],
        out_shape=[
            jax.ShapeDtypeStruct(by_heads.shape, jnp.bfloat16),
            jax.ShapeDtypeStruct(grad_heads.shape, jnp.bfloat16),
        ],
        scratch_shapes=[wide, tall, wide, tall, wide, tall, wide, tall,
                        pltpu.VMEM((length, 128), jnp.float32), total, total],
        compiler_params=pltpu.CompilerParams(vmem_limit_bytes=48 * 1024 * 1024),
        cost_estimate=pl.CostEstimate(
            flops=7 * items * length * length * 256,
            bytes_accessed=4 * by_heads.size,
            transcendentals=items * length * length // 2,
        ),
    )(by_heads, grad_heads, item_base)


def sum_pair(share, axis):
    size = lax.axis_size(axis)
    if size == 2:
        other = lax.ppermute(share, axis, [(0, 1), (1, 0)])
        return share.astype(jnp.float32) + other.astype(jnp.float32)
    return lax.psum(share, axis).astype(jnp.float32)


def shards_general(
    block_input,
    positions,
    first_gain,
    first_shift,
    second_gain,
    second_shift,
    triple_weight,
    triple_bias,
    mixer_weight,
    output_bias,
    widen_weight,
    widen_bias,
    narrow_weight,
    cotangent,
):
    seqs, local_tokens, local_width = block_input.shape
    vectors = (first_gain, first_shift, second_gain, second_shift, output_bias, triple_bias, widen_bias)
    small = lax.all_gather(
        jnp.concatenate([vector.reshape(-1) for vector in vectors]), "fsdp", axis=0, tiled=False
    )
    groups = small.shape[0]
    pieces = []
    offset = 0
    for vector in vectors:
        pieces.append(small[:, offset : offset + vector.size].astype(jnp.float32))
        offset += vector.size
    gain_one, shift_one, gain_two, shift_two, bias_output = [
        piece.reshape(-1) for piece in pieces[:5]
    ]
    bias_triple = jnp.transpose(
        pieces[5].reshape((groups,) + triple_bias.shape), (1, 2, 0, 3)
    ).reshape(triple_bias.shape[0], triple_bias.shape[1], -1)
    bias_widen = jnp.transpose(
        pieces[6].reshape((groups,) + widen_bias.shape), (1, 0, 2)
    ).reshape(-1)
    all_positions = lax.all_gather(positions, "ctx", axis=1, tiled=True)
    whole_input = lax.all_gather(block_input, "tp", axis=2, tiled=True)
    weight_triple = lax.all_gather(triple_weight, "fsdp", axis=0, tiled=True)
    whole_cot = lax.all_gather(cotangent, "tp", axis=2, tiled=True)
    mixer_rows = mixer_weight.shape[0]
    joined = lax.all_gather(
        jnp.concatenate([mixer_weight, narrow_weight], axis=0), "fsdp", axis=1, tiled=True
    )
    weight_mixer, weight_narrow = joined[:mixer_rows], joined[mixer_rows:]
    weight_widen = lax.all_gather(widen_weight, "fsdp", axis=0, tiled=True)
    width = weight_triple.shape[0]
    heads_local, head_size = bias_triple.shape[1:]
    feature_start = lax.axis_index("tp") * local_width
    scale = head_size ** (-0.5)
    half = ROT // 2
    normed, inverse = normalize(whole_input.astype(jnp.float32))
    first_rows = (normed * gain_one + shift_one).astype(jnp.bfloat16)
    second_rows = (normed * gain_two + shift_two).astype(jnp.bfloat16)
    cosine, sine = rotary_tables(positions, ROT)
    weight_four = weight_triple.reshape(width, 3, heads_local, head_size)
    projected = jnp.einsum(
        "std,dchk->shckt", first_rows, weight_four, preferred_element_type=jnp.float32
    )
    projected = projected + jnp.transpose(bias_triple, (1, 0, 2))[None, :, :, :, None]
    turned = rotate_forward(projected[:, :, :2], cosine, sine, half)
    triple = jnp.concatenate([turned, projected[:, :, 2:]], axis=2).astype(jnp.bfloat16)
    parts = lax.axis_size("ctx")
    items = seqs * heads_local // parts
    by_heads = lax.all_to_all(
        triple.reshape(parts, items, 3, head_size, local_tokens),
        "ctx",
        split_axis=0,
        concat_axis=0,
        tiled=True,
    )
    mixer_four = weight_mixer.reshape(heads_local, head_size, width)
    mixed_grad = jnp.einsum(
        "ste,hke->shkt", whole_cot, mixer_four, preferred_element_type=jnp.float32
    ).astype(jnp.bfloat16)
    grad_heads = lax.all_to_all(
        mixed_grad.reshape(parts, items, head_size, local_tokens),
        "ctx",
        split_axis=0,
        concat_axis=0,
        tiled=True,
    )
    length = all_positions.shape[1]
    item_seq = (lax.axis_index("ctx") * items + jnp.arange(items, dtype=jnp.int32)) // heads_local
    base = (jnp.arange(length, dtype=jnp.int32)[None, :] - all_positions).astype(jnp.float32)
    item_base = jnp.take(base, item_seq, axis=0)[:, None, :]
    back_heads, mixed = attend(by_heads, grad_heads, item_base, scale)
    mixed_tokens = lax.all_to_all(
        mixed, "ctx", split_axis=0, concat_axis=0, tiled=True
    ).reshape(seqs, heads_local, head_size, local_tokens)
    back_float = (
        lax.all_to_all(back_heads, "ctx", split_axis=0, concat_axis=0, tiled=True)
        .reshape(seqs, heads_local, 3, head_size, local_tokens)
        .astype(jnp.float32)
    )
    widened = (
        jnp.einsum("std,df->stf", second_rows, weight_widen, preferred_element_type=jnp.float32)
        + bias_widen
    )
    activated_float, slope = gelu_parts(widened)
    activated = activated_float.astype(jnp.bfloat16)
    hidden_grad = (
        jnp.einsum("ste,fe->stf", whole_cot, weight_narrow, preferred_element_type=jnp.float32)
        * slope
    )
    widen_bias_grad = jnp.sum(hidden_grad, axis=(0, 1))
    hidden_rounded = hidden_grad.astype(jnp.bfloat16)
    narrow_grad = jnp.einsum(
        "stf,ste->fe", activated, whole_cot, preferred_element_type=jnp.float32
    ).astype(jnp.bfloat16)
    narrow_share = lax.psum_scatter(narrow_grad, "fsdp", scatter_dimension=1, tiled=True)
    widen_grad = jnp.einsum(
        "std,stf->df", second_rows, hidden_rounded, preferred_element_type=jnp.float32
    ).astype(jnp.bfloat16)
    widen_share = lax.psum_scatter(widen_grad, "fsdp", scatter_dimension=0, tiled=True)
    second_grad = jnp.einsum(
        "stf,df->std", hidden_rounded, weight_widen, preferred_element_type=jnp.float32
    ).astype(jnp.bfloat16)
    attention_part = jnp.einsum(
        "shkt,hke->ste", mixed_tokens, mixer_four, preferred_element_type=jnp.float32
    )
    branches = attention_part + jnp.einsum(
        "stf,fe->ste", activated, weight_narrow, preferred_element_type=jnp.float32
    )
    summed = lax.psum_scatter(
        branches.astype(jnp.bfloat16), "tp", scatter_dimension=2, tiled=True
    ).astype(jnp.float32)
    bias_slice = lax.dynamic_slice_in_dim(bias_output, feature_start, local_width, 0)
    block_output = (block_input.astype(jnp.float32) + summed + bias_slice).astype(jnp.bfloat16)
    mixer_grad = (
        jnp.einsum("shkt,ste->hke", mixed_tokens, whole_cot, preferred_element_type=jnp.float32)
        .reshape(weight_mixer.shape)
        .astype(jnp.bfloat16)
    )
    mixer_share = lax.psum_scatter(mixer_grad, "fsdp", scatter_dimension=1, tiled=True)
    unturned = rotate_back(back_float[:, :, :2], cosine, sine, half)
    projected_grad = jnp.concatenate([unturned, back_float[:, :, 2:]], axis=2)
    triple_bias_grad = jnp.transpose(jnp.sum(projected_grad, axis=(0, 4)), (1, 0, 2))
    projected_rounded = projected_grad.astype(jnp.bfloat16)
    first_grad = jnp.einsum(
        "shckt,dchk->std", projected_rounded, weight_four, preferred_element_type=jnp.float32
    ).astype(jnp.bfloat16)
    first_float = first_grad.astype(jnp.float32)
    second_float = second_grad.astype(jnp.float32)
    scaled = first_float * gain_one + second_float * gain_two
    scattered = lax.psum_scatter(
        scaled.astype(jnp.bfloat16), "tp", scatter_dimension=2, tiled=True
    ).astype(jnp.float32)
    row_sums = lax.psum(
        jnp.stack([jnp.sum(scaled, axis=-1), jnp.sum(scaled * normed, axis=-1)]), "tp"
    ) * (1.0 / width)
    triple_grad = (
        jnp.einsum(
            "std,shckt->dchk", first_rows, projected_rounded, preferred_element_type=jnp.float32
        )
        .reshape(weight_triple.shape)
        .astype(jnp.bfloat16)
    )
    triple_share = lax.psum_scatter(triple_grad, "fsdp", scatter_dimension=0, tiled=True)
    output_bias_grad = jnp.sum(whole_cot.astype(jnp.float32), axis=(0, 1))
    wide_sums = jnp.stack(
        [
            jnp.sum(first_float * normed, axis=(0, 1)),
            jnp.sum(first_float, axis=(0, 1)),
            jnp.sum(second_float * normed, axis=(0, 1)),
            jnp.sum(second_float, axis=(0, 1)),
            jnp.where(lax.axis_index("tp") == 0, output_bias_grad, 0.0),
        ]
    )
    wide_sums = lax.psum(wide_sums, ("fsdp", "ctx", "tp"))
    bias_sums = lax.psum(
        jnp.concatenate([triple_bias_grad.reshape(-1), widen_bias_grad]), ("fsdp", "ctx")
    )
    place = lax.axis_index("fsdp")
    vector_size = first_gain.shape[0]
    wide_sums = lax.dynamic_slice_in_dim(wide_sums, place * vector_size, vector_size, 1)
    triple_bias_out = lax.dynamic_slice_in_dim(
        bias_sums[: triple_bias_grad.size].reshape(triple_bias_grad.shape),
        place * triple_bias.shape[2],
        triple_bias.shape[2],
        2,
    )
    widen_bias_out = lax.dynamic_slice_in_dim(
        bias_sums[triple_bias_grad.size :].reshape(widen_bias.shape[0], -1),
        place * widen_bias.shape[1],
        widen_bias.shape[1],
        1,
    )
    own_normed = lax.dynamic_slice_in_dim(normed, feature_start, local_width, 2)
    input_grad = (
        cotangent.astype(jnp.float32)
        + inverse * (scattered - row_sums[0][..., None] - own_normed * row_sums[1][..., None])
    ).astype(jnp.bfloat16)
    return (
        block_output,
        input_grad,
        wide_sums[0],
        wide_sums[1],
        wide_sums[2],
        wide_sums[3],
        sum_pair(triple_share, "ctx"),
        triple_bias_out,
        sum_pair(mixer_share, "ctx"),
        wide_sums[4],
        sum_pair(widen_share, "ctx"),
        widen_bias_out,
        sum_pair(narrow_share, "ctx"),
    )


class Copies:
    def __init__(self, send, recv, local):
        self.send, self.recv, self.local = send, recv, local
        self.remotes = self.locals = 0

    def remote(self, source, target, device):
        index = self.remotes
        self.remotes += 1
        return pltpu.make_async_remote_copy(
            src_ref=source, dst_ref=target, send_sem=self.send.at[index], recv_sem=self.recv.at[index],
            device_id=device, device_id_type=pl.DeviceIdType.MESH,
        )

    def here(self, source, target):
        index = self.locals
        self.locals += 1
        return pltpu.make_async_copy(source, target, self.local.at[index])


def sem_shapes(remotes, local_copies):
    return [pltpu.SemaphoreType.DMA((remotes,)), pltpu.SemaphoreType.DMA((remotes,)),
            pltpu.SemaphoreType.DMA((local_copies,))]


def places(groups):
    z, c, t = lax.axis_index("fsdp"), lax.axis_index("ctx"), lax.axis_index("tp")
    near = t + 1 - 2 * lax.rem(t, 2)
    far = lax.rem(t + 2, 4)
    return z, c, t, near, far


def greet(devices):
    barrier = pltpu.get_barrier_semaphore()
    for device in devices:
        pl.semaphore_signal(barrier, inc=1, device_id=device, device_id_type=pl.DeviceIdType.MESH)
    pl.semaphore_wait(barrier, len(devices))


def aligned(index, step):
    return pl.ds(pl.multiple_of(index * step, step), step)


def line_peers():
    z = lax.axis_index("fsdp")
    return z + 1 - 2 * lax.rem(z, 2), lax.rem(z + 2, 4), 3 - z


class Spread:
    def __init__(self, groups, copies, shards, wholes, by_rows, halved):
        z, c, t, _, _ = places(groups)
        beside, across, cross = line_peers()
        self.groups, self.shards, self.wholes, self.by_rows, self.halved = groups, shards, wholes, by_rows, halved
        self.keeps, self.shares, self.relays = [], [], []
        for a in range(len(shards)):
            def region(group):
                return self.part(a, group, c) if halved[a] else self.whole_of(a, group)

            own = self.half(a, c) if halved[a] else shards[a]
            self.shares.append([
                copies.remote(own, region(z), (across, c, t)),
                copies.remote(own, region(z), (beside, c, t)),
                copies.remote(region(across), region(across), (beside, c, t)),
            ])
            self.relays.append([
                copies.remote(region(origin), region(origin), (z, 1 - c, t)) for origin in (across, beside, cross)
            ] if halved[a] else [])
            self.keeps.append(copies.here(shards[a], self.whole_of(a, z)))

    def half(self, a, half):
        if len(self.shards[a].shape) == 3:
            return self.shards[a].at[:, aligned(half, self.shards[a].shape[1] // 2)]
        return self.shards[a].at[aligned(half, self.shards[a].shape[0] // 2)]

    def whole_of(self, a, group):
        if len(self.shards[a].shape) == 3:
            return self.wholes[a].at[:, aligned(group, self.shards[a].shape[1])]
        if self.by_rows[a]:
            return self.wholes[a].at[aligned(group, self.shards[a].shape[0])]
        return self.wholes[a].at[:, aligned(group, self.shards[a].shape[1])]

    def part(self, a, group, half):
        if len(self.shards[a].shape) == 3:
            return self.wholes[a].at[:, aligned(group * 2 + half, self.shards[a].shape[1] // 2)]
        rows, columns = self.shards[a].shape
        if self.by_rows[a]:
            return self.wholes[a].at[aligned(group * 2 + half, rows // 2)]
        return self.wholes[a].at[aligned(half, rows // 2), aligned(group, columns)]

    def start(self, a):
        self.shares[a][0].start()
        self.shares[a][1].start()
        self.keeps[a].start()

    def relay(self, a, k):
        self.shares[a][k].wait_recv()
        if k == 0:
            self.shares[a][2].start()
        if self.halved[a]:
            self.relays[a][k].start()

    def arrive(self, a):
        self.keeps[a].wait()
        for relay in self.relays[a]:
            relay.wait_recv()

    def finish(self):
        for a in range(len(self.shards)):
            for copy in self.shares[a] + self.relays[a]:
                copy.wait_send()


def front_kernel(groups, half_rotary, x_in, c_in, pos_in, turn_in, widen_in, triple_in, mixer_in, vec_in,
                 c_out, pos_out, turn_out, widen_out, triple_out, mixer_out, vec_out,
                 normed_out, first_out, second_out, active_out, slope_out, narrow_out, heads_out, mixed_grad_out,
                 stats_out, sums_out,
                 x_all, c_all, turn_all, widen_all, triple_all, mixer_all, vec_all, normed, first, second, active, slope,
                 narrow_grad, heads, mixed_grad, vec_float, send, recv, local):
    z, c, t, near, far = places(groups)
    copies = Copies(send, recv, local)
    y_peer, near_peer, far_peer = (z, 1 - c, t), (z, c, near), (z, c, far)
    ring = [lax.rem(z + k, groups) for k in range(1, groups)]
    greet([y_peer, near_peer, far_peer] + [(peer, c, t) for peer in ring])
    span, width = x_in.shape[1:]
    length, whole = x_all.shape
    started = []

    def start(copy):
        copy.start()
        started.append(copy)
        return copy

    def block(ref, half, feature):
        return ref.at[aligned(half, span), aligned(feature, width)]

    cross = 3 - t
    tensors = ((x_in, x_all), (c_in, c_all))
    stays = [copies.here(pos_in.at[c], pos_out.at[c]), copies.here(vec_in, vec_all.at[z]),
             copies.here(turn_in.at[c], turn_all.at[:, aligned(c, span)])]
    for copy in stays:
        copy.start()
    own = [copies.here(source.at[c], block(target, c, t)) for source, target in tensors]
    swaps = [copies.remote(source.at[1 - c], block(target, c, t), y_peer) for source, target in tensors]
    firsts = [
        [copies.remote(source.at[c], block(target, c, t), far_peer),
         copies.remote(source.at[c], block(target, c, t), near_peer)]
        for source, target in tensors
    ]
    weights = Spread(groups, copies, (widen_in, triple_in, mixer_in), (widen_all, triple_all, mixer_all),
                     (True, True, False), (True, False, True))
    start(swaps[0])
    start(firsts[0][0])
    start(firsts[0][1])
    small = [start(copies.remote(vec_in, vec_all.at[z], (peer, c, t))) for peer in ring]
    position_swap = start(copies.remote(pos_in.at[1 - c], pos_out.at[c], y_peer))
    turn_swap = start(copies.remote(turn_in.at[1 - c], turn_all.at[:, aligned(c, span)], y_peer))
    weights.start(0)
    for copy in own:
        copy.start()

    def second_half(index):
        swaps[index].wait_recv()
        other = block(tensors[index][1], 1 - c, t)
        return [start(copies.remote(other, other, far_peer)), start(copies.remote(other, other, near_peer))]

    def pass_on(index, pair, half):
        pair[0].wait_recv()
        there = block(tensors[index][1], half, far)
        return start(copies.remote(there, there, near_peer))

    step_rows = min(256, span)
    saves = []

    def save(source, target):
        copy = copies.here(source, target)
        copy.start()
        saves.append(copy)

    def row_vector(index):
        pieces = []
        for group in range(groups):
            for k in range(width_rows):
                at = index * width_rows + k
                pieces.append(vec_float[group, at : at + 1])
        return jnp.concatenate(pieces, axis=1)

    width_rows = whole // groups // 128

    def normalise(half):
        gain_one, shift_one, gain_two, shift_two = [row_vector(index) for index in range(4)]

        @pl.loop(0, span // step_rows)
        def _(step):
            at = pl.ds(pl.multiple_of(half * span + step * step_rows, step_rows), step_rows)
            rows = x_all[at].astype(jnp.float32)
            mean = jnp.mean(rows, axis=-1, keepdims=True)
            centred = rows - mean
            inverse = lax.rsqrt(jnp.mean(centred * centred, axis=-1, keepdims=True) + norm_eps)
            unit = centred * inverse
            normed[at] = unit.astype(jnp.bfloat16)
            first[at] = (unit * gain_one + shift_one).astype(jnp.bfloat16)
            second[at] = (unit * gain_two + shift_two).astype(jnp.bfloat16)
            stats_out[0:1, at] = jnp.broadcast_to(mean, (step_rows, 128)).T[0:1]
            stats_out[1:2, at] = jnp.broadcast_to(inverse, (step_rows, 128)).T[0:1]

        for source, target in ((normed, normed_out), (first, first_out), (second, second_out)):
            save(source.at[aligned(half, span)], target.at[aligned(half, span)])

    seconds_x = second_half(0)
    start(swaps[1])
    relayed = [pass_on(0, firsts[0], c)]
    for copy in small:
        copy.wait_recv()
    for copy in stays:
        copy.wait()
    vec_float[...] = vec_all[...].astype(jnp.float32)
    save(vec_all, vec_out)
    firsts[0][1].wait_recv()
    own[0].wait()
    relayed[0].wait_recv()
    normalise(c)
    weights.relay(0, 0)
    weights.relay(0, 1)
    weights.start(1)
    relayed.append(pass_on(0, seconds_x, 1 - c))
    start(firsts[1][0])
    start(firsts[1][1])
    seconds_x[1].wait_recv()
    relayed[1].wait_recv()
    normalise(1 - c)
    weights.relay(0, 2)
    seconds_c = second_half(1)
    weights.relay(1, 0)
    weights.start(2)
    weights.arrive(0)
    save(widen_all, widen_out)
    hidden = widen_all.shape[1]

    def placed_vector(first_row, count):
        pieces = []
        for at in range(first_row, first_row + count):
            piece = vec_float[0, at : at + 1]
            for group in range(1, groups):
                piece = piece + vec_float[group, at : at + 1]
            pieces.append(piece)
        return jnp.concatenate(pieces, axis=1)

    bias = placed_vector(5 * width_rows, hidden // 128)
    columns = triple_all.shape[2]
    bias_row = 5 * width_rows + hidden // 128
    triple_bias = [placed_vector(bias_row + k * (columns // 128), columns // 128) for k in range(3)]
    head_size = heads.shape[2]

    def project(half):
        @pl.loop(0, span // step_rows)
        def _(step):
            at = pl.ds(pl.multiple_of(half * span + step * step_rows, step_rows), step_rows)
            cosine, sine = turn_all[0:half_rotary, at], turn_all[half_rotary : 2 * half_rotary, at]
            for k in range(3):
                block = jnp.dot(first[at], triple_all[k], preferred_element_type=jnp.float32) + triple_bias[k]
                block = block.T
                for head in range(columns // head_size):
                    part = block[head * head_size : (head + 1) * head_size]
                    if k < 2:
                        one, two = part[:half_rotary], part[half_rotary : 2 * half_rotary]
                        part = jnp.concatenate(
                            [one * cosine - two * sine, two * cosine + one * sine, part[2 * half_rotary :]], axis=0
                        )
                    heads[k, head, :, at] = part.astype(jnp.bfloat16)

    def widen(half):
        @pl.loop(0, span // step_rows)
        def _(step):
            at = pl.ds(pl.multiple_of(half * span + step * step_rows, step_rows), step_rows)
            widened = jnp.dot(second[at], widen_all[...], preferred_element_type=jnp.float32) + bias
            value, gradient = gelu_parts(widened)
            active[at] = value.astype(jnp.bfloat16)
            slope[at] = gradient.astype(jnp.bfloat16)

        save(active.at[aligned(half, span)], active_out.at[aligned(half, span)])
        save(slope.at[aligned(half, span)], slope_out.at[aligned(half, span)])

    widen(c)
    weights.relay(1, 1)
    relayed.append(pass_on(1, firsts[1], c))
    widen(1 - c)
    weights.relay(1, 2)
    for k in range(2):
        weights.relay(2, k)
    weights.arrive(1)
    save(triple_all, triple_out)
    position_swap.wait_recv()
    turn_swap.wait_recv()
    save(turn_all, turn_out)
    project(c)
    weights.relay(2, 2)
    relayed.append(pass_on(1, seconds_c, 1 - c))
    project(1 - c)
    save(heads, heads_out)
    weights.arrive(2)
    save(mixer_all, mixer_out)
    own[1].wait()
    firsts[1][1].wait_recv()
    seconds_c[1].wait_recv()
    for copy in relayed[2:]:
        copy.wait_recv()
    save(c_all, c_out)

    @pl.loop(0, length // step_rows)
    def _(step):
        at = pl.ds(pl.multiple_of(step * step_rows, step_rows), step_rows)
        mixed_grad[:, at] = lax.dot_general(
            mixer_all[...], c_all[at], (((1,), (1,)), ((), ())), preferred_element_type=jnp.float32
        ).astype(jnp.bfloat16)

    save(mixed_grad, mixed_grad_out)
    tile = min(256, hidden)
    for at in range(0, hidden, tile):
        narrow_grad[at : at + tile] = lax.dot_general(
            active[:, at : at + tile], c_all[...], (((0,), (0,)), ((), ())), preferred_element_type=jnp.float32
        ).astype(jnp.bfloat16)
    save(narrow_grad, narrow_out)

    sums_out[...] = jnp.zeros_like(sums_out)

    @pl.loop(0, length // step_rows)
    def _(step):
        at = pl.ds(pl.multiple_of(step * step_rows, step_rows), step_rows)
        sums_out[0:1] += jnp.sum(c_all[at].astype(jnp.float32), axis=0, keepdims=True)

    for copy in started:
        copy.wait_send()
    weights.finish()
    for copy in saves:
        copy.wait()


def front(groups, half_rotary, head_size, block_input, cotangent, positions, turns, widen_weight, triple_weight,
          mixer_weight, vectors):
    seqs, span, width = block_input.shape
    length, whole = seqs * span, width * 4
    hidden, columns = widen_weight.shape[1], triple_weight.shape[2]
    any_space = pl.BlockSpec(memory_space=pl.ANY)
    in_vmem = pl.BlockSpec(memory_space=pltpu.VMEM)
    bf16, f32 = jnp.bfloat16, jnp.float32
    vec_shape = (groups,) + vectors.shape
    triple_shape = (3, whole, columns)
    turn_shape = (turns.shape[1], length)
    heads_shape = (3, columns // head_size, head_size, length)
    shapes = [
        ((length, whole), bf16), (turn_shape, f32), ((whole, hidden), bf16), (triple_shape, bf16),
        ((columns, whole), bf16), (vec_shape, bf16), ((length, whole), bf16), ((length, whole), bf16),
        ((length, whole), bf16), ((length, hidden), bf16), ((length, hidden), bf16), ((hidden, whole), bf16),
        (heads_shape, bf16), ((columns, length), bf16),
    ]
    outs = [jax.ShapeDtypeStruct(*shape) for shape in shapes]
    return pl.pallas_call(
        functools.partial(front_kernel, groups, half_rotary),
        in_specs=[any_space] * 8,
        out_specs=[any_space] * 15 + [in_vmem] * 2,
        out_shape=outs[:1] + [jax.ShapeDtypeStruct(positions.shape, positions.dtype)] + outs[1:] + [
            jax.ShapeDtypeStruct((8, length), f32),
            jax.ShapeDtypeStruct((8, whole), f32),
        ],
        scratch_shapes=[pltpu.VMEM((length, whole), bf16)] + [pltpu.VMEM(*shape) for shape in shapes] + [
            pltpu.VMEM(vec_shape, f32),
        ] + sem_shapes(16 + 7 * (groups - 1), 32),
        compiler_params=pltpu.CompilerParams(
            collective_id=0, has_side_effects=True, vmem_limit_bytes=58 * 1024 * 1024
        ),
        name="front",
    )(block_input, cotangent, positions, turns, widen_weight, triple_weight, mixer_weight, vectors)


class Reduce:
    def __init__(self, groups, copies, arrays, outs, by_rows, owns, others, sums, inbox, done):
        self.groups, self.copies, self.arrays, self.outs, self.by_rows = groups, copies, arrays, outs, by_rows
        self.owns, self.others, self.sums, self.inbox, self.done = owns, others, sums, inbox, done
        self.z, self.c, self.t, _, _ = places(groups)
        self.y_peer = (self.z, 1 - self.c, self.t)
        beside, across, cross = line_peers()
        self.order = [beside, cross, across, self.z]
        self.targets = [beside, beside, across]
        self.loads, self.swaps, self.sends, self.backs, self.keeps = [], [], [], [], []

    def piece(self, a, group, half):
        array = self.arrays[a]
        if self.by_rows[a]:
            return array.at[aligned(group * 2 + half, array.shape[0] // (2 * self.groups))]
        return array.at[aligned(half, array.shape[0] // 2), aligned(group, array.shape[1] // self.groups)]

    def out_half(self, a, half):
        return self.outs[a].at[aligned(half, self.outs[a].shape[0] // 2)]

    def make(self):
        for a in range(len(self.arrays)):
            loads, swaps, sends = [], [], []
            for slot, group in enumerate(self.order):
                loads.append(self.copies.here(self.piece(a, group, self.c), self.owns[a].at[slot]))
                swaps.append(self.copies.remote(self.piece(a, group, 1 - self.c), self.others[a].at[slot], self.y_peer))
                if slot < 3:
                    sends.append(self.copies.remote(
                        self.sums[a].at[slot], self.inbox[a].at[slot], (self.targets[slot], self.c, self.t)))
            self.loads.append(loads)
            self.swaps.append(swaps)
            self.sends.append(sends)
            self.backs.append(self.copies.remote(self.done[a], self.out_half(a, self.c), self.y_peer))
            self.keeps.append(self.copies.here(self.done[a], self.out_half(a, self.c)))

    def start(self, a):
        for swap, load in zip(self.swaps[a], self.loads[a]):
            swap.start()
            load.start()

    def add(self, a, slot):
        self.loads[a][slot].wait()
        self.swaps[a][slot].wait_recv()
        total = self.owns[a][slot].astype(jnp.float32) + self.others[a][slot].astype(jnp.float32)
        if slot == 2:
            self.sends[a][1].wait_recv()
            total = total + self.inbox[a][1].astype(jnp.float32)
        self.sums[a][slot] = total.astype(jnp.bfloat16)
        if slot < 3:
            self.sends[a][slot].start()

    def total(self, a):
        total = self.sums[a][3].astype(jnp.float32)
        for slot in (0, 2):
            self.sends[a][slot].wait_recv()
            total = total + self.inbox[a][slot].astype(jnp.float32)
        self.done[a][...] = total.astype(jnp.bfloat16)
        self.backs[a].start()
        self.keeps[a].start()

    def finish(self):
        for a in range(len(self.arrays)):
            for swap in self.swaps[a]:
                swap.wait_send()
            for send in self.sends[a]:
                send.wait_send()
            self.backs[a].wait()
            self.keeps[a].wait()


def reduce_shapes(groups, shapes, by_rows):
    owns, others, sums, inbox, done, outs = [], [], [], [], [], []
    for (rows, columns), along in zip(shapes, by_rows):
        part = (rows // (2 * groups), columns) if along else (rows // 2, columns // groups)
        owns.append(pltpu.VMEM((groups,) + part, jnp.bfloat16))
        others.append(pltpu.VMEM((groups,) + part, jnp.bfloat16))
        sums.append(pltpu.VMEM((groups,) + part, jnp.bfloat16))
        inbox.append(pltpu.VMEM((groups - 1,) + part, jnp.bfloat16))
        done.append(pltpu.VMEM(part, jnp.bfloat16))
        outs.append(jax.ShapeDtypeStruct((2 * part[0], part[1]), jnp.bfloat16))
    return owns + others + sums + inbox + done, outs


def reduce_from(groups, copies, arrays, outs, by_rows, scratch):
    n = len(arrays)
    cut = [scratch[n * i : n * (i + 1)] for i in range(5)]
    made = Reduce(groups, copies, arrays, outs, by_rows, *cut)
    made.make()
    return made


def attend_sequence(block, scale, half_rotary, qkv_ref, grad_ref, hot_ref, turn_ref, back_ref, mixed_ref, bias_ref,
                    turned_all, mixed_all, queries, key_rows, value_rows, key_sum, value_sum):
    head_size, length = grad_ref.shape[1:]
    item = pl.program_id(0)
    f32, bf16 = jnp.float32, jnp.bfloat16
    hot = hot_ref[...]
    blank = jnp.zeros_like(hot)
    queries[...] = jnp.concatenate(
        [qkv_ref[0, 0].astype(f32) * scale, (1.0 - hot) * masked_score, blank], axis=0
    ).astype(bf16)
    key_rows[...] = jnp.concatenate([qkv_ref[1, 0].astype(f32), hot, blank], axis=0).T.astype(bf16)
    value_rows[...] = qkv_ref[2, 0].astype(f32).T.astype(bf16)
    keys, values, grads = qkv_ref.at[1, 0], qkv_ref.at[2, 0], grad_ref.at[0]
    last_dims = (((1,), (1,)), ((), ()))

    def unturn(grad, at):
        rounded = grad.astype(bf16).astype(f32)
        cosine, sine = turn_ref[0:half_rotary, at], turn_ref[half_rotary : 2 * half_rotary, at]
        one, two = rounded[:half_rotary], rounded[half_rotary : 2 * half_rotary]
        return jnp.concatenate(
            [one * cosine + two * sine, two * cosine - one * sine, rounded[2 * half_rotary :]], axis=0
        )

    query_bias = jnp.zeros((head_size, 1), f32)
    for start in range(0, length, block):
        count = start + block
        here = slice(start, count)
        scores = jnp.dot(key_rows[:count], queries[:, here], preferred_element_type=f32)
        key_index = lax.broadcasted_iota(jnp.int32, (block, block), 0)
        query_index = lax.broadcasted_iota(jnp.int32, (block, block), 1)
        last = jnp.where(key_index <= query_index, scores[start:], masked_score)
        scores = jnp.concatenate([scores[:start], last], axis=0) if start else last
        top = jnp.max(scores, axis=0, keepdims=True)
        raised = jnp.exp(scores - top)
        inverse = 1.0 / jnp.sum(raised, axis=0, keepdims=True)
        weights = raised.astype(bf16)
        mixed = (jnp.dot(values[:, :count], weights, preferred_element_type=f32) * inverse).astype(bf16)
        scaled = grads[:, here].astype(f32) * inverse
        delta = jnp.sum(mixed.astype(f32) * scaled, axis=0, keepdims=True)
        scaled = scaled.astype(bf16)
        prob_grads = jnp.dot(value_rows[:count], scaled, preferred_element_type=f32)
        score_grads = (raised * (prob_grads - delta)).astype(bf16)
        query_part = jnp.dot(keys[:, :count], score_grads, preferred_element_type=f32)
        key_part = lax.dot_general(queries[:head_size, here], score_grads, last_dims, preferred_element_type=f32)
        value_part = lax.dot_general(scaled, weights, last_dims, preferred_element_type=f32)
        if start:
            key_sum[:, :start] += key_part[:, :start]
            value_sum[:, :start] += value_part[:, :start]
        key_sum[:, here] = key_part[:, start:]
        value_sum[:, here] = value_part[:, start:]
        mixed_ref[0, :, here] = mixed
        mixed_all[item, :, here] = mixed
        turned = unturn(query_part * scale, here)
        query_bias = query_bias + jnp.sum(turned, axis=1, keepdims=True)
        back_ref[0, 0, :, here] = turned.astype(bf16)
        turned_all[0, item, :, here] = turned.astype(bf16)
    turned = unturn(key_sum[...], slice(0, length))
    back_ref[1, 0] = turned.astype(bf16)
    turned_all[1, item] = turned.astype(bf16)
    rounded = value_sum[...].astype(bf16)
    back_ref[2, 0] = rounded
    turned_all[2, item] = rounded
    bias_ref[0, 0] = jnp.broadcast_to(query_bias, (head_size, 128))
    bias_ref[1, 0] = jnp.broadcast_to(jnp.sum(turned, axis=1, keepdims=True), (head_size, 128))
    bias_ref[2, 0] = jnp.broadcast_to(jnp.sum(rounded.astype(f32), axis=1, keepdims=True), (head_size, 128))


def attend_reduce_kernel(block, scale, half_rotary, groups, items, qkv_ref, grad_ref, hot_ref, turn_ref, grads_in,
                         shard_in, first_in, c_in, back_ref, mixed_ref, bias_ref, triple_grad, mixer_grad, grads_out,
                         whole_out, *refs):
    first, c_all, refs = refs[0], refs[1], refs[2:]
    attention, refs = refs[:7], refs[7:]
    scratch, (send, recv, local) = refs[:-3], refs[-3:]
    item = pl.program_id(0)
    copies = Copies(send, recv, local)
    reduce = reduce_from(groups, copies, (grads_in,), (grads_out,), (False,), scratch)
    weights = Spread(groups, copies, (shard_in,), (whole_out,), (False,), (True,))
    rows_loads = [copies.here(first_in, first), copies.here(c_in, c_all)]
    plan = [[] for _ in range(items + 1)]
    for slot in range(groups):
        plan[min(items, max(1, slot))].append(functools.partial(reduce.add, 0, slot))
    for k in range(groups - 1):
        plan[min(items, 1 + k)].append(functools.partial(weights.relay, 0, k))
    plan[items].append(functools.partial(reduce.total, 0))

    def run(actions):
        for action in actions:
            action()

    def begin():
        z, c, t, _, _ = places(groups)
        greet([(z, 1 - c, t)] + [(lax.rem(z + k, groups), c, t) for k in range(1, groups)])
        reduce.start(0)
        weights.start(0)
        for load in rows_loads:
            load.start()

    pl.when(item == 0)(begin)
    for i in range(1, items):
        if plan[i]:
            pl.when(item == i)(functools.partial(run, plan[i]))

    attend_sequence(block, scale, half_rotary, qkv_ref, grad_ref, hot_ref, turn_ref, back_ref, mixed_ref, bias_ref,
                    *attention)

    def end():
        run(plan[items])
        for load in rows_loads:
            load.wait()
        turned_all, mixed_all = attention[:2]
        columns = mixed_all.shape[0] * mixed_all.shape[1]
        for k in range(3):
            triple_grad[k * columns : (k + 1) * columns] = jnp.dot(
                turned_all[k].reshape(columns, -1), first[...], preferred_element_type=jnp.float32
            ).astype(jnp.bfloat16)
        mixer_grad[...] = jnp.dot(
            mixed_all[...].reshape(columns, -1), c_all[...], preferred_element_type=jnp.float32
        ).astype(jnp.bfloat16)
        reduce.finish()
        weights.arrive(0)
        weights.finish()

    pl.when(item == items - 1)(end)


def attend_reduce(heads, grad_heads, hot, turns, scale, half_rotary, groups, narrow_grad, narrow_weight, first, c_rows):
    _, items, head_size, length = heads.shape
    block = min(512, length)
    bf16, f32 = jnp.bfloat16, jnp.float32
    deep = head_size + 2 * hot.shape[0]
    whole = first.shape[1]
    grads = [(3 * items * head_size, whole), (items * head_size, whole)]
    shapes, outs = reduce_shapes(groups, [narrow_grad.shape], (False,))
    any_space = pl.BlockSpec(memory_space=pl.ANY)
    return pl.pallas_call(
        functools.partial(attend_reduce_kernel, block, scale, half_rotary, groups, items),
        grid=(items,),
        in_specs=[
            pl.BlockSpec((3, 1, head_size, length), lambda i: (0, i, 0, 0)),
            pl.BlockSpec((1, head_size, length), lambda i: (i, 0, 0)),
            pl.BlockSpec(hot.shape, lambda i: (0, 0)),
            pl.BlockSpec(turns.shape, lambda i: (0, 0)),
            any_space,
            any_space,
            any_space,
            any_space,
        ],
        out_specs=[
            pl.BlockSpec((3, 1, head_size, length), lambda i: (0, i, 0, 0)),
            pl.BlockSpec((1, head_size, length), lambda i: (i, 0, 0)),
            pl.BlockSpec((3, 1, head_size, 128), lambda i: (0, i, 0, 0)),
            pl.BlockSpec(grads[0], lambda i: (0, 0)),
            pl.BlockSpec(grads[1], lambda i: (0, 0)),
            any_space,
            any_space,
        ],
        out_shape=[
            jax.ShapeDtypeStruct(heads.shape, bf16),
            jax.ShapeDtypeStruct(grad_heads.shape, bf16),
            jax.ShapeDtypeStruct((3, items, head_size, 128), f32),
            jax.ShapeDtypeStruct(grads[0], bf16),
            jax.ShapeDtypeStruct(grads[1], bf16),
        ] + outs + [
            jax.ShapeDtypeStruct((narrow_weight.shape[0], narrow_weight.shape[1] * groups), bf16)
        ],
        scratch_shapes=[
            pltpu.VMEM(first.shape, bf16),
            pltpu.VMEM(c_rows.shape, bf16),
            pltpu.VMEM(heads.shape, bf16),
            pltpu.VMEM(grad_heads.shape, bf16),
            pltpu.VMEM((deep, length), bf16),
            pltpu.VMEM((length, deep), bf16),
            pltpu.VMEM((length, head_size), bf16),
            pltpu.VMEM((head_size, length), f32),
            pltpu.VMEM((head_size, length), f32),
        ] + shapes + sem_shapes(2 * groups + 2 * (groups - 1), groups + 4),
        compiler_params=pltpu.CompilerParams(
            collective_id=1, has_side_effects=True, vmem_limit_bytes=62 * 1024 * 1024
        ),
        cost_estimate=pl.CostEstimate(
            flops=7 * items * length * length * 256,
            bytes_accessed=4 * heads.size,
            transcendentals=items * length * length // 2,
        ),
        name="attend_reduce",
    )(heads, grad_heads, hot, turns, narrow_grad, narrow_weight, first, c_rows)


class ReduceWhole:
    def __init__(self, groups, copies, arrays, outs, by_rows, scratch):
        z, c, t, _, _ = places(groups)
        n = len(arrays)
        self.groups, self.outs = groups, outs
        self.owns, self.inbox, self.theirs = [scratch[n * i : n * (i + 1)] for i in range(3)]
        self.loads, self.sends, self.swaps = [], [], []
        beside, across, cross = line_peers()

        def piece(a, group):
            array = arrays[a]
            if by_rows[a]:
                return array.at[aligned(group, array.shape[0] // groups)]
            return array.at[:, aligned(group, array.shape[1] // groups)]

        for a in range(n):
            self.loads.append([copies.here(piece(a, group), self.owns[a].at[k]) for k, group in enumerate((z, across))])
            self.sends.append([
                copies.remote(piece(a, cross), self.inbox[a].at[0], (beside, c, t)),
                copies.remote(piece(a, beside), self.inbox[a].at[1], (beside, c, t)),
                copies.remote(self.owns[a].at[1], self.inbox[a].at[2], (across, c, t)),
            ])
            self.swaps.append(copies.remote(self.owns[a].at[0], self.theirs[a], (z, 1 - c, t)))

    def start(self):
        for loads, sends in zip(self.loads, self.sends):
            sends[0].start()
            loads[1].start()
        for loads, sends in zip(self.loads, self.sends):
            sends[1].start()
            loads[0].start()

    def middle(self):
        for a, sends in enumerate(self.sends):
            self.loads[a][1].wait()
            sends[0].wait_recv()
            total = self.owns[a][1].astype(jnp.float32) + self.inbox[a][0].astype(jnp.float32)
            self.owns[a][1] = total.astype(jnp.bfloat16)
            sends[2].start()

    def total(self):
        for a, sends in enumerate(self.sends):
            self.loads[a][0].wait()
            total = self.owns[a][0].astype(jnp.float32)
            for k in (1, 2):
                sends[k].wait_recv()
                total = total + self.inbox[a][k].astype(jnp.float32)
            self.owns[a][0] = total.astype(jnp.bfloat16)
            self.swaps[a].start()

    def finish(self):
        for a, swap in enumerate(self.swaps):
            swap.wait()
            total = self.owns[a][0].astype(jnp.float32) + self.theirs[a][...].astype(jnp.float32)
            if len(self.outs[a].shape) == 3:
                rows = total.shape[0] // 3
                for k in range(3):
                    self.outs[a][k] = total[k * rows : (k + 1) * rows].T
            else:
                self.outs[a][...] = total
            for send in self.sends[a]:
                send.wait_send()


def reduce_whole_shapes(groups, shapes, by_rows):
    parts = [(rows // groups, columns) if along else (rows, columns // groups)
             for (rows, columns), along in zip(shapes, by_rows)]
    scratch = [pltpu.VMEM((2,) + part, jnp.bfloat16) for part in parts]
    scratch += [pltpu.VMEM((3,) + part, jnp.bfloat16) for part in parts]
    scratch += [pltpu.VMEM(part, jnp.bfloat16) for part in parts]
    return scratch, [jax.ShapeDtypeStruct(part, jnp.float32) for part in parts]


def back_kernel(groups, turned_in, mixed_in, c_in, mixer_in, active_in, narrow_in, slope_in, second_in,
                triple_in, widen_in, normed_in, gains, norm_stats, front_sums, triple_bias_in,
                triple_grad, mixer_grad,
                out_ref, grad_ref, stats_out, widen_share, wide_out, bias_out, triple_share, mixer_share,
                turned, mixed, c_all, mixer, active, narrow, hidden, second, triple, widen, normed,
                out_part, grad_part, near_box, far_box, widen_grad, wide_sum, bias_sum,
                row_box, row_sum, wide_box, wide_two, wide_three, bias_two, bias_three, *refs):
    scratch, (send, recv, local) = refs[:-3], refs[-3:]
    z, c, t, near, far = places(groups)
    copies = Copies(send, recv, local)
    y_peer = (z, 1 - c, t)
    near_peer, far_peer, cross_peer = (z, c, near), (z, c, far), (z, c, 3 - t)
    ring = [lax.rem(z + k, groups) for k in range(1, groups)]
    span, width = out_ref.shape[1:]
    length, whole = c_all.shape
    quarter = span // 2
    step_rows = min(256, quarter)
    f32, bf16 = jnp.float32, jnp.bfloat16
    loads = []
    for source, target in (
        (narrow_in, narrow), (c_in, c_all), (slope_in, hidden), (second_in, second), (mixed_in, mixed),
        (mixer_in, mixer), (active_in, active), (turned_in, turned), (triple_in, triple), (widen_in, widen),
        (normed_in, normed),
    ):
        load = copies.here(source, target)
        load.start()
        loads.append(load)
    greet([y_peer, near_peer, far_peer, cross_peer] + [(peer, c, t) for peer in ring])
    started, finals, keeps = [], [], []

    def start(copy):
        copy.start()
        started.append(copy)
        return copy

    whole_scratch, half_scratch = scratch[:6], scratch[6:]
    attention_sums = ReduceWhole(
        groups, copies, (triple_grad, mixer_grad), (triple_share, mixer_share), (False, False), whole_scratch
    )
    widen_sums = reduce_from(groups, copies, (widen_grad,), (widen_share,), (True,), half_scratch)
    parts = (out_part, grad_part)
    halves = (1 - c, c)
    nears = [[], []]
    fars = [[], []]

    def send_near(index, turn):
        rows = aligned(halves[turn], span)
        part = parts[index]
        nears[index].append([
            start(copies.remote(
                part.at[rows, aligned(3 - t, width)], near_box.at[index, 0, rows], near_peer)),
            start(copies.remote(
                part.at[rows, aligned(near, width)], near_box.at[index, 1, rows], near_peer)),
        ])

    def rows_of(turn, step):
        return pl.ds(pl.multiple_of(halves[turn] * span + step * quarter, quarter), quarter)

    def send_far(index, turn):
        nears[index][turn][0].wait_recv()
        part = parts[index]
        for step in range(2):
            rows = rows_of(turn, step)
            total = part[rows, aligned(far, width)].astype(f32) + near_box[index, 0, rows].astype(f32)
            part[rows, aligned(far, width)] = total.astype(bf16)
            fars[index].append(start(copies.remote(
                part.at[rows, aligned(far, width)], far_box.at[index, rows], far_peer)))

    def close(index, turn, target):
        nears[index][turn][1].wait_recv()
        part = parts[index]
        for step in range(2):
            rows = rows_of(turn, step)
            fars[index][2 * turn + step].wait_recv()
            done = part.at[rows, aligned(t, width)]
            total = (
                part[rows, aligned(t, width)].astype(f32)
                + near_box[index, 1, rows].astype(f32)
                + far_box[index, rows].astype(f32)
            )
            part[rows, aligned(t, width)] = total.astype(bf16)
            place = target.at[c, pl.ds(step * quarter, quarter)]
            if turn == 0:
                finals.append(start(copies.remote(done, place, y_peer)))
            else:
                keep = copies.here(done, place)
                keep.start()
                keeps.append(keep)

    def loop(turn, body):
        @pl.loop(0, span // step_rows)
        def _(step):
            body(pl.ds(pl.multiple_of(halves[turn] * span + step * step_rows, step_rows), step_rows))

    attention_sums.start()
    columns = mixer.shape[0]
    for load in loads[:3]:
        load.wait()
    bias_sum[...] = jnp.zeros_like(bias_sum)
    bias_sum[1:2] = triple_bias_in[...]

    def hidden_grads(at):
        grads = lax.dot_general(c_all[at], narrow[...], (((1,), (1,)), ((), ())), preferred_element_type=f32)
        grads = grads * hidden[at].astype(f32)
        bias_sum[0:1] += jnp.sum(grads, axis=0, keepdims=True)
        hidden[at] = grads.astype(bf16)

    loop(0, hidden_grads)
    loop(1, hidden_grads)
    loads[3].wait()
    depth = widen_grad.shape[0]
    tile = min(256, depth)
    for at in range(0, depth, tile):
        widen_grad[at : at + tile] = lax.dot_general(
            second[:, at : at + tile], hidden[...], (((0,), (0,)), ((), ())), preferred_element_type=f32
        ).astype(bf16)
    widen_sums.start(0)
    bias_two[c] = bias_sum[...]
    bias_swap = start(copies.remote(bias_two.at[c], bias_two.at[c], y_peer))
    for load in loads[4:7]:
        load.wait()

    def branches(at):
        total = lax.dot_general(mixed[:, at], mixer[...], (((0,), (0,)), ((), ())), preferred_element_type=f32)
        total = total + jnp.dot(active[at], narrow[...], preferred_element_type=f32)
        out_part[at] = total.astype(bf16)

    for turn in range(2):
        loop(turn, branches)
        send_near(0, turn)
    attention_sums.middle()
    for load in loads[7:]:
        load.wait()
    wide_sum[...] = front_sums[...]
    gain_one, gain_two = gains[0:1], gains[1:2]

    def norm_grads(at):
        unit = normed[at].astype(f32)
        one = sum(
            lax.dot_general(turned[k * columns : (k + 1) * columns, at], triple[k], (((0,), (1,)), ((), ())),
                            preferred_element_type=f32)
            for k in range(3)
        )
        wide_sum[0:1] += jnp.sum(one * unit, axis=0, keepdims=True)
        wide_sum[1:2] += jnp.sum(one, axis=0, keepdims=True)
        two = lax.dot_general(hidden[at], widen[...], (((1,), (1,)), ((), ())), preferred_element_type=f32)
        wide_sum[2:3] += jnp.sum(two * unit, axis=0, keepdims=True)
        wide_sum[3:4] += jnp.sum(two, axis=0, keepdims=True)
        scaled = one * gain_one + two * gain_two
        grad_part[at] = scaled.astype(bf16)
        rows = scaled.shape[0]
        total = jnp.sum(scaled, axis=-1, keepdims=True) * (1.0 / whole)
        along = jnp.sum(scaled * unit, axis=-1, keepdims=True) * (1.0 / whole)
        row_box[t, 0:1, at] = jnp.broadcast_to(total, (rows, 128)).T[0:1]
        row_box[t, 1:2, at] = jnp.broadcast_to(along, (rows, 128)).T[0:1]

    send_far(0, 0)
    send_far(0, 1)
    loop(0, norm_grads)
    send_near(1, 0)
    loop(1, norm_grads)
    send_near(1, 1)
    wide_box[t] = wide_sum[...]
    tp_peers = [(t + k) - 4 * ((t + k) // 4) for k in range(1, 4)]
    tp_sent = [start(copies.remote(row_box.at[t], row_box.at[t], (z, c, peer))) for peer in tp_peers]
    tp_sent += [start(copies.remote(wide_box.at[t], wide_box.at[t], (z, c, peer))) for peer in tp_peers]
    send_far(1, 0)
    widen_sums.add(0, 0)
    close(0, 0, out_ref)
    send_far(1, 1)
    for slot in range(1, groups):
        widen_sums.add(0, slot)
    attention_sums.total()
    close(0, 1, out_ref)
    for copy in tp_sent:
        copy.wait_recv()
    row_sum[0:2] = row_box[0] + row_box[1] + row_box[2] + row_box[3]
    row_sum[2:4] = norm_stats[0:2]
    finals.append(start(copies.remote(row_sum.at[:, aligned(1 - c, span)], stats_out.at[c], y_peer)))
    keeps.append(copies.here(row_sum.at[:, aligned(c, span)], stats_out.at[c]))
    keeps[-1].start()
    wide_two[c] = wide_box[0] + wide_box[1] + wide_box[2] + wide_box[3]
    wide_swap = start(copies.remote(wide_two.at[c], wide_two.at[c], y_peer))
    bias_swap.wait_recv()
    bias_three[z] = bias_two[0] + bias_two[1]
    sums_sent = [start(copies.remote(bias_three.at[z], bias_three.at[z], (peer, c, t))) for peer in ring]
    wide_swap.wait_recv()
    wide_three[z] = wide_two[0] + wide_two[1]
    sums_sent += [start(copies.remote(wide_three.at[z], wide_three.at[z], (peer, c, t))) for peer in ring]
    close(1, 0, grad_ref)
    for copy in sums_sent:
        copy.wait_recv()
    bias_total, wide_total = bias_three[0], wide_three[0]
    for group in range(1, groups):
        bias_total = bias_total + bias_three[group]
        wide_total = wide_total + wide_three[group]
    bias_out[...] = bias_total
    wide_out[...] = wide_total
    widen_sums.total(0)
    close(1, 1, grad_ref)
    attention_sums.finish()
    for copy in finals:
        copy.wait_recv()
    for copy in started:
        copy.wait_send()
    for copy in keeps:
        copy.wait()
    widen_sums.finish()


def back(groups, turned, mixed, c_rows, mixer_weight, active, narrow_weight, slope, second, triple_weight,
         widen_weight, normed, gains, norm_stats, front_sums, triple_bias_row,
         triple_grad, mixer_grad):
    length, whole = c_rows.shape
    hidden = active.shape[1]
    width, span = whole // 4, length // 2
    columns = mixed.shape[0]
    any_space = pl.BlockSpec(memory_space=pl.ANY)
    in_vmem = pl.BlockSpec(memory_space=pltpu.VMEM)
    bf16, f32 = jnp.bfloat16, jnp.float32
    grads = [(3 * columns, whole), (columns, whole)]
    whole_scratch, whole_outs = reduce_whole_shapes(groups, grads, (False, False))
    whole_outs[0] = jax.ShapeDtypeStruct((3, whole // groups, columns), f32)
    half_scratch, half_outs = reduce_shapes(groups, [(whole, hidden)], (True,))
    residents = (turned, mixed, c_rows, mixer_weight, active, narrow_weight, slope, second, triple_weight,
                 widen_weight, normed)
    wide, bias = (8, whole), (8, max(hidden, triple_bias_row.shape[1]))
    return pl.pallas_call(
        functools.partial(back_kernel, groups),
        in_specs=[any_space] * 11 + [in_vmem] * 4 + [any_space] * 2,
        out_specs=[any_space] * 4 + [in_vmem] * 4,
        out_shape=[
            jax.ShapeDtypeStruct((2, span, width), bf16),
            jax.ShapeDtypeStruct((2, span, width), bf16),
            jax.ShapeDtypeStruct((2, 4, span), f32),
        ] + half_outs + [
            jax.ShapeDtypeStruct(wide, f32),
            jax.ShapeDtypeStruct(bias, f32),
        ] + whole_outs,
        scratch_shapes=[pltpu.VMEM(array.shape, bf16) for array in residents] + [
            pltpu.VMEM((length, whole), bf16),
            pltpu.VMEM((length, whole), bf16),
            pltpu.VMEM((2, 2, length, width), bf16),
            pltpu.VMEM((2, length, width), bf16),
            pltpu.VMEM((whole, hidden), bf16),
            pltpu.VMEM(wide, f32),
            pltpu.VMEM(bias, f32),
            pltpu.VMEM((4, 2, length), f32),
            pltpu.VMEM((4, length), f32),
            pltpu.VMEM((4,) + wide, f32),
            pltpu.VMEM((2,) + wide, f32),
            pltpu.VMEM((groups,) + wide, f32),
            pltpu.VMEM((2,) + bias, f32),
            pltpu.VMEM((groups,) + bias, f32),
        ] + whole_scratch + half_scratch + sem_shapes(
            32 + 2 * (groups - 1) + 2 * groups + 2 * groups, 20 + groups + 3),
        compiler_params=pltpu.CompilerParams(
            collective_id=2, has_side_effects=True, vmem_limit_bytes=62 * 1024 * 1024
        ),
        name="back",
    )(*residents, gains, norm_stats, front_sums, triple_bias_row, triple_grad, mixer_grad)


def shards_sequence(
    block_input,
    positions,
    first_gain,
    first_shift,
    second_gain,
    second_shift,
    triple_weight,
    triple_bias,
    mixer_weight,
    output_bias,
    widen_weight,
    widen_bias,
    narrow_weight,
    cotangent,
):
    seqs, span, local_width = block_input.shape
    length = seqs * span
    groups = lax.axis_size("fsdp")
    hidden_rows, hidden_part = widen_bias.shape
    heads_local, bias_part = triple_bias.shape[1:]
    head_size = bias_part * groups
    place = lax.axis_index("fsdp")
    here = jnp.arange(groups) == place
    placed_widen = jnp.where(here[None, :, None], widen_bias[:, None, :], 0)
    placed_triple = jnp.where(here[None, None, :, None], triple_bias[:, :, None, :], 0)
    vectors = (first_gain, first_shift, second_gain, second_shift, output_bias)
    index = jnp.arange(len(vectors), dtype=jnp.int32)[:, None, None]
    stacked = sum(
        jnp.where(index == at, vector.reshape(1, -1, 128), 0) for at, vector in enumerate(vectors)
    ).reshape(-1, 128)
    count = stacked.shape[0] + (placed_widen.size + placed_triple.size) // 128
    packed = jnp.concatenate([
        stacked, placed_widen.reshape(-1, 128), placed_triple.reshape(-1, 128),
        jnp.zeros((-count % 16, 128), jnp.bfloat16),
    ])
    cosine, sine = rotary_tables(positions, ROT)
    turns = jnp.concatenate([cosine[:, 0, 0], sine[:, 0, 0]], axis=1)
    (cot_rows, places_out, turn_rows, weight_widen, weight_triple, weight_mixer, small, normed_rows, first_rows,
     second_rows, activated, slope, narrow_grad, heads, mixed_grad, norm_stats, front_sums) = front(
        groups, ROT // 2, head_size, block_input, cotangent, positions.reshape(seqs, span // 128, 128), turns,
        widen_weight, jnp.transpose(triple_weight, (1, 0, 2)), mixer_weight, packed,
    )
    width = weight_widen.shape[0]
    small = small.reshape(groups, -1)
    vector_size = first_gain.shape[0]
    gain_one, _, gain_two, _, bias_output = [
        small[:, at * vector_size : (at + 1) * vector_size].astype(jnp.float32).reshape(-1) for at in range(5)
    ]
    begun = (places_out.reshape(length // 128, 128) == 0).astype(jnp.float32)
    lanes, token_rows = jnp.arange(128), jnp.arange(length // 128)
    count = jnp.dot(begun, (lanes[:, None] <= lanes[None, :]).astype(jnp.float32))
    before = jnp.dot((token_rows[None, :] < token_rows[:, None]).astype(jnp.float32), begun)
    documents = (count + jnp.sum(before, axis=1, keepdims=True)).reshape(1, length) - 1.0
    hot = (documents == jnp.arange(8, dtype=jnp.float32)[:, None]).astype(jnp.float32)
    turned_back, mixed, bias_lanes, triple_grad, mixer_grad, narrow_share, weight_narrow = attend_reduce(
        heads, mixed_grad.reshape(heads_local, head_size, length), hot, turn_rows, head_size ** (-0.5), ROT // 2,
        groups, narrow_grad, narrow_weight, first_rows, cot_rows,
    )
    row = bias_lanes[..., 0].reshape(1, -1)
    bias_width = max(activated.shape[1], row.shape[1])
    row = jnp.pad(row, ((0, 0), (0, bias_width - row.shape[1])))
    zero = jnp.zeros((width,), jnp.float32)
    first_sums = jnp.stack(
        [zero] * 4 + [jnp.where(lax.axis_index("tp") == 0, front_sums[0], 0.0)] + [zero] * 3
    )
    summed, scattered, row_stats, widen_share, wide_sums, bias_sums, triple_share, mixer_share = back(
        groups, turned_back.reshape(-1, length), mixed.reshape(-1, length), cot_rows, weight_mixer, activated,
        weight_narrow, slope, second_rows, weight_triple, weight_widen, normed_rows, jnp.stack([gain_one, gain_two]),
        norm_stats, first_sums, row, triple_grad, mixer_grad,
    )
    feature_start = lax.axis_index("tp") * local_width
    bias_slice = lax.dynamic_slice_in_dim(bias_output, feature_start, local_width, 0)
    own_rows = block_input.astype(jnp.float32)
    block_output = (own_rows + summed.astype(jnp.float32) + bias_slice).astype(jnp.bfloat16)
    own_normed = (own_rows - row_stats[:, 2, :, None]) * row_stats[:, 3, :, None]
    input_grad = (
        cotangent.astype(jnp.float32)
        + row_stats[:, 3, :, None]
        * (scattered.astype(jnp.float32) - row_stats[:, 0, :, None] - own_normed * row_stats[:, 1, :, None])
    ).astype(jnp.bfloat16)
    wide_sums = lax.dynamic_slice_in_dim(wide_sums, place * vector_size, vector_size, 1)
    triple_bias_out = lax.dynamic_slice_in_dim(
        bias_sums[1, : 3 * heads_local * head_size].reshape(3, heads_local, head_size),
        place * triple_bias.shape[2],
        triple_bias.shape[2],
        2,
    )
    widen_bias_out = lax.dynamic_slice_in_dim(
        bias_sums[0, : activated.shape[1]].reshape(hidden_rows, -1), place * hidden_part, hidden_part, 1
    )
    return (
        block_output,
        input_grad,
        wide_sums[0],
        wide_sums[1],
        wide_sums[2],
        wide_sums[3],
        jnp.transpose(triple_share, (1, 0, 2)),
        triple_bias_out,
        mixer_share,
        wide_sums[4],
        widen_share.astype(jnp.float32),
        widen_bias_out,
        narrow_share.astype(jnp.float32),
    )


def shards(block_input, *others):
    seqs = block_input.shape[0]
    if seqs == 2 and lax.axis_size("ctx") == 2 and lax.axis_size("tp") == 4 and lax.axis_size("fsdp") == 4:
        return shards_sequence(block_input, *others)
    return shards_general(block_input, *others)


def solution(mesh):
    in_specs = (
        P("fsdp", "ctx", "tp"),
        P("fsdp", "ctx"),
        P("fsdp"),
        P("fsdp"),
        P("fsdp"),
        P("fsdp"),
        P("fsdp", None, "tp"),
        P(None, "tp", "fsdp"),
        P("tp", "fsdp"),
        P("fsdp"),
        P("fsdp", "tp"),
        P("tp", "fsdp"),
        P("tp", "fsdp"),
        P("fsdp", "ctx", "tp"),
    )
    out_specs = (
        P("fsdp", "ctx", "tp"),
        P("fsdp", "ctx", "tp"),
        P("fsdp"),
        P("fsdp"),
        P("fsdp"),
        P("fsdp"),
        P("fsdp", None, "tp"),
        P(None, "tp", "fsdp"),
        P("tp", "fsdp"),
        P("fsdp"),
        P("fsdp", "tp"),
        P("tp", "fsdp"),
        P("tp", "fsdp"),
    )
    return jax.shard_map(shards, mesh=mesh, in_specs=in_specs, out_specs=out_specs, check_vma=False)
```
